32 devices in a mesh: dp: 16 (over z, y, x), fsdp: 2 (over core).
Axes of the slice: x: 2, y: 2, z: 4, core: 2. Of those that a mesh axis runs over, the one named last changes fastest.
Arguments:
- tokens: bfloat16 [32, 256, 1152], P(('dp', 'fsdp')), may hold values from -6 to 6
- condition: bfloat16 [32, 1152], P(('dp', 'fsdp')), may hold values from -6 to 6
- cotangent: bfloat16 [32, 256, 1152], P(('dp', 'fsdp')), may hold values from -6 to 6
- image_grids: int32 [32, 2], P(('dp', 'fsdp')), may hold values from 12 to 20, as said below
- noise_bins: int32 [32], P(('dp', 'fsdp')), may hold values from 0 to 15, as said below
- bin_weights: int32 [16], replicated, may hold values from 1 to 4
- w_qkv: bfloat16 [1152, 3456], P('dp', 'fsdp'), may hold values from -0.1875 to 0.1875
- b_query: float32 [1152], replicated, may hold values from -3 to 3
- b_value: float32 [1152], replicated, may hold values from -0.625 to 0.625
- w_proj: bfloat16 [1152, 1152], P('dp', 'fsdp'), may hold values from -1.5 to 1.5
- b_proj: float32 [1152], replicated, may hold values from -1.75 to 1.75
- w_fc1: bfloat16 [1152, 4608], P('dp', 'fsdp'), may hold values from -0.1875 to 0.1875
- b_fc1: float32 [4608], replicated, may hold values from -3 to 3
- w_fc2: bfloat16 [4608, 1152], P('dp', 'fsdp'), may hold values from -0.09375 to 0.09375
- b_fc2: float32 [1152], replicated, may hold values from -1.75 to 1.75
- w_ada: bfloat16 [6912, 1152], replicated, may hold values from -0.1875 to 0.1875
- b_ada: float32 [6912], replicated, may hold values from -1.75 to 1.75
Outputs:
- result: bfloat16 [32, 256, 1152], P(('dp', 'fsdp'))
- grad_tokens: bfloat16 [32, 256, 1152], P(('dp', 'fsdp'))
- grad_condition: float32 [32, 1152], P(('dp', 'fsdp'))
- grad_w_qkv: float32 [1152, 3456], P('dp', 'fsdp')
- grad_b_query: float32 [1152], replicated
- grad_b_value: float32 [1152], replicated
- grad_w_proj: float32 [1152, 1152], P('dp', 'fsdp')
- grad_b_proj: float32 [1152], replicated
- grad_w_fc1: float32 [1152, 4608], P('dp', 'fsdp')
- grad_b_fc1: float32 [4608], replicated
- grad_w_fc2: float32 [4608, 1152], P('dp', 'fsdp')
- grad_b_fc2: float32 [1152], replicated
- grad_w_ada: float32 [6912, 1152], P(('dp', 'fsdp'))
- grad_b_ada: float32 [6912], replicated
The draws below stay inside these ranges and needn't reach their ends.
Inputs may be any that keep to these rules, and one draw needn't show every extreme that they name: `image_grids`: each row is a height and a width that sum to 32; an image's tokens are the first height * width of its 256 slots. `noise_bins`: bin ids never fall along the image slots, and every bin holds at least one image.
All inputs are finite; a program needn't handle non-finite values.
Results may differ from the reference program's by a relative error of at most 0.014.
The reference program's roundings to bfloat16 on the way count: a program that leaves them out, or rounds other values in their place, can miss the bound.
Values may be sent and summed in bfloat16 or wider, within the bound.
A program may use at most 256 MiB of HBM per device.

```python
import jax
import jax.numpy as jnp
from jax import lax

D = 1152
H = 16
HD = 72
FF = 4608
SIDE = 16
BINS = 16
SEQ = 256
IMAGES = 32


def draw_image_grids(key, part):
    side_key = jax.random.fold_in(key, 4099)
    side_reach = SIDE // 4
    height = jax.random.randint(side_key, (IMAGES,), SIDE - side_reach, SIDE + side_reach + 1, dtype=jnp.int32)
    height = height.at[0].set(SIDE + side_reach).at[1].set(SIDE - side_reach)
    width_cells = 2 * SIDE - height
    return jnp.stack([height, width_cells], axis=1)


def draw_noise_bins(key, part):
    bins_key = jax.random.fold_in(key, 4111)
    extra_bins = jax.random.randint(bins_key, (IMAGES - BINS,), 0, BINS, dtype=jnp.int32)
    return jnp.sort(jnp.concatenate([jnp.arange(BINS, dtype=jnp.int32), extra_bins]))


def set_ends(entries, rng, least, largest):
    shape = entries.shape
    index_at = [jax.random.randint(jax.random.fold_in(rng, axis), (), 0, shape[axis]) for axis in range(len(shape))]
    entries = entries.at[tuple(index_at)].set(least)
    longest = shape.index(max(shape))
    index_at[longest] = (index_at[longest] + 1) % shape[longest]
    return entries.at[tuple(index_at)].set(largest)


def strengthened(values, key, source, target, parts, factor):
    def block_of(dim):
        return (jnp.arange(values.shape[dim]) // (values.shape[dim] // parts)).reshape((-1,) + (1,) * (values.ndim - 1 - dim))

    first = jax.random.permutation(key, parts)[block_of(target)]
    second = (block_of(target) + parts // 2) % parts
    return jnp.where((block_of(source) == first) | (block_of(source) == second), factor * values, values)


def levels(key, extent, split, smallest, high):
    level = 1.0
    for position, parts in split:
        heights = jax.random.uniform(jax.random.fold_in(jax.random.fold_in(key, 6), position), (parts,), jnp.float32, smallest / len(split), high / len(split))
        level = level * jnp.repeat(jnp.exp(heights), extent[position] // parts).reshape((-1,) + (1,) * (len(extent) - 1 - position))
    return level


def gaussian(own_key, dims, scale, reach, cuts=(), kind=jnp.bfloat16):
    values = scale * jax.random.normal(own_key, dims, jnp.float32)
    if cuts:
        values = values * levels(own_key, dims, cuts, -0.22, 0.18)
    return jnp.clip(values, -reach, reach).astype(kind)


def noise_with(rng, extent, width, most, split, heavy, kind=jnp.bfloat16):
    entries = width * jax.random.normal(rng, extent, jnp.float32)
    if split:
        entries = entries * levels(rng, extent, split, -0.22, 0.18)
    return jnp.clip(strengthened(entries, jax.random.fold_in(rng, 3), *heavy), -most, most).astype(kind)


def setup_inputs(seed: int = 0) -> dict:
    key_of = jax.random.split(jax.random.key(seed), 18)
    tokens = gaussian(key_of[0], (IMAGES, SEQ, D), 1.0, 6.0, ((0, 32),))
    condition = gaussian(key_of[1], (IMAGES, D), 1.0, 6.0, ((0, 32),))
    cotangent = noise_with(key_of[2], (IMAGES, SEQ, D), 1.0, 6.0, ((0, 32),), (0, 2, 32, 2.75))
    image_grids = draw_image_grids(jax.random.fold_in(key_of[17], 71), 0)
    noise_bins = draw_noise_bins(jax.random.fold_in(key_of[17], 71), 0)
    bin_weights = set_ends(jax.random.randint(key_of[5], (BINS,), 1, 5), jax.random.fold_in(key_of[5], 1), 1, 4).astype(jnp.int32)
    w_qkv = gaussian(key_of[6], (D, 3 * D), D ** -0.5, 0.1875, ((0, 16), (1, 2)))
    b_query = gaussian(key_of[7], (D,), 0.5, 3.0, (), jnp.float32)
    b_value = gaussian(key_of[8], (D,), 0.1, 0.625, (), jnp.float32)
    w_proj = gaussian(key_of[9], (D, D), (D // 64) ** -0.5, 1.5, ((0, 16), (1, 2)))
    b_proj = gaussian(key_of[10], (D,), 0.3, 1.75, (), jnp.float32)
    w_fc1 = gaussian(key_of[11], (D, FF), D ** -0.5, 0.1875, ((0, 16), (1, 2)))
    b_fc1 = gaussian(key_of[12], (FF,), 0.5, 3.0, (), jnp.float32)
    w_fc2 = gaussian(key_of[13], (FF, D), FF ** -0.5, 0.09375, ((0, 16), (1, 2)))
    b_fc2 = gaussian(key_of[14], (D,), 0.3, 1.75, (), jnp.float32)
    w_ada = gaussian(key_of[15], (6 * D, D), D ** -0.5, 0.1875)
    b_ada = gaussian(key_of[16], (6 * D,), 0.3, 1.75, (), jnp.float32)
    return dict(tokens=tokens, condition=condition, cotangent=cotangent, image_grids=image_grids, noise_bins=noise_bins, bin_weights=bin_weights, w_qkv=w_qkv, b_query=b_query, b_value=b_value, w_proj=w_proj, b_proj=b_proj, w_fc1=w_fc1, b_fc1=b_fc1, w_fc2=w_fc2, b_fc2=b_fc2, w_ada=w_ada, b_ada=b_ada)


@jax.custom_vjp
def low(v):
    return lax.optimization_barrier(v.astype(jnp.bfloat16)).astype(jnp.float32)

@jax.custom_vjp
def low_back(v):
    return v

def low_keep(v):
    return (low(v), None)

def low_pass(kept, grad):
    return (grad,)

def back_keep(v):
    return (v, None)

def back_low(kept, grad):
    return (low(grad),)
low.defvjp(low_keep, low_pass)
low_back.defvjp(back_keep, back_low)
NEG_FILL = -1e+30
NORM_EPS = 1e-06
GELU_COEF = 0.7978845608028654
CUBIC_COEF = 0.044715

def gelu_tanh(values_in):
    return 0.5 * values_in * (1.0 + jnp.tanh(GELU_COEF * (values_in + CUBIC_COEF * values_in * values_in * values_in)))

def layer_norm(inputs):
    centered = inputs - lax.optimization_barrier(jnp.mean(inputs, axis=-1, keepdims=True))
    variance = lax.optimization_barrier(jnp.mean(centered * centered, axis=-1, keepdims=True))
    return centered * lax.rsqrt(variance + NORM_EPS)

def project(inputs, matrix):
    return jnp.einsum('gld,de->gle', inputs, matrix, precision=lax.Precision.HIGHEST)

def forward(params, tokens, condition, valid_keys):
    w_qkv, b_query, b_value, w_proj, b_proj, w_fc1, b_fc1, w_fc2, b_fc2, w_ada, b_ada = params
    group_size = tokens.shape[0]
    silu_cond = low(jax.nn.silu(condition))
    modul = low_back(jnp.dot(silu_cond, w_ada.T, precision=lax.Precision.HIGHEST) + b_ada)
    pieces = [modul[:, None, part_index * D:(part_index + 1) * D] for part_index in range(6)]
    shift_one, scale_one, gate_one, shift_two, scale_two, gate_two = pieces
    attn_in = low(layer_norm(tokens) * (1.0 + scale_one) + shift_one)
    bias_qkv = jnp.concatenate([b_query, jnp.zeros_like(b_query), b_value])
    qkv_all = low_back(low(project(attn_in, w_qkv) + bias_qkv))
    qkv_heads = qkv_all.reshape(group_size, SEQ, 3, H, HD)
    query, keys, values = (qkv_heads[:, :, 0], qkv_heads[:, :, 1], qkv_heads[:, :, 2])
    scores = low_back(jnp.einsum('glhc,gmhc->ghlm', query, keys, precision=lax.Precision.HIGHEST) * HD ** (-0.5))
    scores = jnp.where(valid_keys[:, None, None, :], scores, NEG_FILL)
    soft_probs = low(jax.nn.softmax(scores, axis=-1))
    attended = jnp.einsum('ghlm,gmhc->glhc', soft_probs, values, precision=lax.Precision.HIGHEST)
    attended = low_back(low(attended.reshape(group_size, SEQ, D)))
    attn_out = low_back(project(attended, w_proj) + b_proj)
    middle = tokens + gate_one * attn_out
    mlp_in = low(layer_norm(middle) * (1.0 + scale_two) + shift_two)
    hidden = low_back(project(mlp_in, w_fc1) + b_fc1)
    active = low(gelu_tanh(hidden))
    branch = low_back(project(active, w_fc2) + b_fc2)
    return middle + gate_two * branch

def reference(tokens, condition, cotangent, image_grids, noise_bins, bin_weights, w_qkv, b_query, b_value, w_proj, b_proj, w_fc1, b_fc1, w_fc2, b_fc2, w_ada, b_ada):
    token_count = image_grids[:, 0] * image_grids[:, 1]
    positions = jnp.arange(SEQ, dtype=jnp.int32)
    valid_keys = positions[None, :] < token_count[:, None]
    bin_table = (noise_bins[:, None] == jnp.arange(BINS, dtype=jnp.int32)[None, :]).astype(jnp.float32)
    counts = lax.optimization_barrier(jnp.sum(bin_table * token_count[:, None].astype(jnp.float32), axis=0))
    bin_scale = bin_weights.astype(jnp.float32) * (jnp.sum(counts) / BINS) / counts
    image_scale = lax.optimization_barrier(jnp.sum(bin_table * bin_scale[None, :], axis=1))
    loss_weight = valid_keys.astype(jnp.float32) * image_scale[:, None]
    params = tuple((member.astype(jnp.float32) for member in (w_qkv, b_query, b_value, w_proj, b_proj, w_fc1, b_fc1, w_fc2, b_fc2, w_ada, b_ada)))
    group_size = 16
    groups = IMAGES // group_size

    def split_groups(whole_array):
        return whole_array.reshape((groups, group_size) + whole_array.shape[1:])

    def one_group(totals, group_data):
        tok_block, cond_block, cot_block, valid_block, weight_block = group_data

        def local_forward(param_set, tok_in, cond_in):
            return forward(param_set, tok_in, cond_in, valid_block)
        out_block, pull_back = jax.vjp(local_forward, params, tok_block.astype(jnp.float32), cond_block.astype(jnp.float32))
        grad_params, grad_tok, grad_cond = pull_back(cot_block.astype(jnp.float32) * weight_block[:, :, None])
        totals = jax.tree.map(jnp.add, totals, grad_params)
        return (totals, (out_block.astype(jnp.bfloat16), grad_tok.astype(jnp.bfloat16), grad_cond))
    zeros_init = jax.tree.map(jnp.zeros_like, params)
    totals, outputs = lax.scan(one_group, zeros_init, (split_groups(tokens), split_groups(condition), split_groups(cotangent), split_groups(valid_keys), split_groups(loss_weight)))
    result = outputs[0].reshape(IMAGES, SEQ, D)
    grad_tokens = outputs[1].reshape(IMAGES, SEQ, D)
    grad_condition = outputs[2].reshape(IMAGES, D)
    return (result, grad_tokens, grad_condition, totals[0], totals[1], totals[2], totals[3], totals[4], totals[5], totals[6], totals[7], totals[8], totals[9], totals[10])
```

```python
import functools

import jax
import jax.numpy as jnp
from jax import lax
from jax.experimental import pallas as pl
from jax.experimental.pallas import tpu as pltpu
from jax.sharding import PartitionSpec as P

D = 1152
H = 16
HD = 72
BINS = 16
SEQ = 256


NEG_FILL = -1e30
NORM_EPS = 1e-06
GELU_COEF = 0.7978845608028654
CUBIC_COEF = 0.044715
ROWS_DIMS = (((0,), (0,)), ((), ()))
LAST_DIMS = (((1,), (1,)), ((), ()))


def gelu_tanh(values_in):
    return (
        0.5
        * values_in
        * (1.0 + jnp.tanh(GELU_COEF * (values_in + CUBIC_COEF * values_in * values_in * values_in)))
    )


def norm_rows(inputs):
    centered = inputs - jnp.mean(inputs, axis=-1, keepdims=True)
    inverse = lax.rsqrt(jnp.mean(centered * centered, axis=-1, keepdims=True) + NORM_EPS)
    return (centered * inverse, inverse)


def norm_back(grad_normed, normed, inverse):
    centered_grad = grad_normed - jnp.mean(grad_normed, axis=-1, keepdims=True)
    return inverse * (
        centered_grad - normed * jnp.mean(grad_normed * normed, axis=-1, keepdims=True)
    )


VMEM_LIMIT = 66_000_000
ANY = pl.BlockSpec(memory_space=pl.ANY)
VMEM = pl.BlockSpec(memory_space=pltpu.VMEM)
ZS = 4
OFFSETS = (0, -1, 1, -2, 2, -3, 3)


class Place:
    def __init__(self):
        self.i = lax.axis_index("dp")
        self.c = lax.axis_index("fsdp")
        self.z = self.i // 4
        self.q = self.i % 4
        self.y = self.q // 2
        self.x = self.q % 2
        self.to_y = 2 * (1 - 2 * self.y)
        self.to_x = 1 - 2 * self.x

    def partners(self, level):
        odd = level % 2
        first = odd * self.to_x + (1 - odd) * self.to_y
        return first, self.to_x + self.to_y - first

    def greet(self):
        barrier = pltpu.get_barrier_semaphore()

        def signal(i, c):
            pl.semaphore_signal(
                barrier,
                inc=1,
                device_id={"dp": i, "fsdp": c},
                device_id_type=pl.DeviceIdType.MESH,
            )

        signal(self.i, 1 - self.c)
        signal(self.i + self.to_y, self.c)
        signal(self.i + self.to_x, self.c)
        up, down = self.z < ZS - 1, self.z > 0
        pl.when(up)(lambda: signal(self.i + 4, self.c))
        pl.when(down)(lambda: signal(self.i - 4, self.c))
        pl.semaphore_wait(barrier, 3 + up.astype(jnp.int32) + down.astype(jnp.int32))


def remote(src, dst, send, recv, i, c):
    return pltpu.make_async_remote_copy(
        src_ref=src,
        dst_ref=dst,
        send_sem=send,
        recv_sem=recv,
        device_id={"dp": i, "fsdp": c},
        device_id_type=pl.DeviceIdType.MESH,
    )


def gather_sems(count):
    dma = pltpu.SemaphoreType.DMA
    return [
        dma((count, 16)),
        dma((count, 16)),
        dma((count, 2, ZS)),
        dma((count, ZS, 3)),
        dma((count, 16)),
        dma((count,)),
    ]


class Gather:
    def __init__(self, at, k, shard, own, sib, sems):
        self.at, self.k, self.shard, self.own, self.sib = at, k, shard, own, sib
        self.recv, self.core, self.line, self.pair, self.over, self.local = sems

    def send(self, src, j, sem, i):
        return remote(src, self.own.at[j], sem, self.recv.at[self.k, j], i, self.at.c)

    def across(self, src, j):
        at, k = self.at, self.k
        return remote(
            src, self.sib.at[j], self.over.at[k, j], self.core.at[k, j], at.i, 1 - at.c
        )

    def arrived(self, j):
        at = self.at
        remote(
            self.own.at[j],
            self.own.at[j],
            self.over.at[self.k, j],
            self.recv.at[self.k, j],
            at.i,
            1 - at.c,
        ).wait_recv()

    def pieces(self, level):
        first, second = self.at.partners(level)
        column = level * 4 + self.at.q
        return first, second, column

    def guard(self, off, run):
        level = self.at.z + off
        if off == 0:
            run(level)
        else:
            pl.when((level >= 0) & (level < ZS))(lambda: run(level))

    def column_copies(self, off, level):
        at, k = self.at, self.k
        first, second, j = self.pieces(level)
        src = self.shard if off == 0 else self.own.at[j]
        always = [
            self.send(src, j, self.pair.at[k, level, 0], at.i + first),
            self.send(src, j, self.pair.at[k, level, 1], at.i + second),
            self.across(src, j),
        ]
        up = self.send(src, j, self.line.at[k, 0, level], at.i + 4) if off <= 0 else None
        down = self.send(src, j, self.line.at[k, 1, level], at.i - 4) if off >= 0 else None
        return always, up, down

    def column(self, off):
        def run(level):
            if off:
                self.arrived(level * 4 + self.at.q)
            always, up, down = self.column_copies(off, level)
            if up is not None:
                pl.when(self.at.z < ZS - 1)(up.start)
            if down is not None:
                pl.when(self.at.z > 0)(down.start)
            for copy in always:
                copy.start()
            if off == 0:
                self.keep().start()

        self.guard(off, run)

    def keep(self):
        return pltpu.make_async_copy(
            self.shard, self.own.at[self.at.i], self.local.at[self.k]
        )

    def relay_copies(self, level):
        first, second, column = self.pieces(level)
        j = column + first
        return (
            self.send(self.own.at[j], j, self.pair.at[self.k, level, 2], self.at.i + second),
            self.across(self.own.at[j], j),
        )

    def relay(self, off):
        def run(level):
            first, _, column = self.pieces(level)
            self.arrived(column + first)
            for copy in self.relay_copies(level):
                copy.start()

        self.guard(off, run)

    def last_copies(self, level):
        first, second, column = self.pieces(level)
        return [(j, self.across(self.own.at[j], j)) for j in (column + second, column + first + second)]

    def last(self, off):
        def run(level):
            for j, copy in self.last_copies(level):
                self.arrived(j)
                copy.start()

        self.guard(off, run)

    def finish(self):
        at = self.at
        self.keep().wait()
        for off in OFFSETS:

            def run(level, off=off):
                always, up, down = self.column_copies(off, level)
                if up is not None:
                    pl.when(at.z < ZS - 1)(up.wait_send)
                if down is not None:
                    pl.when(at.z > 0)(down.wait_send)
                for copy in always:
                    copy.wait_send()
                for copy in self.relay_copies(level):
                    copy.wait_send()
                for _, copy in self.last_copies(level):
                    copy.wait_send()

            self.guard(off, run)

        @pl.loop(0, 16)
        def _(j):
            self.across(self.sib.at[j], j).wait_recv()

    def events(self, start, span):
        out = []
        for off in OFFSETS:
            far = abs(off)
            out.append((start + span * 0.15 * far, functools.partial(self.column, off)))
            out.append((start + span * (0.3 + 0.2 * far), functools.partial(self.relay, off)))
            out.append((start + span * (0.6 + 0.2 * far), functools.partial(self.last, off)))
        return out


def gather_kernel(count, *refs):
    shards, own, sib = refs[:count], refs[count : 2 * count], refs[2 * count : 3 * count]
    sems = refs[3 * count :]
    at = Place()
    at.greet()
    steps, start = [], 0.0
    jobs = []
    for k in range(count):
        job = Gather(at, k, shards[k], own[k], sib[k], sems)
        jobs.append(job)
        span = float(shards[k].shape[0] * shards[k].shape[1])
        steps += job.events(start, span)
        start += span
    for _, action in sorted(steps, key=lambda item: item[0]):
        action()
    for job in jobs:
        job.finish()


def gather_all(shards):
    count = len(shards)
    spread = [jax.ShapeDtypeStruct((16,) + s.shape, s.dtype) for s in shards]
    outs = pl.pallas_call(
        functools.partial(gather_kernel, count),
        out_shape=spread + spread,
        in_specs=[VMEM] * count,
        out_specs=[ANY] * (2 * count),
        scratch_shapes=gather_sems(count),
        compiler_params=pltpu.CompilerParams(
            collective_id=0, has_side_effects=True, vmem_limit_bytes=16_000_000
        ),
        name="gather_all",
    )(*shards)
    return outs[:count], outs[count:]


def total(*values):
    out = values[0].astype(jnp.float32)
    for value in values[1:]:
        out = out + value.astype(jnp.float32)
    return out


class Scatter:
    def __init__(self, at, k, mine, other, result, bufs, sems):
        self.at, self.k = at, k
        self.mine, self.other, self.result = mine, other, result
        self.held, self.cross, self.near, self.far, self.line = bufs
        (
            self.load_sem,
            self.cross_send,
            self.cross_recv,
            self.near_send,
            self.near_recv,
            self.far_send,
            self.far_recv,
            self.line_send,
            self.line_recv,
        ) = sems

    def load(self):
        return pltpu.make_async_copy(self.mine, self.held, self.load_sem.at[self.k])

    def cross_copy(self, level):
        at, k = self.at, self.k
        rows = pl.ds(level * 4, 4)
        return remote(
            self.other.at[rows],
            self.cross.at[rows],
            self.cross_send.at[k, level],
            self.cross_recv.at[k, level],
            at.i,
            1 - at.c,
        )

    def near_copies(self, level):
        at, k = self.at, self.k
        first, second = at.partners(level)
        column = level * 4 + at.q
        return [
            remote(
                self.held.at[j],
                self.near.at[level, slot],
                self.near_send.at[k, level, slot],
                self.near_recv.at[k, level, slot],
                at.i + second,
                at.c,
            )
            for slot, j in enumerate((column + second, column + first + second))
        ]

    def far_copy(self, level):
        at, k = self.at, self.k
        first, _ = at.partners(level)
        j = level * 4 + at.q + first
        return remote(
            self.held.at[j],
            self.far.at[level],
            self.far_send.at[k, level],
            self.far_recv.at[k, level],
            at.i + first,
            at.c,
        )

    def line_copy(self, way, level):
        at, k = self.at, self.k
        j = level * 4 + at.q
        return remote(
            self.held.at[j],
            self.line.at[way, level],
            self.line_send.at[k, way, level],
            self.line_recv.at[k, way, level],
            at.i + (4 if way == 0 else -4),
            at.c,
        )

    def begin(self):
        self.load().start()

        @pl.loop(0, ZS)
        def _(level):
            self.cross_copy(level).start()

        zeros = jnp.zeros(self.line.shape[2:], self.line.dtype)

        @pl.when(self.at.z == 0)
        def _():
            @pl.loop(0, ZS)
            def _(level):
                self.line[0, level] = zeros

        @pl.when(self.at.z == ZS - 1)
        def _():
            @pl.loop(0, ZS)
            def _(level):
                self.line[1, level] = zeros

    def stage_near(self):
        self.load().wait()

        @pl.loop(0, ZS)
        def _(level):
            first, second = self.at.partners(level)
            column = level * 4 + self.at.q
            self.cross_copy(level).wait_recv()
            copies = self.near_copies(level)
            for copy, j in zip(copies, (column + second, column + first + second)):
                self.held[j] = total(self.held[j], self.cross[j]).astype(jnp.bfloat16)
                copy.start()

    def stage_far(self):
        @pl.loop(0, ZS)
        def _(level):
            first, _ = self.at.partners(level)
            j = level * 4 + self.at.q + first
            for copy in self.near_copies(level):
                copy.wait_recv()
            self.held[j] = total(self.held[j], self.cross[j], self.near[level, 1]).astype(
                jnp.bfloat16
            )
            self.far_copy(level).start()

    def stage_line(self):
        z = self.at.z

        def pass_on(way, level):
            j = level * 4 + self.at.q
            self.far_copy(level).wait_recv()
            if way == 0:
                pl.when(z > 0)(self.line_copy(0, level).wait_recv)
            else:
                pl.when(z < ZS - 1)(self.line_copy(1, level).wait_recv)
            self.held[j] = total(
                self.held[j],
                self.cross[j],
                self.near[level, 0],
                self.far[level],
                self.line[way, level],
            ).astype(jnp.bfloat16)
            self.line_copy(way, level).start()

        @pl.loop(0, ZS - 1)
        def _(back):
            level = ZS - 1 - back
            pl.when(level > z)(lambda: pass_on(0, level))
            low = back
            pl.when(low < z)(lambda: pass_on(1, low))

    def stage_own(self):
        z = self.at.z
        j = self.at.i
        self.far_copy(z).wait_recv()
        pl.when(z > 0)(self.line_copy(0, z).wait_recv)
        pl.when(z < ZS - 1)(self.line_copy(1, z).wait_recv)
        self.result[...] = total(
            self.held[j],
            self.cross[j],
            self.near[z, 0],
            self.far[z],
            self.line[0, z],
            self.line[1, z],
        )

    def finish(self):
        z = self.at.z

        @pl.loop(0, ZS)
        def _(level):
            self.cross_copy(level).wait_send()
            for copy in self.near_copies(level):
                copy.wait_send()
            self.far_copy(level).wait_send()
            pl.when(level > z)(self.line_copy(0, level).wait_send)
            pl.when(level < z)(self.line_copy(1, level).wait_send)


def scatter_kernel(count, *refs):
    refs = list(refs)

    def take(n):
        out = refs[:n]
        del refs[:n]
        return out

    mine, other, note = take(count), take(count), take(1)[0]
    results = take(count)
    note_own, note_sib = take(2)
    bufs = [take(5) for _ in range(count)]
    sems, note_sems = take(9), take(6)
    at = Place()
    at.greet()
    jobs = [
        Scatter(at, k, mine[k], other[k], results[k], bufs[k], sems) for k in range(count)
    ]
    word = Gather(at, 0, note, note_own, note_sib, note_sems)
    whisper = [action for _, action in sorted(word.events(0.0, 1.0), key=lambda item: item[0])]
    for job in jobs:
        job.begin()

    def speak(n):
        for action in whisper[:n]:
            action()
        del whisper[:n]

    speak(1)
    jobs[0].stage_near()
    speak(5)
    for k in range(count):
        if k + 1 < count:
            jobs[k + 1].stage_near()
        jobs[k].stage_far()
        speak(5)
        if k:
            jobs[k - 1].stage_own()
        jobs[k].stage_line()
    speak(len(whisper))
    jobs[-1].stage_own()
    for job in jobs:
        job.finish()
    word.finish()


def scatter_all(mine, other, note):
    count = len(mine)
    shapes = [g.shape[1:] for g in mine]
    spread = jax.ShapeDtypeStruct((16,) + note.shape, note.dtype)
    scratch = []
    for shape in shapes:
        for lead in ((16,), (16,), (ZS, 2), (ZS,), (2, ZS)):
            scratch.append(pltpu.VMEM(lead + shape, jnp.bfloat16))
    dma = pltpu.SemaphoreType.DMA
    scratch += [
        dma((count,)),
        dma((count, ZS)),
        dma((count, ZS)),
        dma((count, ZS, 2)),
        dma((count, ZS, 2)),
        dma((count, ZS)),
        dma((count, ZS)),
        dma((count, 2, ZS)),
        dma((count, 2, ZS)),
    ]
    outs = pl.pallas_call(
        functools.partial(scatter_kernel, count),
        out_shape=[jax.ShapeDtypeStruct(s, jnp.float32) for s in shapes] + [spread, spread],
        in_specs=[ANY] * (2 * count) + [VMEM],
        out_specs=[VMEM] * count + [ANY, ANY],
        scratch_shapes=scratch + gather_sems(1),
        compiler_params=pltpu.CompilerParams(
            collective_id=1, has_side_effects=True, vmem_limit_bytes=VMEM_LIMIT
        ),
        name="scatter_all",
    )(*mine, *other, note)
    return outs[:count], outs[count], outs[count + 1]


def gather_plain(shards):
    own = [lax.all_gather(s, "dp", axis=0) for s in shards]
    pair = [lax.all_gather(g, "fsdp", axis=0) for g in own]
    other = 1 - lax.axis_index("fsdp")
    return own, [lax.dynamic_index_in_dim(p, other, 0, keepdims=False) for p in pair]


def scatter_plain(mine, other, note):
    c = lax.axis_index("fsdp")
    results = []
    for own, sib in zip(mine, other):
        pair = jnp.where(c == 0, jnp.stack([own, sib]), jnp.stack([sib, own]))
        half = lax.psum_scatter(pair, "fsdp", scatter_dimension=0, tiled=False)
        results.append(
            lax.psum_scatter(
                half.astype(jnp.float32), "dp", scatter_dimension=0, tiled=False
            )
        )
    own, sib = gather_plain([note])
    return results, own[0], sib[0]


def masked_scores(query, keys, valid_keys):
    scaled = jnp.einsum(
        "blhc,bmhc->bhlm", query, keys, preferred_element_type=jnp.float32
    ) * HD ** (-0.5)
    return jnp.where(valid_keys[:, None, None, :], scaled, NEG_FILL)


def shards(
    fast,
    tokens,
    condition,
    cotangent,
    image_grids,
    noise_bins,
    bin_weights,
    w_qkv,
    b_query,
    b_value,
    w_proj,
    b_proj,
    w_fc1,
    b_fc1,
    w_fc2,
    b_fc2,
    w_ada,
    b_ada,
):
    images = tokens.shape[0]
    row_count = images * SEQ
    core = lax.axis_index("fsdp")

    def join(own, sib):
        return jnp.where(
            core == 0,
            jnp.concatenate([own, sib], axis=-1),
            jnp.concatenate([sib, own], axis=-1),
        )

    def split(full):
        half = full.shape[-1] // 2
        low, high = full[..., :half], full[..., half:]
        return jnp.where(core == 0, low, high), jnp.where(core == 0, high, low)

    token_count = image_grids[:, 0] * image_grids[:, 1]
    valid_keys = lax.broadcasted_iota(jnp.int32, (images, SEQ), 1) < token_count[:, None]
    bin_table = (noise_bins[:, None] == lax.broadcasted_iota(jnp.int32, (images, BINS), 1)).astype(
        jnp.float32
    )
    local_counts = jnp.sum(bin_table * token_count[:, None].astype(jnp.float32), axis=0)
    cond_float = condition.astype(jnp.float32)
    silu_cond = jax.nn.silu(cond_float).astype(jnp.bfloat16)
    lanes = 128
    head = jnp.concatenate([local_counts, jnp.zeros((lanes - BINS,), jnp.float32)])[None]
    facts = jnp.concatenate(
        [
            head,
            silu_cond.astype(jnp.float32).reshape(-1, lanes),
            jnp.zeros((6, lanes), jnp.float32),
        ]
    )
    gather = gather_all if fast else gather_plain
    scatter = scatter_all if fast else scatter_plain
    own, sib = gather([facts, w_qkv, w_proj, w_fc1, w_fc2])
    flat = lambda w: w.reshape(-1, w.shape[-1])
    qkv_own, proj_own, fc1_own, fc2_own = [flat(w) for w in own[1:]]
    qkv_sib, proj_sib, fc1_sib, fc2_sib = [flat(w) for w in sib[1:]]
    counts = (jnp.sum(own[0], axis=0) + jnp.sum(sib[0], axis=0))[0, :BINS]
    bin_scale = bin_weights.astype(jnp.float32) * (jnp.sum(counts) / BINS) / counts
    image_scale = jnp.sum(bin_table * bin_scale[None, :], axis=1)

    def times(left, right):
        return jnp.dot(left, right, preferred_element_type=jnp.float32)

    def times_t(left, right):
        return lax.dot_general(left, right, LAST_DIMS, preferred_element_type=jnp.float32)

    def outer(left, right):
        return lax.dot_general(left, right, ROWS_DIMS, preferred_element_type=jnp.float32)

    modul = lax.dot_general(silu_cond, w_ada, LAST_DIMS, preferred_element_type=jnp.float32) + b_ada
    pieces = [modul[:, None, part_index * D : (part_index + 1) * D] for part_index in range(6)]
    shift_one, scale_one, gate_one, shift_two, scale_two, gate_two = pieces
    token_float = tokens.astype(jnp.float32)
    normed_one, inverse_one = norm_rows(token_float)
    attn_in = (
        (normed_one * (1.0 + scale_one) + shift_one).astype(jnp.bfloat16).reshape(row_count, D)
    )
    bias_qkv = jnp.concatenate([b_query, jnp.zeros_like(b_query), b_value])
    qkv_all = (join(times(attn_in, qkv_own), times(attn_in, qkv_sib)) + bias_qkv).astype(
        jnp.bfloat16
    )
    qkv_heads = qkv_all.reshape(images, SEQ, 3, H, HD)
    query, keys, values = (qkv_heads[:, :, 0], qkv_heads[:, :, 1], qkv_heads[:, :, 2])
    scores = masked_scores(query, keys, valid_keys)
    row_max = jnp.max(scores, axis=-1, keepdims=True)
    exponent = jnp.exp(scores - row_max)
    row_total = jnp.sum(exponent, axis=-1, keepdims=True)
    soft_probs = exponent / row_total
    log_total = row_max + jnp.log(row_total)
    attended = jnp.einsum(
        "bhlm,bmhc->blhc",
        soft_probs.astype(jnp.bfloat16),
        values,
        preferred_element_type=jnp.float32,
    )
    attended = attended.astype(jnp.bfloat16).reshape(row_count, D)
    attn_out = (join(times(attended, proj_own), times(attended, proj_sib)) + b_proj).reshape(
        images, SEQ, D
    )
    middle = token_float + gate_one * attn_out
    normed_two, inverse_two = norm_rows(middle)
    mlp_in = (normed_two * (1.0 + scale_two) + shift_two).astype(jnp.bfloat16).reshape(row_count, D)
    bias_own, bias_sib = split(b_fc1)
    hidden_own = times(mlp_in, fc1_own) + bias_own
    hidden_sib = times(mlp_in, fc1_sib) + bias_sib
    active = join(
        gelu_tanh(hidden_own).astype(jnp.bfloat16), gelu_tanh(hidden_sib).astype(jnp.bfloat16)
    )
    branch = (join(times(active, fc2_own), times(active, fc2_sib)) + b_fc2).reshape(
        images, SEQ, D
    )
    result = (middle + gate_two * branch).astype(jnp.bfloat16)
    grad_out = (
        cotangent.astype(jnp.float32)
        * (valid_keys.astype(jnp.float32) * image_scale[:, None])[:, :, None]
    )
    d_gate_two = jnp.sum(grad_out * branch, axis=1)
    d_branch = (gate_two * grad_out).astype(jnp.bfloat16).reshape(row_count, D)
    d_branch_own, d_branch_sib = split(d_branch)
    fc2_mine, fc2_other = outer(active, d_branch_own), outer(active, d_branch_sib)
    bias_fc2 = jnp.sum(d_branch, axis=0, dtype=jnp.float32)
    d_active = times_t(d_branch_own, fc2_own) + times_t(d_branch_sib, fc2_sib)
    d_active_own, d_active_sib = split(d_active)
    d_hidden_own = jax.vjp(gelu_tanh, hidden_own)[1](d_active_own)[0].astype(jnp.bfloat16)
    d_hidden_sib = jax.vjp(gelu_tanh, hidden_sib)[1](d_active_sib)[0].astype(jnp.bfloat16)
    fc1_mine, fc1_other = outer(mlp_in, d_hidden_own), outer(mlp_in, d_hidden_sib)
    bias_fc1 = join(
        jnp.sum(d_hidden_own, axis=0, dtype=jnp.float32),
        jnp.sum(d_hidden_sib, axis=0, dtype=jnp.float32),
    )
    d_mlp_in = (times_t(d_hidden_own, fc1_own) + times_t(d_hidden_sib, fc1_sib)).reshape(
        images, SEQ, D
    )
    d_shift_two = jnp.sum(d_mlp_in, axis=1)
    d_scale_two = jnp.sum(d_mlp_in * normed_two, axis=1)
    d_middle = grad_out + norm_back(d_mlp_in * (1.0 + scale_two), normed_two, inverse_two)
    d_gate_one = jnp.sum(d_middle * attn_out, axis=1)
    d_attn = (gate_one * d_middle).astype(jnp.bfloat16).reshape(row_count, D)
    d_attn_own, d_attn_sib = split(d_attn)
    proj_mine, proj_other = outer(attended, d_attn_own), outer(attended, d_attn_sib)
    bias_proj = jnp.sum(d_attn, axis=0, dtype=jnp.float32)
    d_attended = times_t(d_attn_own, proj_own) + times_t(d_attn_sib, proj_sib)
    d_attended = d_attended.astype(jnp.bfloat16).reshape(images, SEQ, H, HD)
    soft_again = jnp.exp(masked_scores(query, keys, valid_keys) - log_total)
    grad_values = jnp.einsum(
        "bhlm,blhc->bmhc",
        soft_again.astype(jnp.bfloat16),
        d_attended,
        preferred_element_type=jnp.float32,
    )
    d_probs = jnp.einsum("blhc,bmhc->bhlm", d_attended, values, preferred_element_type=jnp.float32)
    d_scores = soft_again * (d_probs - jnp.sum(soft_again * d_probs, axis=-1, keepdims=True))
    d_scores = jnp.where(valid_keys[:, None, None, :], d_scores, 0.0).astype(jnp.bfloat16)
    grad_query = jnp.einsum(
        "bhlm,bmhc->blhc", d_scores, keys, preferred_element_type=jnp.float32
    ) * HD ** (-0.5)
    grad_keys = jnp.einsum(
        "bhlm,blhc->bmhc", d_scores, query, preferred_element_type=jnp.float32
    ) * HD ** (-0.5)
    d_qkv = (
        jnp.stack([grad_query, grad_keys, grad_values], axis=2)
        .astype(jnp.bfloat16)
        .reshape(row_count, 3 * D)
    )
    d_qkv_own, d_qkv_sib = split(d_qkv)
    qkv_mine, qkv_other = outer(attn_in, d_qkv_own), outer(attn_in, d_qkv_sib)
    bias_query = jnp.sum(d_qkv[:, :D], axis=0, dtype=jnp.float32)
    bias_value = jnp.sum(d_qkv[:, 2 * D :], axis=0, dtype=jnp.float32)
    d_attn_in = (times_t(d_qkv_own, qkv_own) + times_t(d_qkv_sib, qkv_sib)).reshape(
        images, SEQ, D
    )
    d_shift_one = jnp.sum(d_attn_in, axis=1)
    d_scale_one = jnp.sum(d_attn_in * normed_one, axis=1)
    grad_tokens = (
        d_middle + norm_back(d_attn_in * (1.0 + scale_one), normed_one, inverse_one)
    ).astype(jnp.bfloat16)
    d_modul = jnp.concatenate(
        [d_shift_one, d_scale_one, d_gate_one, d_shift_two, d_scale_two, d_gate_two], axis=1
    ).astype(jnp.bfloat16)
    silu_pull = jax.vjp(jax.nn.silu, cond_float)[1]
    grad_condition = silu_pull(jnp.dot(d_modul, w_ada, preferred_element_type=jnp.float32))[0]
    biases = [bias_query, bias_value, bias_proj, bias_fc1, bias_fc2]
    note = jnp.concatenate(
        biases + [d_modul.astype(jnp.float32).reshape(-1), jnp.zeros((2 * lanes,), jnp.float32)]
    ).reshape(-1, lanes)

    def blocks(grad, shard):
        return grad.astype(jnp.bfloat16).reshape((-1,) + shard.shape)

    owners = [w_fc1, w_fc2, w_qkv, w_proj]
    mine = [blocks(g, w) for g, w in zip([fc1_mine, fc2_mine, qkv_mine, proj_mine], owners)]
    other = [blocks(g, w) for g, w in zip([fc1_other, fc2_other, qkv_other, proj_other], owners)]
    (grad_fc1, grad_fc2, grad_qkv, grad_proj), note_own, note_sib = scatter(mine, other, note)
    total_note = (jnp.sum(note_own, axis=0) + jnp.sum(note_sib, axis=0)).reshape(-1)
    summed, start = [], 0
    for vector in biases + [b_ada]:
        summed.append(total_note[start : start + vector.shape[0]])
        start += vector.shape[0]
    first = start - b_ada.shape[0]
    share_rows = 6 * D // lax.axis_size(("dp", "fsdp"))
    own_start = first + lax.axis_index(("dp", "fsdp")) * share_rows
    notes = jnp.concatenate([note_own, note_sib]).reshape(-1, note.size)
    silus = jnp.concatenate([own[0], sib[0]])[:, 1:10].reshape(-1, D)
    columns = lax.dynamic_slice_in_dim(notes, own_start, share_rows, 1)
    grad_ada = lax.dot_general(
        columns.astype(jnp.bfloat16),
        silus.astype(jnp.bfloat16),
        ROWS_DIMS,
        preferred_element_type=jnp.float32,
    )
    return (
        result,
        grad_tokens,
        grad_condition,
        grad_qkv,
        summed[0],
        summed[1],
        grad_proj,
        summed[2],
        grad_fc1,
        summed[3],
        grad_fc2,
        summed[4],
        grad_ada,
        summed[5],
    )


def solution(mesh):
    in_specs = (
        P(("dp", "fsdp"), None, None),
        P(("dp", "fsdp"), None),
        P(("dp", "fsdp"), None, None),
        P(("dp", "fsdp"), None),
        P(("dp", "fsdp")),
        P(),
        P("dp", "fsdp"),
        P(),
        P(),
        P("dp", "fsdp"),
        P(),
        P("dp", "fsdp"),
        P(),
        P("dp", "fsdp"),
        P(),
        P(),
        P(),
    )
    out_specs = (
        P(("dp", "fsdp"), None, None),
        P(("dp", "fsdp"), None, None),
        P(("dp", "fsdp"), None),
        P("dp", "fsdp"),
        P(),
        P(),
        P("dp", "fsdp"),
        P(),
        P("dp", "fsdp"),
        P(),
        P("dp", "fsdp"),
        P(),
        P(("dp", "fsdp"), None),
        P(),
    )
    return jax.shard_map(
        functools.partial(shards, dict(mesh.shape) == {"dp": 16, "fsdp": 2}),
        mesh=mesh,
        in_specs=in_specs,
        out_specs=out_specs,
        check_vma=False,
    )
```

```python
import functools

import jax
import jax.numpy as jnp
from jax import lax
from jax.experimental import pallas as pl
from jax.experimental.pallas import tpu as pltpu
from jax.sharding import PartitionSpec as P

D = 1152
H = 16
HD = 72
BINS = 16
SEQ = 256


NEG_FILL = -1e30
NORM_EPS = 1e-06
GELU_COEF = 0.7978845608028654
CUBIC_COEF = 0.044715
ROWS_DIMS = (((0,), (0,)), ((), ()))
LAST_DIMS = (((1,), (1,)), ((), ()))


def gelu_tanh(values_in):
    return (
        0.5
        * values_in
        * (1.0 + jnp.tanh(GELU_COEF * (values_in + CUBIC_COEF * values_in * values_in * values_in)))
    )


def norm_rows(inputs):
    centered = inputs - jnp.mean(inputs, axis=-1, keepdims=True)
    inverse = lax.rsqrt(jnp.mean(centered * centered, axis=-1, keepdims=True) + NORM_EPS)
    return (centered * inverse, inverse)


def norm_back(grad_normed, normed, inverse):
    centered_grad = grad_normed - jnp.mean(grad_normed, axis=-1, keepdims=True)
    return inverse * (
        centered_grad - normed * jnp.mean(grad_normed * normed, axis=-1, keepdims=True)
    )


VMEM_LIMIT = 66_000_000
ANY = pl.BlockSpec(memory_space=pl.ANY)
VMEM = pl.BlockSpec(memory_space=pltpu.VMEM)
ZS = 4
TILE = 256
MID = ((72, 1728), (72, 576))
ORDER = (
    ("near", 0, 1),
    ("near", 0, 0),
    ("near", 1, 0),
    ("near", 2, 0),
    ("line", 0, 0),
    ("far", 1, 0),
    ("line", 0, 1),
    ("near", 3, 0),
    ("near", 2, 1),
    ("near", 1, 1),
    ("line", 2, 0),
    ("line", 1, 0),
    ("line", 0, 2),
    ("far", 3, 0),
    ("line", 2, 1),
    ("line", 2, 2),
    ("far", 1, 1),
    ("near", 3, 1),
    ("line", 3, 0),
    ("line", 1, 1),
    ("far", 0, 0),
    ("far", 3, 1),
    ("line", 1, 2),
    ("line", 3, 1),
    ("line", 3, 2),
    ("own", 1, 0),
    ("own", 0, 0),
    ("far", 2, 0),
    ("own", 2, 0),
    ("own", 3, 0),
)
OFFSETS = (0, -1, 1, -2, 2, -3, 3)
GATHER_MID = (3, 4)
GATHER_ORDER = (
    ("column", 1, 0),
    ("column", 2, 0),
    ("column", 0, 0),
    ("column", 1, 1),
    ("column", 3, 0),
    ("column", 2, 1),
    ("column", 1, -1),
    ("column", 0, 1),
    ("column", 2, -1),
    ("relay", 1, 0),
    ("column", 4, 0),
    ("column", 2, 2),
    ("column", 1, -2),
    ("column", 0, 2),
    ("column", 2, -2),
    ("column", 1, -3),
    ("column", 1, 2),
    ("relay", 1, 1),
    ("relay", 3, 0),
    ("column", 1, 3),
    ("relay", 4, 0),
    ("relay", 1, -1),
    ("relay", 0, 1),
    ("column", 2, 3),
    ("column", 3, 1),
    ("column", 4, -1),
    ("column", 0, -1),
    ("relay", 1, 2),
    ("relay", 1, 3),
    ("relay", 2, -1),
    ("relay", 2, 1),
    ("relay", 3, -1),
    ("last", 1, 0),
    ("relay", 1, -3),
    ("last", 1, 1),
    ("column", 0, -2),
    ("relay", 1, -2),
    ("relay", 4, 1),
    ("last", 1, -1),
    ("column", 0, 3),
    ("column", 2, -3),
    ("column", 3, -1),
    ("relay", 3, 1),
    ("relay", 0, -1),
    ("relay", 2, -2),
    ("relay", 4, 2),
    ("relay", 2, 0),
    ("last", 1, 2),
    ("relay", 2, 3),
    ("last", 4, 0),
    ("relay", 4, -1),
    ("last", 1, 3),
    ("last", 1, -3),
    ("column", 4, 1),
    ("relay", 0, 2),
    ("last", 1, -2),
    ("relay", 3, -2),
    ("column", 0, -3),
    ("relay", 2, 2),
    ("last", 2, 2),
    ("last", 2, -1),
    ("relay", 4, -2),
    ("last", 2, 0),
    ("relay", 0, 3),
    ("last", 2, 1),
    ("relay", 4, 3),
    ("last", 2, -2),
    ("last", 2, 3),
    ("relay", 2, -3),
    ("relay", 3, -3),
    ("relay", 0, 0),
    ("column", 3, 2),
    ("last", 2, -3),
    ("column", 3, 3),
    ("relay", 3, 2),
    ("column", 4, -2),
    ("last", 0, 1),
    ("column", 4, 2),
    ("relay", 3, 3),
    ("relay", 0, -3),
    ("column", 3, -2),
    ("relay", 4, -3),
    ("last", 3, 1),
    ("last", 3, 2),
    ("last", 3, -1),
    ("column", 4, -3),
    ("column", 4, 3),
    ("last", 4, -1),
    ("last", 0, -3),
    ("column", 3, -3),
    ("last", 4, 2),
    ("last", 0, 2),
    ("last", 4, -2),
    ("last", 0, 3),
    ("last", 0, -1),
    ("relay", 0, -2),
    ("last", 3, -2),
    ("last", 4, 1),
    ("last", 3, 3),
    ("last", 0, -2),
    ("last", 3, 0),
    ("last", 4, -3),
    ("last", 4, 3),
    ("last", 3, -3),
    ("last", 0, 0),
)


class Place:
    def __init__(self):
        self.i = lax.axis_index("dp")
        self.c = lax.axis_index("fsdp")
        self.z = self.i // 4
        self.q = self.i % 4
        self.y = self.q // 2
        self.x = self.q % 2
        self.to_y = 2 * (1 - 2 * self.y)
        self.to_x = 1 - 2 * self.x

    def partners(self, level):
        odd = level % 2
        first = odd * self.to_x + (1 - odd) * self.to_y
        return first, self.to_x + self.to_y - first

    def greet(self):
        barrier = pltpu.get_barrier_semaphore()

        def signal(i, c):
            pl.semaphore_signal(
                barrier,
                inc=1,
                device_id={"dp": i, "fsdp": c},
                device_id_type=pl.DeviceIdType.MESH,
            )

        signal(self.i, 1 - self.c)
        signal(self.i + self.to_y, self.c)
        signal(self.i + self.to_x, self.c)
        up, down = self.z < ZS - 1, self.z > 0
        pl.when(up)(lambda: signal(self.i + 4, self.c))
        pl.when(down)(lambda: signal(self.i - 4, self.c))
        pl.semaphore_wait(barrier, 3 + up.astype(jnp.int32) + down.astype(jnp.int32))


def remote(src, dst, send, recv, i, c):
    return pltpu.make_async_remote_copy(
        src_ref=src,
        dst_ref=dst,
        send_sem=send,
        recv_sem=recv,
        device_id={"dp": i, "fsdp": c},
        device_id_type=pl.DeviceIdType.MESH,
    )


def gather_sems(count):
    dma = pltpu.SemaphoreType.DMA
    return [
        dma((count, 16)),
        dma((count, 16)),
        dma((count, 2, ZS, 2)),
        dma((count, ZS, 3)),
        dma((count, 16)),
        dma((count,)),
    ]


class Gather:
    def __init__(self, at, k, shard, own, sib, sems, mid=False):
        self.mid = mid
        self.at, self.k, self.shard, self.own, self.sib = at, k, shard, own, sib
        self.recv, self.core, self.line, self.pair, self.over, self.local = sems

    def send(self, src, j, sem, i):
        return remote(src, self.own.at[j], sem, self.recv.at[self.k, j], i, self.at.c)

    def across(self, src, j):
        at, k = self.at, self.k
        return remote(
            src, self.sib.at[j], self.over.at[k, j], self.core.at[k, j], at.i, 1 - at.c
        )

    def arrived(self, j):
        at = self.at
        remote(
            self.own.at[j],
            self.own.at[j],
            self.over.at[self.k, j],
            self.recv.at[self.k, j],
            at.i,
            1 - at.c,
        ).wait_recv()

    def pieces(self, level):
        first, second = self.at.partners(level)
        column = level * 4 + self.at.q
        return first, second, column

    def guard(self, off, run):
        level = self.at.z + off
        if off == 0:
            run(level)
        else:
            pl.when((level >= 0) & (level < ZS))(lambda: run(level))

    def line_copies(self, off, level, slot, src, j):
        at, k = self.at, self.k
        out = []
        if off <= 0:
            copy = self.send(src, j, self.line.at[k, 0, level, slot], at.i + 4)
            out.append((at.z < ZS - 1, copy))
        if off >= 0:
            copy = self.send(src, j, self.line.at[k, 1, level, slot], at.i - 4)
            out.append((at.z > 0, copy))
        return out

    def column_copies(self, off, level):
        at, k = self.at, self.k
        first, second, j = self.pieces(level)
        src = self.shard if off == 0 else self.own.at[j]
        lines = self.line_copies(off, level, 0, src, j)
        near = [self.send(src, j, self.pair.at[k, level, 0], at.i + first)]
        rest = [self.send(src, j, self.pair.at[k, level, 1], at.i + second), self.across(src, j)]
        if not self.mid:
            return [], lines, near + rest
        return (near if off == 0 else []), lines, rest

    def column(self, off):
        def run(level):
            if off:
                self.arrived(level * 4 + self.at.q)
            before, lines, after = self.column_copies(off, level)
            for copy in before:
                copy.start()
            for where, copy in lines:
                pl.when(where)(copy.start)
            for copy in after:
                copy.start()
            if off == 0:
                self.keep().start()

        self.guard(off, run)

    def keep(self):
        return pltpu.make_async_copy(
            self.shard, self.own.at[self.at.i], self.local.at[self.k]
        )

    def relay_copies(self, off, level):
        first, second, column = self.pieces(level)
        j = column + first
        src = self.own.at[j]
        lines = self.line_copies(off, level, 1, src, j) if self.mid else []
        return lines, [
            self.send(src, j, self.pair.at[self.k, level, 2], self.at.i + second),
            self.across(src, j),
        ]

    def relay(self, off):
        def run(level):
            first, _, column = self.pieces(level)
            self.arrived(column + first)
            lines, after = self.relay_copies(off, level)
            for where, copy in lines:
                pl.when(where)(copy.start)
            for copy in after:
                copy.start()

        self.guard(off, run)

    def last_copies(self, level):
        first, second, column = self.pieces(level)
        return [(j, self.across(self.own.at[j], j)) for j in (column + second, column + first + second)]

    def last(self, off):
        def run(level):
            for j, copy in self.last_copies(level):
                self.arrived(j)
                copy.start()

        self.guard(off, run)

    def finish(self):
        at = self.at
        self.keep().wait()
        for off in OFFSETS:

            def run(level, off=off):
                before, lines, after = self.column_copies(off, level)
                more, relays = self.relay_copies(off, level)
                for where, copy in lines + more:
                    pl.when(where)(copy.wait_send)
                for copy in before + after + relays:
                    copy.wait_send()
                for _, copy in self.last_copies(level):
                    copy.wait_send()

            self.guard(off, run)

        @pl.loop(0, 16)
        def _(j):
            self.across(self.sib.at[j], j).wait_recv()

    def events(self, start, span):
        out = []
        for off in OFFSETS:
            far = abs(off)
            out.append((start + span * 0.15 * far, functools.partial(self.column, off)))
            out.append((start + span * (0.3 + 0.2 * far), functools.partial(self.relay, off)))
            out.append((start + span * (0.6 + 0.2 * far), functools.partial(self.last, off)))
        return out


def gather_kernel(count, *refs):
    shards, own, sib = refs[:count], refs[count : 2 * count], refs[2 * count : 3 * count]
    sems = refs[3 * count :]
    at = Place()
    at.greet()
    jobs = [
        Gather(at, k, shards[k], own[k], sib[k], sems, k in GATHER_MID) for k in range(count)
    ]
    for step, k, off in GATHER_ORDER:
        getattr(jobs[k], step)(off)
    for job in jobs:
        job.finish()


def gather_all(shards):
    count = len(shards)
    spread = [jax.ShapeDtypeStruct((16,) + s.shape, s.dtype) for s in shards]
    outs = pl.pallas_call(
        functools.partial(gather_kernel, count),
        out_shape=spread + spread,
        in_specs=[VMEM] * count,
        out_specs=[ANY] * (2 * count),
        scratch_shapes=gather_sems(count),
        compiler_params=pltpu.CompilerParams(
            collective_id=0, has_side_effects=True, vmem_limit_bytes=16_000_000
        ),
        name="gather_all",
    )(*shards)
    return outs[:count], outs[count:]


def blocked(shape):
    rows, cols = shape
    return (rows, cols) if rows % 16 == 0 else (rows // 8, 8, cols)


def total(*values):
    out = values[0].astype(jnp.float32)
    for value in values[1:]:
        out = out + value.astype(jnp.float32)
    return out


class Scatter:
    def __init__(self, at, k, ins, result, bufs, sems):
        self.at, self.k = at, k
        self.left, self.right, self.away = ins
        self.result = result
        self.left_sib, self.right_sib, self.held, self.near, self.far, self.line = bufs
        self.mid = self.line.shape[2] == 2
        (
            self.swap_send,
            self.swap_recv,
            self.near_send,
            self.near_recv,
            self.far_send,
            self.far_recv,
            self.line_send,
            self.line_recv,
        ) = sems

    def swaps(self):
        at, k = self.at, self.k
        pairs = ((self.left, self.left_sib), (self.away, self.right_sib))
        return [
            remote(
                src, dst, self.swap_send.at[k, s], self.swap_recv.at[k, s], at.i, 1 - at.c
            )
            for s, (src, dst) in enumerate(pairs)
        ]

    def near_copies(self, level):
        at, k = self.at, self.k
        first, second = at.partners(level)
        column = level * 4 + at.q
        return [
            remote(
                self.held.at[j],
                self.near.at[level, slot],
                self.near_send.at[k, level, slot],
                self.near_recv.at[k, level, slot],
                at.i + second,
                at.c,
            )
            for slot, j in enumerate((column + second, column + first + second))
        ]

    def far_copy(self, level):
        at, k = self.at, self.k
        first, _ = at.partners(level)
        j = level * 4 + at.q + first
        slot = 0 if self.mid else level
        return remote(
            self.held.at[j],
            self.far.at[slot],
            self.far_send.at[k, slot],
            self.far_recv.at[k, slot],
            at.i + first,
            at.c,
        )

    def line_copies(self, way, level):
        at, k = self.at, self.k
        first, _ = at.partners(level)
        column = level * 4 + at.q
        return [
            remote(
                self.held.at[j],
                self.line.at[way, level, slot],
                self.line_send.at[k, way, level, slot],
                self.line_recv.at[k, way, level, slot],
                at.i + (4 if way == 0 else -4),
                at.c,
            )
            for slot, j in enumerate((column, column + first)[: 2 if self.mid else 1])
        ]

    def line_arrived(self, way, level):
        for copy in self.line_copies(way, level):
            if way == 0:
                pl.when(self.at.z > 0)(copy.wait_recv)
            else:
                pl.when(self.at.z < ZS - 1)(copy.wait_recv)

    def begin(self):
        for copy in self.swaps():
            copy.start()

        zeros = jnp.zeros(self.line.shape[3:], self.line.dtype)

        @pl.when(self.at.z == 0)
        def _():
            @pl.loop(0, ZS)
            def _(level):
                for slot in range(self.line.shape[2]):
                    self.line[0, level, slot] = zeros

        @pl.when(self.at.z == ZS - 1)
        def _():
            @pl.loop(0, ZS)
            def _(level):
                for slot in range(self.line.shape[2]):
                    self.line[1, level, slot] = zeros

    def multiply(self, level):
        cols = self.held.shape[-1]
        rows = self.left.shape[0] // 16
        group = max(1, 288 // rows)
        height = group * rows
        wide = cols // TILE

        def block(part, columns):
            where = pl.ds(pl.multiple_of((level * 4 + part * group) * rows, 32), height)
            value = jnp.dot(
                self.left[where, :], self.right[:, columns], preferred_element_type=jnp.float32
            ) + jnp.dot(
                self.left_sib[where, :],
                self.right_sib[:, columns],
                preferred_element_type=jnp.float32,
            )
            for g in range(group):
                piece = value[g * rows : (g + 1) * rows]
                if len(self.held.shape) == 4:
                    piece = piece.reshape((rows // 8, 8, piece.shape[-1]))
                self.held[level * 4 + part * group + g, ..., columns] = piece.astype(jnp.bfloat16)

        @pl.loop(0, 4 // group)
        def _(part):
            @pl.loop(0, wide)
            def _(t):
                block(part, pl.ds(pl.multiple_of(t * TILE, TILE), TILE))

            if cols % TILE:
                block(part, pl.ds(wide * TILE, cols % TILE))

    def ready(self):
        for copy in self.swaps():
            copy.wait_recv()

    def stage_near(self, pair):
        @pl.loop(0, 2)
        def _(t):
            level = (1 - pair) * 3 * t + pair * (1 + t)
            self.multiply(level)
            for copy in self.near_copies(level):
                copy.start()

    def stage_far(self, pair):
        if self.mid:
            self.far_mid()
        else:
            pl.loop(0, 2)(lambda t: self.far_level((1 - pair) * 3 * t + pair * (1 + t)))

    def far_level(self, level):
        first, _ = self.at.partners(level)
        j = level * 4 + self.at.q + first
        for copy in self.near_copies(level):
            copy.wait_recv()
        self.held[j] = total(self.held[j], self.near[level, 1]).astype(jnp.bfloat16)
        self.far_copy(level).start()

    def far_mid(self):
        level = self.at.z
        first, _ = self.at.partners(level)
        j = level * 4 + self.at.q + first
        for copy in self.near_copies(level):
            copy.wait_recv()
        self.line_arrived(0, level)
        self.line_arrived(1, level)
        self.held[j] = total(
            self.held[j], self.near[level, 1], self.line[0, level, 1], self.line[1, level, 1]
        ).astype(jnp.bfloat16)
        self.far_copy(level).start()

    def pass_on(self, way, level):
        first, _ = self.at.partners(level)
        column = level * 4 + self.at.q
        if self.mid:
            for copy in self.near_copies(level):
                copy.wait_recv()
        else:
            self.far_copy(level).wait_recv()
        self.line_arrived(way, level)
        copies = self.line_copies(way, level)
        for slot, copy in enumerate(copies):
            j = column + slot * first
            values = [self.held[j], self.near[level, slot], self.line[way, level, slot]]
            if not self.mid:
                values.append(self.far[level])
            self.held[j] = total(*values).astype(jnp.bfloat16)
            copy.start()

    def stage_line(self, back):
        z = self.at.z
        if back < ZS - 1:
            up, down = ZS - 1 - back, back
            pl.when(z < up)(lambda: self.pass_on(0, up))
            pl.when(z > down)(lambda: self.pass_on(1, down))

    def stage_own(self, _):
        z = self.at.z
        j = self.at.i
        self.far_copy(z).wait_recv()
        if not self.mid:
            self.line_arrived(0, z)
            self.line_arrived(1, z)
        whole = total(
            self.held[j],
            self.near[z, 0],
            self.far[0 if self.mid else z],
            self.line[0, z, 0],
            self.line[1, z, 0],
        )
        self.result[...] = whole.reshape(self.result.shape)

    def finish(self):
        z = self.at.z
        for copy in self.swaps():
            copy.wait_send()

        if self.mid:
            self.far_copy(z).wait_send()

        @pl.loop(0, ZS)
        def _(level):
            for copy in self.near_copies(level):
                copy.wait_send()
            if not self.mid:
                self.far_copy(level).wait_send()
            for way in (0, 1):
                beyond = level > z if way == 0 else level < z
                for copy in self.line_copies(way, level):
                    pl.when(beyond)(copy.wait_send)


def scatter_kernel(count, *refs):
    refs = list(refs)

    def take(n):
        out = refs[:n]
        del refs[:n]
        return out

    ins = [take(3) for _ in range(count)]
    note = take(1)[0]
    results = take(count)
    note_own, note_sib = take(2)
    bufs = [take(6) for _ in range(count)]
    sems, note_sems = take(8), take(6)
    at = Place()
    at.greet()
    jobs = [Scatter(at, k, ins[k], results[k], bufs[k], sems) for k in range(count)]
    word = Gather(at, 0, note, note_own, note_sib, note_sems)
    whisper = [action for _, action in sorted(word.events(0.0, 1.0), key=lambda item: item[0])]
    for job in jobs:
        job.begin()

    def speak(n):
        for action in whisper[:n]:
            action()
        del whisper[:n]

    speak(1)
    seen = set()
    for stage, k, part in ORDER:
        if k not in seen:
            jobs[k].ready()
            seen.add(k)
        getattr(jobs[k], "stage_" + stage)(part)
        speak(1)
    speak(len(whisper))
    for job in jobs:
        job.finish()
    word.finish()


def scatter_all(terms, note):
    count = len(terms)
    spread = jax.ShapeDtypeStruct((16,) + note.shape, note.dtype)
    scratch, operands = [], []
    for left, right, away, shard in terms:
        operands += [left, right, away]
        scratch.append(pltpu.VMEM(left.shape, jnp.bfloat16))
        scratch.append(pltpu.VMEM(right.shape, jnp.bfloat16))
        mid = shard.shape in MID
        piece = blocked(shard.shape)
        for lead in ((16,), (ZS, 2), (1 if mid else ZS,), (2, ZS, 2 if mid else 1)):
            scratch.append(pltpu.VMEM(lead + piece, jnp.bfloat16))
    dma = pltpu.SemaphoreType.DMA
    scratch += [
        dma((count, 2)),
        dma((count, 2)),
        dma((count, ZS, 2)),
        dma((count, ZS, 2)),
        dma((count, ZS)),
        dma((count, ZS)),
        dma((count, 2, ZS, 2)),
        dma((count, 2, ZS, 2)),
    ]
    outs = pl.pallas_call(
        functools.partial(scatter_kernel, count),
        out_shape=[jax.ShapeDtypeStruct(t[3].shape, jnp.float32) for t in terms]
        + [spread, spread],
        in_specs=[VMEM, VMEM, ANY] * count + [VMEM],
        out_specs=[VMEM] * count + [ANY, ANY],
        scratch_shapes=scratch + gather_sems(1),
        compiler_params=pltpu.CompilerParams(
            collective_id=1, has_side_effects=True, vmem_limit_bytes=VMEM_LIMIT
        ),
        name="scatter_all",
    )(*operands, note)
    return outs[:count], outs[count], outs[count + 1]


def gather_plain(shards):
    own = [lax.all_gather(s, "dp", axis=0) for s in shards]
    pair = [lax.all_gather(g, "fsdp", axis=0) for g in own]
    other = 1 - lax.axis_index("fsdp")
    return own, [lax.dynamic_index_in_dim(p, other, 0, keepdims=False) for p in pair]


def scatter_plain(terms, note):
    c = lax.axis_index("fsdp")
    results = []
    for left, right, away, shard in terms:
        own, sib = [
            jnp.dot(left, half, preferred_element_type=jnp.float32)
            .astype(jnp.bfloat16)
            .reshape((-1,) + shard.shape)
            for half in (right, away)
        ]
        pair = jnp.where(c == 0, jnp.stack([own, sib]), jnp.stack([sib, own]))
        half = lax.psum_scatter(pair, "fsdp", scatter_dimension=0, tiled=False)
        results.append(
            lax.psum_scatter(
                half.astype(jnp.float32), "dp", scatter_dimension=0, tiled=False
            )
        )
    own, sib = gather_plain([note])
    return results, own[0], sib[0]


def masked_scores(query, keys, valid_keys):
    scaled = jnp.einsum(
        "blhc,bmhc->bhlm", query, keys, preferred_element_type=jnp.float32
    ) * HD ** (-0.5)
    return jnp.where(valid_keys[:, None, None, :], scaled, NEG_FILL)


def shards(
    fast,
    tokens,
    condition,
    cotangent,
    image_grids,
    noise_bins,
    bin_weights,
    w_qkv,
    b_query,
    b_value,
    w_proj,
    b_proj,
    w_fc1,
    b_fc1,
    w_fc2,
    b_fc2,
    w_ada,
    b_ada,
):
    images = tokens.shape[0]
    row_count = images * SEQ
    core = lax.axis_index("fsdp")

    def join(own, sib):
        return jnp.where(
            core == 0,
            jnp.concatenate([own, sib], axis=-1),
            jnp.concatenate([sib, own], axis=-1),
        )

    def split(full):
        half = full.shape[-1] // 2
        low, high = full[..., :half], full[..., half:]
        return jnp.where(core == 0, low, high), jnp.where(core == 0, high, low)

    token_count = image_grids[:, 0] * image_grids[:, 1]
    valid_keys = lax.broadcasted_iota(jnp.int32, (images, SEQ), 1) < token_count[:, None]
    bin_table = (noise_bins[:, None] == lax.broadcasted_iota(jnp.int32, (images, BINS), 1)).astype(
        jnp.float32
    )
    local_counts = jnp.sum(bin_table * token_count[:, None].astype(jnp.float32), axis=0)
    cond_float = condition.astype(jnp.float32)
    silu_cond = jax.nn.silu(cond_float).astype(jnp.bfloat16)
    lanes = 128
    head = jnp.concatenate([local_counts, jnp.zeros((lanes - BINS,), jnp.float32)])[None]
    facts = jnp.concatenate(
        [
            head,
            silu_cond.astype(jnp.float32).reshape(-1, lanes),
            jnp.zeros((6, lanes), jnp.float32),
        ]
    )
    gather = gather_all if fast else gather_plain
    scatter = scatter_all if fast else scatter_plain
    own, sib = gather([facts, w_qkv, w_proj, w_fc1, w_fc2])
    flat = lambda w: w.reshape(-1, w.shape[-1])
    qkv_own, proj_own, fc1_own, fc2_own = [flat(w) for w in own[1:]]
    qkv_sib, proj_sib, fc1_sib, fc2_sib = [flat(w) for w in sib[1:]]
    counts = (jnp.sum(own[0], axis=0) + jnp.sum(sib[0], axis=0))[0, :BINS]
    bin_scale = bin_weights.astype(jnp.float32) * (jnp.sum(counts) / BINS) / counts
    image_scale = jnp.sum(bin_table * bin_scale[None, :], axis=1)

    def times(left, right):
        return jnp.dot(left, right, preferred_element_type=jnp.float32)

    def times_t(left, right):
        return lax.dot_general(left, right, LAST_DIMS, preferred_element_type=jnp.float32)

    modul = lax.dot_general(silu_cond, w_ada, LAST_DIMS, preferred_element_type=jnp.float32) + b_ada
    pieces = [modul[:, None, part_index * D : (part_index + 1) * D] for part_index in range(6)]
    shift_one, scale_one, gate_one, shift_two, scale_two, gate_two = pieces
    token_float = tokens.astype(jnp.float32)
    normed_one, inverse_one = norm_rows(token_float)
    attn_in = (
        (normed_one * (1.0 + scale_one) + shift_one).astype(jnp.bfloat16).reshape(row_count, D)
    )
    bias_qkv = jnp.concatenate([b_query, jnp.zeros_like(b_query), b_value])
    qkv_all = (join(times(attn_in, qkv_own), times(attn_in, qkv_sib)) + bias_qkv).astype(
        jnp.bfloat16
    )
    qkv_heads = qkv_all.reshape(images, SEQ, 3, H, HD)
    query, keys, values = (qkv_heads[:, :, 0], qkv_heads[:, :, 1], qkv_heads[:, :, 2])
    scores = masked_scores(query, keys, valid_keys)
    row_max = jnp.max(scores, axis=-1, keepdims=True)
    exponent = jnp.exp(scores - row_max)
    row_total = jnp.sum(exponent, axis=-1, keepdims=True)
    soft_probs = exponent / row_total
    log_total = row_max + jnp.log(row_total)
    attended = jnp.einsum(
        "bhlm,bmhc->blhc",
        soft_probs.astype(jnp.bfloat16),
        values,
        preferred_element_type=jnp.float32,
    )
    attended = attended.astype(jnp.bfloat16).reshape(row_count, D)
    attn_out = (join(times(attended, proj_own), times(attended, proj_sib)) + b_proj).reshape(
        images, SEQ, D
    )
    middle = token_float + gate_one * attn_out
    normed_two, inverse_two = norm_rows(middle)
    mlp_in = (normed_two * (1.0 + scale_two) + shift_two).astype(jnp.bfloat16).reshape(row_count, D)
    bias_own, bias_sib = split(b_fc1)
    hidden_own = times(mlp_in, fc1_own) + bias_own
    hidden_sib = times(mlp_in, fc1_sib) + bias_sib
    active = join(
        gelu_tanh(hidden_own).astype(jnp.bfloat16), gelu_tanh(hidden_sib).astype(jnp.bfloat16)
    )
    branch = (join(times(active, fc2_own), times(active, fc2_sib)) + b_fc2).reshape(
        images, SEQ, D
    )
    result = (middle + gate_two * branch).astype(jnp.bfloat16)
    grad_out = (
        cotangent.astype(jnp.float32)
        * (valid_keys.astype(jnp.float32) * image_scale[:, None])[:, :, None]
    )
    d_gate_two = jnp.sum(grad_out * branch, axis=1)
    d_branch = (gate_two * grad_out).astype(jnp.bfloat16).reshape(row_count, D)
    d_branch_own, d_branch_sib = split(d_branch)
    bias_fc2 = jnp.sum(d_branch, axis=0, dtype=jnp.float32)
    d_active = times_t(d_branch_own, fc2_own) + times_t(d_branch_sib, fc2_sib)
    d_active_own, d_active_sib = split(d_active)
    d_hidden_own = jax.vjp(gelu_tanh, hidden_own)[1](d_active_own)[0].astype(jnp.bfloat16)
    d_hidden_sib = jax.vjp(gelu_tanh, hidden_sib)[1](d_active_sib)[0].astype(jnp.bfloat16)
    bias_fc1 = join(
        jnp.sum(d_hidden_own, axis=0, dtype=jnp.float32),
        jnp.sum(d_hidden_sib, axis=0, dtype=jnp.float32),
    )
    d_mlp_in = (times_t(d_hidden_own, fc1_own) + times_t(d_hidden_sib, fc1_sib)).reshape(
        images, SEQ, D
    )
    d_shift_two = jnp.sum(d_mlp_in, axis=1)
    d_scale_two = jnp.sum(d_mlp_in * normed_two, axis=1)
    d_middle = grad_out + norm_back(d_mlp_in * (1.0 + scale_two), normed_two, inverse_two)
    d_gate_one = jnp.sum(d_middle * attn_out, axis=1)
    d_attn = (gate_one * d_middle).astype(jnp.bfloat16).reshape(row_count, D)
    d_attn_own, d_attn_sib = split(d_attn)
    bias_proj = jnp.sum(d_attn, axis=0, dtype=jnp.float32)
    d_attended = times_t(d_attn_own, proj_own) + times_t(d_attn_sib, proj_sib)
    d_attended = d_attended.astype(jnp.bfloat16).reshape(images, SEQ, H, HD)
    soft_again = jnp.exp(masked_scores(query, keys, valid_keys) - log_total)
    grad_values = jnp.einsum(
        "bhlm,blhc->bmhc",
        soft_again.astype(jnp.bfloat16),
        d_attended,
        preferred_element_type=jnp.float32,
    )
    d_probs = jnp.einsum("blhc,bmhc->bhlm", d_attended, values, preferred_element_type=jnp.float32)
    d_scores = soft_again * (d_probs - jnp.sum(soft_again * d_probs, axis=-1, keepdims=True))
    d_scores = jnp.where(valid_keys[:, None, None, :], d_scores, 0.0).astype(jnp.bfloat16)
    grad_query = jnp.einsum(
        "bhlm,bmhc->blhc", d_scores, keys, preferred_element_type=jnp.float32
    ) * HD ** (-0.5)
    grad_keys = jnp.einsum(
        "bhlm,blhc->bmhc", d_scores, query, preferred_element_type=jnp.float32
    ) * HD ** (-0.5)
    d_qkv = (
        jnp.stack([grad_query, grad_keys, grad_values], axis=2)
        .astype(jnp.bfloat16)
        .reshape(row_count, 3 * D)
    )
    d_qkv_own, d_qkv_sib = split(d_qkv)
    bias_query = jnp.sum(d_qkv[:, :D], axis=0, dtype=jnp.float32)
    bias_value = jnp.sum(d_qkv[:, 2 * D :], axis=0, dtype=jnp.float32)
    d_attn_in = (times_t(d_qkv_own, qkv_own) + times_t(d_qkv_sib, qkv_sib)).reshape(
        images, SEQ, D
    )
    d_shift_one = jnp.sum(d_attn_in, axis=1)
    d_scale_one = jnp.sum(d_attn_in * normed_one, axis=1)
    grad_tokens = (
        d_middle + norm_back(d_attn_in * (1.0 + scale_one), normed_one, inverse_one)
    ).astype(jnp.bfloat16)
    d_modul = jnp.concatenate(
        [d_shift_one, d_scale_one, d_gate_one, d_shift_two, d_scale_two, d_gate_two], axis=1
    ).astype(jnp.bfloat16)
    silu_pull = jax.vjp(jax.nn.silu, cond_float)[1]
    grad_condition = silu_pull(jnp.dot(d_modul, w_ada, preferred_element_type=jnp.float32))[0]
    biases = [bias_query, bias_value, bias_proj, bias_fc1, bias_fc2]
    note = jnp.concatenate(
        biases + [d_modul.astype(jnp.float32).reshape(-1), jnp.zeros((2 * lanes,), jnp.float32)]
    ).reshape(-1, lanes)

    terms = [
        (attended.T, d_attn_own, d_attn_sib, w_proj),
        (active.T, d_branch_own, d_branch_sib, w_fc2),
        (attn_in.T, d_qkv_own, d_qkv_sib, w_qkv),
        (mlp_in.T, d_hidden_own, d_hidden_sib, w_fc1),
    ]
    (grad_proj, grad_fc2, grad_qkv, grad_fc1), note_own, note_sib = scatter(terms, note)
    total_note = (jnp.sum(note_own, axis=0) + jnp.sum(note_sib, axis=0)).reshape(-1)
    summed, start = [], 0
    for vector in biases + [b_ada]:
        summed.append(total_note[start : start + vector.shape[0]])
        start += vector.shape[0]
    first = start - b_ada.shape[0]
    share_rows = 6 * D // lax.axis_size(("dp", "fsdp"))
    own_start = first + lax.axis_index(("dp", "fsdp")) * share_rows
    notes = jnp.concatenate([note_own, note_sib]).reshape(-1, note.size)
    silus = jnp.concatenate([own[0], sib[0]])[:, 1:10].reshape(-1, D)
    columns = lax.dynamic_slice_in_dim(notes, own_start, share_rows, 1)
    grad_ada = lax.dot_general(
        columns.astype(jnp.bfloat16),
        silus.astype(jnp.bfloat16),
        ROWS_DIMS,
        preferred_element_type=jnp.float32,
    )
    return (
        result,
        grad_tokens,
        grad_condition,
        grad_qkv,
        summed[0],
        summed[1],
        grad_proj,
        summed[2],
        grad_fc1,
        summed[3],
        grad_fc2,
        summed[4],
        grad_ada,
        summed[5],
    )


def solution(mesh):
    in_specs = (
        P(("dp", "fsdp"), None, None),
        P(("dp", "fsdp"), None),
        P(("dp", "fsdp"), None, None),
        P(("dp", "fsdp"), None),
        P(("dp", "fsdp")),
        P(),
        P("dp", "fsdp"),
        P(),
        P(),
        P("dp", "fsdp"),
        P(),
        P("dp", "fsdp"),
        P(),
        P("dp", "fsdp"),
        P(),
        P(),
        P(),
    )
    out_specs = (
        P(("dp", "fsdp"), None, None),
        P(("dp", "fsdp"), None, None),
        P(("dp", "fsdp"), None),
        P("dp", "fsdp"),
        P(),
        P(),
        P("dp", "fsdp"),
        P(),
        P("dp", "fsdp"),
        P(),
        P("dp", "fsdp"),
        P(),
        P(("dp", "fsdp"), None),
        P(),
    )
    return jax.shard_map(
        functools.partial(shards, dict(mesh.shape) == {"dp": 16, "fsdp": 2}),
        mesh=mesh,
        in_specs=in_specs,
        out_specs=out_specs,
        check_vma=False,
    )
```

```python
import functools

import jax
import jax.numpy as jnp
from jax import lax
from jax.experimental import pallas as pl
from jax.experimental.pallas import tpu as pltpu
from jax.sharding import PartitionSpec as P

D = 1152
H = 16
HD = 72
BINS = 16
SEQ = 256


NEG_FILL = -1e30
NORM_EPS = 1e-06
GELU_COEF = 0.7978845608028654
CUBIC_COEF = 0.044715
ROWS_DIMS = (((0,), (0,)), ((), ()))
LAST_DIMS = (((1,), (1,)), ((), ()))


def gelu_tanh(values_in):
    return (
        0.5
        * values_in
        * (1.0 + jnp.tanh(GELU_COEF * (values_in + CUBIC_COEF * values_in * values_in * values_in)))
    )


def norm_rows(inputs):
    centered = inputs - jnp.mean(inputs, axis=-1, keepdims=True)
    inverse = lax.rsqrt(jnp.mean(centered * centered, axis=-1, keepdims=True) + NORM_EPS)
    return (centered * inverse, inverse)


def norm_back(grad_normed, normed, inverse):
    centered_grad = grad_normed - jnp.mean(grad_normed, axis=-1, keepdims=True)
    return inverse * (
        centered_grad - normed * jnp.mean(grad_normed * normed, axis=-1, keepdims=True)
    )


VMEM_LIMIT = 67_000_000
ANY = pl.BlockSpec(memory_space=pl.ANY)
VMEM = pl.BlockSpec(memory_space=pltpu.VMEM)
ZS = 4
TILE = 256
MID = (1,)
ORDER = (
    (0, 1, 0),
    (0, 0, 0),
    (2, 1, 0),
    (1, 0, 0),
    (0, 0, 1),
    (0, 1, 1),
    (2, 0, 0),
    (1, 0, 1),
    (2, 1, 1),
    (2, 1, 2),
    (2, 0, 1),
    (1, 1, 0),
    (2, 0, 2),
    (3, 1, 0),
    (3, 0, 0),
)
BACK_MID = ()
BACK_ORDER = (
    (0, -1, 0),
    (1, -1, 0),
    (0, 0, 0),
    (0, 0, 1),
    (1, -1, 1),
    (1, -1, 2),
    (2, -1, 0),
    (0, 1, 0),
    (3, -1, 0),
    (4, -1, 0),
    (5, -1, 0),
    (5, -1, 1),
    (1, 0, 0),
    (1, 0, 1),
    (5, -1, 2),
    (1, 1, 0),
    (0, 1, 1),
    (2, 0, 0),
    (2, 0, 1),
    (5, -1, 3),
    (1, 1, 1),
    (2, 1, 0),
    (6, -1, 0),
    (2, 0, 2),
    (3, 0, 0),
    (2, 1, 1),
    (2, 1, 2),
    (7, -1, 0),
    (8, -1, 0),
    (3, 1, 0),
)
BACK_TASKS = ("seed", "widen", "mix", "centre", "project", "attend", "part", "query", "leave")
OFFSETS = (0, -1, 1, -2, 2, -3, 3)
STEPS = ("column", "relay", "last")
TASKS = ("start", "mod", "ln", "load", "query", "attend", "project", "mid", "widen", "narrow", "last")
WEIGHTS = ("qkv", "proj", "fc1", "fc2")
STAGES = ("near", "far", "line", "own")
GATHER_MID = (3,)
GATHER_ORDER = (
    (0, 0, 0),
    (0, 1, 0),
    (0, 2, 0),
    (0, 1, -1),
    (0, 1, 1),
    (0, 3, 0),
    (0, 1, -2),
    (0, 0, -1),
    (0, 1, 2),
    (0, 2, 1),
    (0, -1, 0),
    (0, 1, 3),
    (0, 1, -3),
    (1, 1, 0),
    (0, 2, -1),
    (1, 2, 0),
    (0, 2, 2),
    (0, 0, -2),
    (0, 2, -2),
    (0, 3, 1),
    (0, 2, -3),
    (1, -1, 0),
    (1, 1, -3),
    (0, 0, 1),
    (0, 4, 0),
    (2, 1, -3),
    (1, 2, 1),
    (0, 3, 2),
    (0, 0, -3),
    (1, 1, 3),
    (1, 1, 1),
    (1, 3, 0),
    (0, 3, -1),
    (1, 2, -1),
    (0, 0, 2),
    (1, 1, -1),
    (1, 0, 0),
    (1, 0, -3),
    (1, 3, -1),
    (1, 1, -2),
    (1, 0, -2),
    (2, 1, 3),
    (2, 1, 0),
    (2, 0, -3),
    (1, 1, 2),
    (1, 3, -2),
    (0, 4, -1),
    (1, 2, -3),
    (0, 4, 1),
    (1, 2, -2),
    (1, -1, 1),
    (2, -1, 0),
    (1, 3, -3),
    (2, 0, -2),
    (0, 4, -2),
    (0, 2, 3),
    (1, 3, 1),
    (1, 2, 2),
    (2, 1, 2),
    (2, 0, 0),
    (1, 3, 2),
    (2, 1, -1),
    (0, 0, 3),
    (2, 1, 1),
    (2, 1, -2),
    (0, 4, 2),
    (2, 3, 0),
    (0, 4, -3),
    (3, -1, 0),
    (2, 2, -3),
    (1, 4, 0),
    (4, -1, 0),
    (4, -1, 1),
    (1, 3, 3),
    (0, 3, -2),
    (1, 0, 2),
    (1, 2, 3),
    (2, 3, -1),
    (5, -1, 0),
    (5, -1, 1),
    (2, 2, 0),
    (1, 4, -2),
    (0, 3, -3),
    (0, 3, 3),
    (1, 4, -1),
    (2, 2, 1),
    (1, 0, 3),
    (5, -1, 2),
    (2, 2, 2),
    (2, 2, 3),
    (5, -1, 3),
    (2, 2, -1),
    (2, 2, -2),
    (0, 4, 3),
    (3, -1, 1),
    (1, 4, -3),
    (2, 0, 3),
    (2, 0, 2),
    (2, 3, -3),
    (2, 3, 3),
    (1, 4, 2),
    (1, 4, 1),
    (2, 4, 0),
    (2, 3, 2),
    (6, -1, 0),
    (2, 3, 1),
    (6, -1, 1),
    (1, 4, 3),
    (2, 3, -2),
    (7, -1, 0),
    (3, -1, 2),
    (8, -1, 0),
    (1, 0, 1),
    (2, 4, -1),
    (2, 4, 1),
    (8, -1, 1),
    (2, 4, 2),
    (2, 4, -2),
    (2, 4, -3),
    (8, -1, 2),
    (2, 4, 3),
    (1, 0, -1),
    (2, 0, 1),
    (3, -1, 3),
    (2, 0, -1),
    (9, -1, 0),
    (9, -1, 1),
    (10, -1, 0),
)


class Place:
    def __init__(self):
        self.i = lax.axis_index("dp")
        self.c = lax.axis_index("fsdp")
        self.z = self.i // 4
        self.q = self.i % 4
        self.y = self.q // 2
        self.x = self.q % 2
        self.to_y = 2 * (1 - 2 * self.y)
        self.to_x = 1 - 2 * self.x

    def partners(self, level):
        odd = level % 2
        first = odd * self.to_x + (1 - odd) * self.to_y
        return first, self.to_x + self.to_y - first

    def greet(self):
        barrier = pltpu.get_barrier_semaphore()

        def signal(i, c):
            pl.semaphore_signal(
                barrier,
                inc=1,
                device_id={"dp": i, "fsdp": c},
                device_id_type=pl.DeviceIdType.MESH,
            )

        signal(self.i, 1 - self.c)
        signal(self.i + self.to_y, self.c)
        signal(self.i + self.to_x, self.c)
        up, down = self.z < ZS - 1, self.z > 0
        pl.when(up)(lambda: signal(self.i + 4, self.c))
        pl.when(down)(lambda: signal(self.i - 4, self.c))
        pl.semaphore_wait(barrier, 3 + up.astype(jnp.int32) + down.astype(jnp.int32))


def remote(src, dst, send, recv, i, c):
    return pltpu.make_async_remote_copy(
        src_ref=src,
        dst_ref=dst,
        send_sem=send,
        recv_sem=recv,
        device_id={"dp": i, "fsdp": c},
        device_id_type=pl.DeviceIdType.MESH,
    )


def gather_sems(count):
    dma = pltpu.SemaphoreType.DMA
    return [
        dma((count, 16)),
        dma((count, 16)),
        dma((count, 2, ZS, 2)),
        dma((count, ZS, 3)),
        dma((count, 16)),
        dma((count,)),
    ]


class Gather:
    def __init__(self, at, k, shard, own, sib, sems, mid=False):
        self.mid = mid
        self.at, self.k, self.shard, self.own, self.sib = at, k, shard, own, sib
        self.recv, self.core, self.line, self.pair, self.over, self.local = sems

    def block(self, ref, j):
        rows = self.shard.shape[0]
        return ref.at[pl.ds(pl.multiple_of(j * rows, 8), rows)]

    def send(self, src, j, sem, i):
        return remote(src, self.block(self.own, j), sem, self.recv.at[self.k, j], i, self.at.c)

    def across(self, src, j):
        at, k = self.at, self.k
        return remote(
            src, self.block(self.sib, j), self.over.at[k, j], self.core.at[k, j], at.i, 1 - at.c
        )

    def arrived(self, j):
        at = self.at
        remote(
            self.block(self.own, j),
            self.block(self.own, j),
            self.over.at[self.k, j],
            self.recv.at[self.k, j],
            at.i,
            1 - at.c,
        ).wait_recv()

    def pieces(self, level):
        first, second = self.at.partners(level)
        column = level * 4 + self.at.q
        return first, second, column

    def guard(self, off, run):
        level = self.at.z + off
        if off == 0:
            run(level)
        else:
            pl.when((level >= 0) & (level < ZS))(lambda: run(level))

    def line_copies(self, off, level, slot, src, j):
        at, k = self.at, self.k
        out = []
        if off <= 0:
            copy = self.send(src, j, self.line.at[k, 0, level, slot], at.i + 4)
            out.append((at.z < ZS - 1, copy))
        if off >= 0:
            copy = self.send(src, j, self.line.at[k, 1, level, slot], at.i - 4)
            out.append((at.z > 0, copy))
        return out

    def column_copies(self, off, level):
        at, k = self.at, self.k
        first, second, j = self.pieces(level)
        src = self.shard if off == 0 else self.block(self.own, j)
        lines = self.line_copies(off, level, 0, src, j)
        near = [self.send(src, j, self.pair.at[k, level, 0], at.i + first)]
        rest = [self.send(src, j, self.pair.at[k, level, 1], at.i + second), self.across(src, j)]
        if not self.mid:
            return [], lines, near + rest
        return (near if off == 0 else []), lines, rest

    def column(self, off):
        def run(level):
            if off:
                self.arrived(level * 4 + self.at.q)
            before, lines, after = self.column_copies(off, level)
            for copy in before:
                copy.start()
            for where, copy in lines:
                pl.when(where)(copy.start)
            for copy in after:
                copy.start()
            if off == 0:
                self.keep().start()

        self.guard(off, run)

    def keep(self):
        return pltpu.make_async_copy(
            self.shard, self.block(self.own, self.at.i), self.local.at[self.k]
        )

    def relay_copies(self, off, level):
        first, second, column = self.pieces(level)
        j = column + first
        src = self.block(self.own, j)
        lines = self.line_copies(off, level, 1, src, j) if self.mid else []
        return lines, [
            self.send(src, j, self.pair.at[self.k, level, 2], self.at.i + second),
            self.across(src, j),
        ]

    def relay(self, off):
        def run(level):
            first, _, column = self.pieces(level)
            self.arrived(column + first)
            lines, after = self.relay_copies(off, level)
            for where, copy in lines:
                pl.when(where)(copy.start)
            for copy in after:
                copy.start()

        self.guard(off, run)

    def last_copies(self, level):
        first, second, column = self.pieces(level)
        return [(j, self.across(self.block(self.own, j), j)) for j in (column + second, column + first + second)]

    def last(self, off):
        def run(level):
            for j, copy in self.last_copies(level):
                self.arrived(j)
                copy.start()

        self.guard(off, run)

    def complete(self):
        self.keep().wait()

        @pl.loop(0, 16)
        def _(j):
            self.across(self.block(self.sib, j), j).wait_recv()

    def finish(self):
        at = self.at
        for off in OFFSETS:

            def run(level, off=off):
                before, lines, after = self.column_copies(off, level)
                more, relays = self.relay_copies(off, level)
                for where, copy in lines + more:
                    pl.when(where)(copy.wait_send)
                for copy in before + after + relays:
                    copy.wait_send()
                for _, copy in self.last_copies(level):
                    copy.wait_send()

            self.guard(off, run)

    def events(self, start, span):
        out = []
        for off in OFFSETS:
            far = abs(off)
            out.append((start + span * 0.15 * far, functools.partial(self.column, off)))
            out.append((start + span * (0.3 + 0.2 * far), functools.partial(self.relay, off)))
            out.append((start + span * (0.6 + 0.2 * far), functools.partial(self.last, off)))
        return out


def spread_rows(rows):
    def over(step):
        @pl.loop(0, rows // 32)
        def _(part):
            step(pl.ds(pl.multiple_of(part * 32, 32), 32))

    return over


def flip(source, out):
    @pl.loop(0, source.shape[-1] // 128)
    def _(t):
        part = pl.ds(pl.multiple_of(t * 128, 128), 128)
        out[part, :] = source[:, part].astype(jnp.float32).T.astype(jnp.bfloat16)


def by_tiles(left, right, emit):
    width = right.shape[-1]

    @pl.loop(0, width // TILE)
    def _(t):
        columns = pl.ds(pl.multiple_of(t * TILE, TILE), TILE)
        emit(columns, jnp.dot(left[...], right[:, columns], preferred_element_type=jnp.float32))

    if width % TILE:
        columns = pl.ds(width // TILE * TILE, width % TILE)
        emit(columns, jnp.dot(left[...], right[:, columns], preferred_element_type=jnp.float32))


class Forward:
    def __init__(self, at, ins, outs, scratch, jobs):
        self.at, self.jobs = at, jobs
        (
            self.tokens,
            self.silu,
            self.w_ada,
            self.b_ada,
            self.valid,
            self.b_qkv,
            self.b_proj,
            self.b_fc1,
            self.b_fc2,
        ) = ins
        (
            self.modul,
            self.attn_in_t,
            self.qkv,
            self.lse,
            self.attended_t,
            self.attn_out,
            self.middle,
            self.mlp_in_t,
            self.hidden,
            self.active_t,
            self.branch,
            self.result,
        ) = outs
        self.ada, self.loose = scratch[:2]
        self.weights = dict(zip(WEIGHTS, scratch[2:6]))
        self.attn_in, self.attended, self.mlp_in, self.active = scratch[6:10]
        self.ada_sem, self.load_sem = scratch[10:]

    def ada_copy(self, part):
        slot = part % 2
        rows = pl.ds(pl.multiple_of(part * D, D), D)
        return pltpu.make_async_copy(
            self.w_ada.at[rows], self.ada.at[slot], self.ada_sem.at[slot]
        )

    def start(self, _):
        self.ada_copy(0).start()
        self.lse[...] = jnp.zeros(self.lse.shape, jnp.float32)
        self.attended[...] = jnp.zeros(self.attended.shape, jnp.bfloat16)

    def mod(self, half):
        @pl.loop(half * 3, half * 3 + 3)
        def _(part):
            pl.when(part < 5)(lambda: self.ada_copy(part + 1).start())
            self.ada_copy(part).wait()
            value = lax.dot_general(
                self.silu[...],
                self.ada[part % 2],
                LAST_DIMS,
                preferred_element_type=jnp.float32,
            )
            self.modul[part] = value[:8] + self.b_ada[part]

    def piece(self, index):
        return self.modul[index, 0:1, :]

    def ln(self, _):
        @spread_rows(SEQ)
        def _(rows):
            normed, _ = norm_rows(self.tokens[rows, :].astype(jnp.float32))
            self.attn_in[rows, :] = (normed * (1.0 + self.piece(1)) + self.piece(0)).astype(
                jnp.bfloat16
            )

        flip(self.attn_in, self.attn_in_t)

    def load_copies(self, name):
        k = WEIGHTS.index(name)
        job, held, c = self.jobs[k + 1], self.weights[name], self.at.c
        return [
            pltpu.make_async_copy(job.own, held.at[c], self.load_sem.at[k, 0]),
            pltpu.make_async_copy(job.sib, held.at[1 - c], self.load_sem.at[k, 1]),
        ]

    def load(self, k):
        name = WEIGHTS[k]
        self.jobs[k + 1].complete()
        for copy in self.load_copies(name):
            copy.start()

    def loaded(self, name):
        for copy in self.load_copies(name):
            copy.wait()

    def loosely(self, columns, value):
        self.loose[:, columns] = value

    def merge(self, out, bias, start):
        width = out.shape[-1] - start

        @spread_rows(SEQ)
        def _(rows):
            value = pltpu.roll(self.loose[rows, :width], 64, 1) + bias[0:1, start:]
            before = out[rows, start : start + 128].astype(jnp.float32)
            lane = lax.broadcasted_iota(jnp.int32, before.shape, 1)
            seam = jnp.where(lane < 64, before, value[:, :128])
            out[rows, start : start + 128] = seam.astype(out.dtype)
            out[rows, start + 128 :] = value[:, 128:].astype(out.dtype)

    def product(self, left, name, half, out, bias):
        if half == 0:
            self.loaded(name)

            def emit(columns, value):
                out[:, columns] = (value + bias[0:1, columns]).astype(out.dtype)

            by_tiles(left, self.weights[name].at[0], emit)
        else:
            by_tiles(left, self.weights[name].at[1], self.loosely)
            self.merge(out, bias, out.shape[-1] // 256 * 128)

    def query(self, half):
        self.product(self.attn_in, "qkv", half, self.qkv, self.b_qkv)

    def attend(self, part):
        @pl.loop(part * 4, part * 4 + 4)
        def _(head):
            begin = head * HD
            tile = begin // 128
            tile = tile - tile // 8
            first = pl.multiple_of(tile * 128, 128)
            window = pl.ds(first, 256)
            lane = lax.broadcasted_iota(jnp.int32, (SEQ, 256), 1) + tile * 128
            inside = (lane >= begin) & (lane < begin + HD)
            query = jnp.where(inside, self.qkv[:, window].astype(jnp.float32), 0.0)
            keys = self.qkv[:, pl.ds(pl.multiple_of(D + tile * 128, 128), 256)]
            values = self.qkv[:, pl.ds(pl.multiple_of(2 * D + tile * 128, 128), 256)]
            scores = lax.dot_general(
                query.astype(jnp.bfloat16), keys, LAST_DIMS, preferred_element_type=jnp.float32
            ) * HD ** (-0.5)
            scores = jnp.where(self.valid[0:1, :] > 0.5, scores, NEG_FILL)
            row_max = jnp.max(scores, axis=1, keepdims=True)
            exponent = jnp.exp(scores - row_max)
            row_total = jnp.sum(exponent, axis=1, keepdims=True)
            probs = (exponent / row_total).astype(jnp.bfloat16)
            value = jnp.dot(probs, values, preferred_element_type=jnp.float32)
            before = self.attended[:, window].astype(jnp.float32)
            self.attended[:, window] = jnp.where(inside, value, before).astype(jnp.bfloat16)
            column = lax.broadcasted_iota(jnp.int32, (SEQ, 128), 1)
            self.lse[...] = jnp.where(
                column == head, row_max + jnp.log(row_total), self.lse[...]
            )

    def project(self, half):
        self.product(self.attended, "proj", half, self.attn_out, self.b_proj)
        if half:
            flip(self.attended, self.attended_t)

    def mid(self, _):
        @spread_rows(SEQ)
        def _(rows):
            middle = (
                self.tokens[rows, :].astype(jnp.float32) + self.piece(2) * self.attn_out[rows, :]
            )
            self.middle[rows, :] = middle
            normed, _ = norm_rows(middle)
            self.mlp_in[rows, :] = (normed * (1.0 + self.piece(4)) + self.piece(3)).astype(
                jnp.bfloat16
            )

        flip(self.mlp_in, self.mlp_in_t)

    def widen(self, part):
        if part == 0:
            self.loaded("fc1")
        weight = self.weights["fc1"]

        @pl.loop(part * 6, part * 6 + 6)
        def _(t):
            columns = pl.ds(pl.multiple_of(t * TILE, TILE), TILE)
            within = pl.ds(pl.multiple_of(t % 9 * TILE, TILE), TILE)
            hidden = (
                jnp.dot(
                    self.mlp_in[...],
                    weight[t // 9, :, within],
                    preferred_element_type=jnp.float32,
                )
                + self.b_fc1[0:1, columns]
            )
            self.hidden[:, columns] = hidden
            active = gelu_tanh(hidden)
            self.active[:, columns] = active.astype(jnp.bfloat16)
            self.active_t[columns, :] = active.T.astype(jnp.bfloat16)

    def narrow(self, half):
        self.product(self.active, "fc2", half, self.branch, self.b_fc2)

    def last(self, _):
        @spread_rows(SEQ)
        def _(rows):
            self.result[rows, :] = (
                self.middle[rows, :] + self.piece(5) * self.branch[rows, :]
            ).astype(jnp.bfloat16)


def gather_kernel(count, *refs):
    refs = list(refs)

    def take(n):
        out = refs[:n]
        del refs[:n]
        return out

    shards, ins = take(count), take(9)
    own, sib, outs = take(count), take(count), take(12)
    sems, scratch = take(6), take(12)
    at = Place()
    at.greet()
    jobs = [
        Gather(at, k, shards[k], own[k], sib[k], sems, k in GATHER_MID) for k in range(count)
    ]
    forward = Forward(at, ins, outs, scratch, jobs)
    for step, k, off in GATHER_ORDER:
        getattr(forward if k < 0 else jobs[k], (TASKS if k < 0 else STEPS)[step])(off)
    jobs[0].complete()
    for job in jobs:
        job.finish()


def gather_all(shards, ins):
    count = len(shards)
    spread = [jax.ShapeDtypeStruct((16 * s.shape[0], s.shape[1]), s.dtype) for s in shards]
    kinds = [
        ((6, 8, D), jnp.float32),
        ((D, SEQ), jnp.bfloat16),
        ((SEQ, 3 * D), jnp.bfloat16),
        ((SEQ, 128), jnp.float32),
        ((D, SEQ), jnp.bfloat16),
        ((SEQ, D), jnp.float32),
        ((SEQ, D), jnp.float32),
        ((D, SEQ), jnp.bfloat16),
        ((SEQ, 4 * D), jnp.float32),
        ((4 * D, SEQ), jnp.bfloat16),
        ((SEQ, D), jnp.float32),
        ((SEQ, D), jnp.bfloat16),
    ]
    dma = pltpu.SemaphoreType.DMA
    outs = pl.pallas_call(
        functools.partial(gather_kernel, count),
        out_shape=spread + spread + [jax.ShapeDtypeStruct(*kind) for kind in kinds],
        in_specs=[VMEM] * count + [VMEM, VMEM, ANY] + [VMEM] * 6,
        out_specs=[ANY] * (2 * count) + [VMEM] * len(kinds),
        scratch_shapes=gather_sems(count)
        + [pltpu.VMEM((2, D, D), jnp.bfloat16), pltpu.VMEM((SEQ, 1792), jnp.float32)]
        + [pltpu.VMEM((2,) + s.shape, s.dtype) for s in spread[1:]]
        + [pltpu.VMEM((SEQ, width), jnp.bfloat16) for width in (D, D, D, 4 * D)]
        + [dma((2,)), dma((4, 2))],
        compiler_params=pltpu.CompilerParams(
            collective_id=0, has_side_effects=True, vmem_limit_bytes=VMEM_LIMIT
        ),
        name="gather_all",
    )(*shards, *ins)
    return outs[:count], outs[count : 2 * count], outs[2 * count :]


def blocked(shape):
    rows, cols = shape
    return (rows, cols) if rows % 16 == 0 else (rows // 8, 8, cols)


def total(*values):
    out = values[0].astype(jnp.float32)
    for value in values[1:]:
        out = out + value.astype(jnp.float32)
    return out


class Scatter:
    def __init__(self, at, k, ins, result, bufs, sems):
        self.at, self.k = at, k
        self.left, halves = ins
        self.right, self.away = halves.at[at.c], halves.at[1 - at.c]
        self.result = result
        self.left_sib, self.right_sib, self.held, self.near, self.far, self.line = bufs
        self.mid = self.line.shape[2] == 2
        (
            self.swap_send,
            self.swap_recv,
            self.near_send,
            self.near_recv,
            self.far_send,
            self.far_recv,
            self.line_send,
            self.line_recv,
        ) = sems

    def swaps(self):
        at, k = self.at, self.k
        pairs = ((self.left, self.left_sib), (self.away, self.right_sib))
        return [
            remote(
                src, dst, self.swap_send.at[k, s], self.swap_recv.at[k, s], at.i, 1 - at.c
            )
            for s, (src, dst) in enumerate(pairs)
        ]

    def near_copies(self, level):
        at, k = self.at, self.k
        first, second = at.partners(level)
        column = level * 4 + at.q
        return [
            remote(
                self.held.at[j],
                self.near.at[level, slot],
                self.near_send.at[k, level, slot],
                self.near_recv.at[k, level, slot],
                at.i + second,
                at.c,
            )
            for slot, j in enumerate((column + second, column + first + second))
        ]

    def far_copy(self, level):
        at, k = self.at, self.k
        first, _ = at.partners(level)
        j = level * 4 + at.q + first
        slot = 0 if self.mid else level
        return remote(
            self.held.at[j],
            self.far.at[slot],
            self.far_send.at[k, slot],
            self.far_recv.at[k, slot],
            at.i + first,
            at.c,
        )

    def line_copies(self, way, level):
        at, k = self.at, self.k
        first, _ = at.partners(level)
        column = level * 4 + at.q
        return [
            remote(
                self.held.at[j],
                self.line.at[way, level, slot],
                self.line_send.at[k, way, level, slot],
                self.line_recv.at[k, way, level, slot],
                at.i + (4 if way == 0 else -4),
                at.c,
            )
            for slot, j in enumerate((column, column + first)[: 2 if self.mid else 1])
        ]

    def line_arrived(self, way, level):
        for copy in self.line_copies(way, level):
            if way == 0:
                pl.when(self.at.z > 0)(copy.wait_recv)
            else:
                pl.when(self.at.z < ZS - 1)(copy.wait_recv)

    def begin(self, part):
        self.swaps()[part].start()

    def clear(self):
        zeros = jnp.zeros(self.line.shape[3:], self.line.dtype)

        @pl.when(self.at.z == 0)
        def _():
            @pl.loop(0, ZS)
            def _(level):
                for slot in range(self.line.shape[2]):
                    self.line[0, level, slot] = zeros

        @pl.when(self.at.z == ZS - 1)
        def _():
            @pl.loop(0, ZS)
            def _(level):
                for slot in range(self.line.shape[2]):
                    self.line[1, level, slot] = zeros

    def multiply(self, level):
        cols = self.held.shape[-1]
        rows = self.left.shape[0] // 16
        group = max(1, 288 // rows)
        height = group * rows
        wide = cols // TILE

        def block(part, columns):
            where = pl.ds(pl.multiple_of((level * 4 + part * group) * rows, 32), height)
            value = jnp.dot(
                self.left[where, :], self.right[:, columns], preferred_element_type=jnp.float32
            ) + jnp.dot(
                self.left_sib[where, :],
                self.right_sib[:, columns],
                preferred_element_type=jnp.float32,
            )
            for g in range(group):
                piece = value[g * rows : (g + 1) * rows]
                if len(self.held.shape) == 4:
                    piece = piece.reshape((rows // 8, 8, piece.shape[-1]))
                self.held[level * 4 + part * group + g, ..., columns] = piece.astype(jnp.bfloat16)

        @pl.loop(0, 4 // group)
        def _(part):
            @pl.loop(0, wide)
            def _(t):
                block(part, pl.ds(pl.multiple_of(t * TILE, TILE), TILE))

            if cols % TILE:
                block(part, pl.ds(wide * TILE, cols % TILE))

    def ready(self):
        for copy in self.swaps():
            copy.wait_recv()

    def stage_near(self, pair):
        @pl.loop(0, 2)
        def _(t):
            level = (1 - pair) * 3 * t + pair * (1 + t)
            self.multiply(level)
            for copy in self.near_copies(level):
                copy.start()

    def stage_far(self, pair):
        if self.mid:
            self.far_mid()
        else:
            pl.loop(0, 2)(lambda t: self.far_level((1 - pair) * 3 * t + pair * (1 + t)))

    def far_level(self, level):
        first, _ = self.at.partners(level)
        j = level * 4 + self.at.q + first
        for copy in self.near_copies(level):
            copy.wait_recv()
        self.held[j] = total(self.held[j], self.near[level, 1]).astype(jnp.bfloat16)
        self.far_copy(level).start()

    def far_mid(self):
        level = self.at.z
        first, _ = self.at.partners(level)
        j = level * 4 + self.at.q + first
        for copy in self.near_copies(level):
            copy.wait_recv()
        self.line_arrived(0, level)
        self.line_arrived(1, level)
        self.held[j] = total(
            self.held[j], self.near[level, 1], self.line[0, level, 1], self.line[1, level, 1]
        ).astype(jnp.bfloat16)
        self.far_copy(level).start()

    def pass_on(self, way, level):
        first, _ = self.at.partners(level)
        column = level * 4 + self.at.q
        if self.mid:
            for copy in self.near_copies(level):
                copy.wait_recv()
        else:
            self.far_copy(level).wait_recv()
        self.line_arrived(way, level)
        copies = self.line_copies(way, level)
        for slot, copy in enumerate(copies):
            j = column + slot * first
            values = [self.held[j], self.near[level, slot], self.line[way, level, slot]]
            if not self.mid:
                values.append(self.far[level])
            self.held[j] = total(*values).astype(jnp.bfloat16)
            copy.start()

    def stage_line(self, back):
        z = self.at.z
        if back < ZS - 1:
            up, down = ZS - 1 - back, back
            pl.when(z < up)(lambda: self.pass_on(0, up))
            pl.when(z > down)(lambda: self.pass_on(1, down))

    def stage_own(self, _):
        z = self.at.z
        j = self.at.i
        self.far_copy(z).wait_recv()
        if not self.mid:
            self.line_arrived(0, z)
            self.line_arrived(1, z)
        whole = total(
            self.held[j],
            self.near[z, 0],
            self.far[0 if self.mid else z],
            self.line[0, z, 0],
            self.line[1, z, 0],
        )
        self.result[...] = whole.reshape(self.result.shape)

    def finish(self):
        z = self.at.z
        for copy in self.swaps():
            copy.wait_send()

        if self.mid:
            self.far_copy(z).wait_send()

        @pl.loop(0, ZS)
        def _(level):
            for copy in self.near_copies(level):
                copy.wait_send()
            if not self.mid:
                self.far_copy(level).wait_send()
            for way in (0, 1):
                beyond = level > z if way == 0 else level < z
                for copy in self.line_copies(way, level):
                    pl.when(beyond)(copy.wait_send)


def fold(value):
    rows, cols = value.shape
    return jnp.sum(value.reshape(rows // 8, 8, cols), axis=0)


def halve(out, rows, value):
    width = out.shape[-1]
    rest = value[:, width // 128 * 128 :]
    out[0, rows, :] = value[:, :width].astype(jnp.bfloat16)
    rest = pltpu.roll(rest, rest.shape[-1] - 64, 1)
    out[1, rows, :] = rest[:, :width].astype(jnp.bfloat16)


class Backward:
    def __init__(self, at, ins, outs, scratch, jobs):
        self.at, self.jobs = at, jobs
        (
            self.modul,
            self.weight,
            self.cotangent,
            self.branch,
            self.hidden,
            self.middle,
            self.attn_out,
            self.lse,
            self.qkv,
            self.valid,
            self.tokens,
        ) = ins[:11]
        self.own, self.sib = ins[11:15], ins[15:19]
        self.d_attn, self.d_split, self.grad_tokens, self.sums, self.sums_fc1 = outs
        (
            self.d_branch,
            self.d_hidden,
            self.flow,
            self.d_middle,
            self.d_attended,
            self.d_qkv,
            self.slim,
            self.wide,
            self.long,
            self.slim_sem,
            self.wide_sem,
            self.long_sem,
        ) = scratch

    def piece(self, index):
        return self.modul[index, 0:1, :]

    def fetches(self, k, t):
        if k in (1, 3):
            buffer, sem = self.slim.at[t % 2], self.slim_sem.at[t % 2]
        else:
            buffer, sem = (self.long, self.long_sem) if k == 0 else (self.wide, self.wide_sem)
        rows = pl.ds(pl.multiple_of(t * 384, 384), 384)
        return [
            pltpu.make_async_copy(self.own[k].at[rows], buffer.at[self.at.c], sem.at[0]),
            pltpu.make_async_copy(self.sib[k].at[rows], buffer.at[1 - self.at.c], sem.at[1]),
        ]

    def fetch(self, k, t):
        for copy in self.fetches(k, t):
            copy.start()

    def fetched(self, k, t):
        for copy in self.fetches(k, t):
            copy.wait()

    def back(self, halves, buffer):
        return lax.dot_general(
            halves[0], buffer[0], LAST_DIMS, preferred_element_type=jnp.float32
        ) + lax.dot_general(halves[1], buffer[1], LAST_DIMS, preferred_element_type=jnp.float32)

    def seed(self, _):
        self.fetch(3, 0)
        self.fetch(2, 0)
        self.fetch(0, 0)
        self.sums[...] = jnp.zeros(self.sums.shape, jnp.float32)
        self.d_qkv[...] = jnp.zeros(self.d_qkv.shape, jnp.bfloat16)

        @spread_rows(SEQ)
        def _(rows):
            grad = self.cotangent[rows, :].astype(jnp.float32) * self.weight[rows, 0:1]
            d_branch = (self.piece(5) * grad).astype(jnp.bfloat16).astype(jnp.float32)
            self.sums[5] += fold(grad * self.branch[rows, :])
            self.sums[9] += fold(d_branch)
            halve(self.d_branch, rows, d_branch)

        self.jobs[0].begin(1)

    def widen(self, part):
        @pl.loop(part * 4, part * 4 + 4)
        def _(t):
            pl.when(t < 11)(lambda: self.fetch(3, t + 1))
            self.fetched(3, t)
            columns = pl.ds(pl.multiple_of(t * 384, 384), 384)
            within = pl.ds(pl.multiple_of(t % 6 * 384, 384), 384)
            d_active = self.back(self.d_branch, self.slim.at[t % 2])
            pull = jax.vjp(gelu_tanh, self.hidden[:, columns])[1]
            d_hidden = pull(d_active)[0].astype(jnp.bfloat16)
            self.d_hidden[t // 6, :, within] = d_hidden
            self.sums_fc1[:, columns] = fold(d_hidden.astype(jnp.float32))

        if part == 2:
            self.jobs[1].begin(1)
            self.fetch(1, 0)

    def mix(self, _):
        @pl.loop(0, 3)
        def _(t):
            self.fetched(2, t)
            columns = pl.ds(pl.multiple_of(t * 384, 384), 384)
            self.flow[:, columns] = self.back(self.d_hidden, self.wide)
            pl.when(t < 2)(lambda: self.fetch(2, t + 1))

    def centre(self, _):
        @spread_rows(SEQ)
        def _(rows):
            grad = self.cotangent[rows, :].astype(jnp.float32) * self.weight[rows, 0:1]
            normed, inverse = norm_rows(self.middle[rows, :])
            d_mlp = self.flow[rows, :]
            self.sums[3] += fold(d_mlp)
            self.sums[4] += fold(d_mlp * normed)
            d_middle = grad + norm_back(d_mlp * (1.0 + self.piece(4)), normed, inverse)
            self.d_middle[rows, :] = d_middle
            self.sums[2] += fold(d_middle * self.attn_out[rows, :])
            d_attn = (self.piece(2) * d_middle).astype(jnp.bfloat16).astype(jnp.float32)
            self.sums[8] += fold(d_attn)
            halve(self.d_attn, rows, d_attn)

    def project(self, _):
        @pl.loop(0, 3)
        def _(t):
            pl.when(t < 2)(lambda: self.fetch(1, t + 1))
            self.fetched(1, t)
            columns = pl.ds(pl.multiple_of(t * 384, 384), 384)
            self.d_attended[:, columns] = self.back(self.d_attn, self.slim.at[t % 2]).astype(
                jnp.bfloat16
            )

    def attend(self, part):
        @pl.loop(part * 4, part * 4 + 4)
        def _(head):
            begin = head * HD
            tile = begin // 128
            tile = tile - tile // 8
            spots = [
                pl.ds(pl.multiple_of(kind * D + tile * 128, 128), 256) for kind in range(3)
            ]
            lane = lax.broadcasted_iota(jnp.int32, (SEQ, 256), 1) + tile * 128
            inside = (lane >= begin) & (lane < begin + HD)

            def only(ref, spot):
                return jnp.where(inside, ref[:, spot].astype(jnp.float32), 0.0).astype(
                    jnp.bfloat16
                )

            query, d_out = only(self.qkv, spots[0]), only(self.d_attended, spots[0])
            keys, values = self.qkv[:, spots[1]], self.qkv[:, spots[2]]
            column = lax.broadcasted_iota(jnp.int32, (SEQ, 128), 1)
            log_total = jnp.sum(
                jnp.where(column == head, self.lse[...], 0.0), axis=1, keepdims=True
            )
            is_valid = self.valid[0:1, :] > 0.5
            scores = lax.dot_general(
                query, keys, LAST_DIMS, preferred_element_type=jnp.float32
            ) * HD ** (-0.5)
            probs = jnp.exp(jnp.where(is_valid, scores, NEG_FILL) - log_total)
            d_probs = lax.dot_general(
                d_out, values, LAST_DIMS, preferred_element_type=jnp.float32
            )
            inner = jnp.sum(probs * d_probs, axis=1, keepdims=True)
            d_scores = jnp.where(is_valid, probs * (d_probs - inner), 0.0).astype(jnp.bfloat16)
            grads = (
                jnp.dot(d_scores, keys, preferred_element_type=jnp.float32) * HD ** (-0.5),
                lax.dot_general(d_scores, query, ROWS_DIMS, preferred_element_type=jnp.float32)
                * HD ** (-0.5),
                lax.dot_general(
                    probs.astype(jnp.bfloat16),
                    d_out,
                    ROWS_DIMS,
                    preferred_element_type=jnp.float32,
                ),
            )
            for spot, grad in zip(spots, grads):
                before = self.d_qkv[:, spot].astype(jnp.float32)
                self.d_qkv[:, spot] = jnp.where(inside, grad, before).astype(jnp.bfloat16)

    def part(self, _):
        @spread_rows(SEQ)
        def _(rows):
            value = self.d_qkv[rows, :].astype(jnp.float32)
            self.sums[6] += fold(value[:, :D])
            self.sums[7] += fold(value[:, 2 * D :])
            halve(self.d_split, rows, value)

    def query(self, _):
        @pl.loop(0, 3)
        def _(t):
            self.fetched(0, t)
            columns = pl.ds(pl.multiple_of(t * 384, 384), 384)
            self.flow[:, columns] = self.back(self.d_split, self.long)
            pl.when(t < 2)(lambda: self.fetch(0, t + 1))

    def leave(self, _):
        @spread_rows(SEQ)
        def _(rows):
            normed, inverse = norm_rows(self.tokens[rows, :].astype(jnp.float32))
            d_in = self.flow[rows, :]
            self.sums[0] += fold(d_in)
            self.sums[1] += fold(d_in * normed)
            self.grad_tokens[rows, :] = (
                self.d_middle[rows, :] + norm_back(d_in * (1.0 + self.piece(1)), normed, inverse)
            ).astype(jnp.bfloat16)


def scatter_bufs(terms):
    scratch = []
    for left, halves, shard, mid in terms:
        piece = blocked(shard.shape)
        scratch.append(pltpu.VMEM(left.shape, jnp.bfloat16))
        scratch.append(pltpu.VMEM((SEQ, shard.shape[1]), jnp.bfloat16))
        for lead in ((16,), (ZS, 2), (1 if mid else ZS,), (2, ZS, 2 if mid else 1)):
            scratch.append(pltpu.VMEM(lead + piece, jnp.bfloat16))
    dma, count = pltpu.SemaphoreType.DMA, len(terms)
    pairs = ((count, 2), (count, ZS, 2), (count, ZS), (count, 2, ZS, 2))
    return scratch + [dma(shape) for shape in pairs for _ in range(2)]


def back_kernel(*refs):
    refs = list(refs)

    def take(n):
        out = refs[:n]
        del refs[:n]
        return out

    lefts, ins = take(2), take(19)
    results, outs = take(2), take(5)
    scratch = take(12)
    bufs = [take(6) for _ in range(2)]
    sems = take(8)
    at = Place()
    at.greet()
    jobs = [
        Scatter(at, k, (lefts[k], scratch[k]), results[k], bufs[k], sems) for k in range(2)
    ]
    for job in jobs:
        job.begin(0)
        job.clear()
    backward = Backward(at, ins, outs, scratch, jobs)
    seen = set()
    for stage, k, part in BACK_ORDER:
        if k < 0:
            getattr(backward, BACK_TASKS[stage])(part)
            continue
        if k not in seen:
            jobs[k].ready()
            seen.add(k)
        getattr(jobs[k], "stage_" + STAGES[stage])(part)
    for job in jobs:
        job.finish()


def back_all(lefts, ins, shards):
    bf16, f32 = jnp.bfloat16, jnp.float32
    kinds = [
        ((2, SEQ, D // 2), bf16),
        ((2, SEQ, 3 * D // 2), bf16),
        ((SEQ, D), bf16),
        ((10, 8, D), f32),
        ((8, 4 * D), f32),
    ]
    own = [
        ((2, SEQ, D // 2), bf16),
        ((2, SEQ, 2 * D), bf16),
        ((SEQ, D), f32),
        ((SEQ, D), f32),
        ((SEQ, D), bf16),
        ((SEQ, 3 * D), bf16),
        ((2, 2, 384, D // 2), bf16),
        ((2, 384, 2 * D), bf16),
        ((2, 384, 3 * D // 2), bf16),
    ]
    dma = pltpu.SemaphoreType.DMA
    terms = [(left, None, shard, k in BACK_MID) for k, (left, shard) in enumerate(zip(lefts, shards))]
    outs = pl.pallas_call(
        back_kernel,
        out_shape=[jax.ShapeDtypeStruct(shard.shape, f32) for shard in shards]
        + [jax.ShapeDtypeStruct(*kind) for kind in kinds],
        in_specs=[VMEM] * 13 + [ANY] * 8,
        out_specs=[VMEM] * 7,
        scratch_shapes=[pltpu.VMEM(*kind) for kind in own]
        + [dma((2, 2)), dma((2,)), dma((2,))]
        + scatter_bufs(terms),
        compiler_params=pltpu.CompilerParams(
            collective_id=1, has_side_effects=True, vmem_limit_bytes=VMEM_LIMIT
        ),
        name="back_all",
    )(*lefts, *ins)
    return outs[:2], outs[2:]


def scatter_kernel(count, *refs):
    refs = list(refs)

    def take(n):
        out = refs[:n]
        del refs[:n]
        return out

    ins = [take(2) for _ in range(count)]
    note = take(1)[0]
    results = take(count)
    note_own, note_sib = take(2)
    bufs = [take(6) for _ in range(count)]
    sems, note_sems = take(8), take(6)
    at = Place()
    at.greet()
    jobs = [Scatter(at, k, ins[k], results[k], bufs[k], sems) for k in range(count)]
    word = Gather(at, 0, note, note_own, note_sib, note_sems)
    whisper = [action for _, action in sorted(word.events(0.0, 1.0), key=lambda item: item[0])]
    for job in jobs:
        job.begin(0)
        job.begin(1)
        job.clear()

    def speak(n):
        for action in whisper[:n]:
            action()
        del whisper[:n]

    speak(1)
    seen = set()
    for stage, k, part in ORDER:
        if k not in seen:
            jobs[k].ready()
            seen.add(k)
        getattr(jobs[k], "stage_" + STAGES[stage])(part)
        speak(2)
    speak(len(whisper))
    for job in jobs:
        job.finish()
    word.complete()
    word.finish()


def scatter_all(pairs, shards, note):
    count = len(pairs)
    spread = jax.ShapeDtypeStruct((16 * note.shape[0], note.shape[1]), note.dtype)
    terms = [
        (left, halves, shard, k in MID) for k, ((left, halves), shard) in enumerate(zip(pairs, shards))
    ]
    outs = pl.pallas_call(
        functools.partial(scatter_kernel, count),
        out_shape=[jax.ShapeDtypeStruct(shard.shape, jnp.float32) for shard in shards]
        + [spread, spread],
        in_specs=[VMEM, VMEM] * count + [VMEM],
        out_specs=[VMEM] * count + [ANY, ANY],
        scratch_shapes=scatter_bufs(terms) + gather_sems(1),
        compiler_params=pltpu.CompilerParams(
            collective_id=2, has_side_effects=True, vmem_limit_bytes=VMEM_LIMIT
        ),
        name="scatter_all",
    )(*[part for pair in pairs for part in pair], note)
    return outs[:count], outs[count], outs[count + 1]


def gather_plain(shards):
    own = [lax.all_gather(s, "dp", axis=0, tiled=True) for s in shards]
    pair = [lax.all_gather(g, "fsdp", axis=0) for g in own]
    other = 1 - lax.axis_index("fsdp")
    return own, [lax.dynamic_index_in_dim(p, other, 0, keepdims=False) for p in pair]


def scatter_plain(terms, note):
    c = lax.axis_index("fsdp")
    results = []
    for left, right, away, shard in terms:
        own, sib = [
            jnp.dot(left, half, preferred_element_type=jnp.float32)
            .astype(jnp.bfloat16)
            .reshape((-1,) + shard.shape)
            for half in (right, away)
        ]
        pair = jnp.where(c == 0, jnp.stack([own, sib]), jnp.stack([sib, own]))
        half = lax.psum_scatter(pair, "fsdp", scatter_dimension=0, tiled=False)
        results.append(
            lax.psum_scatter(
                half.astype(jnp.float32), "dp", scatter_dimension=0, tiled=False
            )
        )
    own, sib = gather_plain([note])
    return results, own[0], sib[0]


def masked_scores(query, keys, valid_keys):
    scaled = jnp.einsum(
        "blhc,bmhc->bhlm", query, keys, preferred_element_type=jnp.float32
    ) * HD ** (-0.5)
    return jnp.where(valid_keys[:, None, None, :], scaled, NEG_FILL)


def shards(
    fast,
    tokens,
    condition,
    cotangent,
    image_grids,
    noise_bins,
    bin_weights,
    w_qkv,
    b_query,
    b_value,
    w_proj,
    b_proj,
    w_fc1,
    b_fc1,
    w_fc2,
    b_fc2,
    w_ada,
    b_ada,
):
    images = tokens.shape[0]
    row_count = images * SEQ
    core = lax.axis_index("fsdp")

    def join(own, sib):
        return jnp.where(
            core == 0,
            jnp.concatenate([own, sib], axis=-1),
            jnp.concatenate([sib, own], axis=-1),
        )

    def split(full):
        half = full.shape[-1] // 2
        low, high = full[..., :half], full[..., half:]
        return jnp.where(core == 0, low, high), jnp.where(core == 0, high, low)

    token_count = image_grids[:, 0] * image_grids[:, 1]
    valid_keys = lax.broadcasted_iota(jnp.int32, (images, SEQ), 1) < token_count[:, None]
    bin_table = (noise_bins[:, None] == lax.broadcasted_iota(jnp.int32, (images, BINS), 1)).astype(
        jnp.float32
    )
    local_counts = jnp.sum(bin_table * token_count[:, None].astype(jnp.float32), axis=0)
    cond_float = condition.astype(jnp.float32)
    silu_cond = jax.nn.silu(cond_float).astype(jnp.bfloat16)
    lanes = 128
    head = jnp.concatenate([local_counts, jnp.zeros((lanes - BINS,), jnp.float32)])[None]
    facts = jnp.concatenate(
        [
            head,
            silu_cond.astype(jnp.float32).reshape(-1, lanes),
            jnp.zeros((6, lanes), jnp.float32),
        ]
    )
    shares = [facts, w_qkv, w_proj, w_fc1, w_fc2]
    bias_qkv = jnp.concatenate([b_query, jnp.zeros_like(b_query), b_value])
    if fast:
        row = lambda vector: vector.reshape(1, -1)
        ins = [
            tokens.reshape(SEQ, D),
            jnp.broadcast_to(silu_cond, (16, D)),
            w_ada,
            jnp.broadcast_to(b_ada.reshape(6, 1, D), (6, 8, D)),
            jnp.broadcast_to(valid_keys.astype(jnp.float32), (8, SEQ)),
            row(bias_qkv),
            row(b_proj),
            row(b_fc1),
            row(b_fc2),
        ]
        own, sib, outs = gather_all(shares, ins)
    else:
        own, sib = gather_plain(shares)
        outs = None
    qkv_own, proj_own, fc1_own, fc2_own = own[1:]
    qkv_sib, proj_sib, fc1_sib, fc2_sib = sib[1:]
    own_facts, sib_facts = own[0].reshape(-1, 16, lanes), sib[0].reshape(-1, 16, lanes)
    counts = (jnp.sum(own_facts, axis=0) + jnp.sum(sib_facts, axis=0))[0, :BINS]
    bin_scale = bin_weights.astype(jnp.float32) * (jnp.sum(counts) / BINS) / counts
    image_scale = jnp.sum(bin_table * bin_scale[None, :], axis=1)

    def times(left, right):
        return jnp.dot(left, right, preferred_element_type=jnp.float32)

    def times_t(left, right):
        return lax.dot_general(left, right, LAST_DIMS, preferred_element_type=jnp.float32)

    if fast:
        modul, attn_in_t, qkv_all, lse, attended_t, attn_out, middle = outs[:7]
        mlp_in_t, hidden, active_t, branch, result = outs[7:]
        weight = valid_keys.astype(jnp.float32) * image_scale[:, None]
        ins_back = [
            modul,
            jnp.broadcast_to(weight.reshape(SEQ, 1), (SEQ, lanes)),
            cotangent.reshape(SEQ, D),
            branch,
            hidden,
            middle,
            attn_out,
            lse,
            qkv_all,
            ins[4],
            tokens.reshape(SEQ, D),
        ]
        (grad_fc2, grad_fc1), outs = back_all(
            [active_t, mlp_in_t], ins_back + list(own[1:]) + list(sib[1:]), [w_fc2, w_fc1]
        )
        d_attn, d_split, grad_tokens, sums, sums_fc1 = outs
        sums = jnp.sum(sums, axis=1)
        bias_query, bias_value, bias_proj, bias_fc2 = sums[6], sums[7], sums[8], sums[9]
        bias_fc1 = jnp.sum(sums_fc1, axis=0)
        d_modul = sums[:6].reshape(1, 6 * D).astype(jnp.bfloat16)
        result, grad_tokens = result.reshape(tokens.shape), grad_tokens.reshape(tokens.shape)
    else:
        token_float = tokens.astype(jnp.float32)
        normed_one, inverse_one = norm_rows(token_float)
        modul = (
            lax.dot_general(silu_cond, w_ada, LAST_DIMS, preferred_element_type=jnp.float32) + b_ada
        )
        pieces = [modul[:, None, part_index * D : (part_index + 1) * D] for part_index in range(6)]
        shift_one, scale_one, gate_one, shift_two, scale_two, gate_two = pieces
        attn_in = (
            (normed_one * (1.0 + scale_one) + shift_one).astype(jnp.bfloat16).reshape(row_count, D)
        )
        qkv_all = (join(times(attn_in, qkv_own), times(attn_in, qkv_sib)) + bias_qkv).astype(
            jnp.bfloat16
        )
        qkv_heads = qkv_all.reshape(images, SEQ, 3, H, HD)
        query, keys, values = (qkv_heads[:, :, 0], qkv_heads[:, :, 1], qkv_heads[:, :, 2])
        scores = masked_scores(query, keys, valid_keys)
        row_max = jnp.max(scores, axis=-1, keepdims=True)
        exponent = jnp.exp(scores - row_max)
        row_total = jnp.sum(exponent, axis=-1, keepdims=True)
        soft_probs = exponent / row_total
        log_total = row_max + jnp.log(row_total)
        attended = jnp.einsum(
            "bhlm,bmhc->blhc",
            soft_probs.astype(jnp.bfloat16),
            values,
            preferred_element_type=jnp.float32,
        )
        attended = attended.astype(jnp.bfloat16).reshape(row_count, D)
        attn_out = (join(times(attended, proj_own), times(attended, proj_sib)) + b_proj).reshape(
            images, SEQ, D
        )
        middle = token_float + gate_one * attn_out
        normed_two, inverse_two = norm_rows(middle)
        mlp_in = (
            (normed_two * (1.0 + scale_two) + shift_two).astype(jnp.bfloat16).reshape(row_count, D)
        )
        hidden = join(times(mlp_in, fc1_own), times(mlp_in, fc1_sib)) + b_fc1
        active = gelu_tanh(hidden).astype(jnp.bfloat16)
        branch = (join(times(active, fc2_own), times(active, fc2_sib)) + b_fc2).reshape(
            images, SEQ, D
        )
        result = (middle + gate_two * branch).astype(jnp.bfloat16)
        grad_out = (
            cotangent.astype(jnp.float32)
            * (valid_keys.astype(jnp.float32) * image_scale[:, None])[:, :, None]
        )
        d_gate_two = jnp.sum(grad_out * branch, axis=1)
        d_branch = (gate_two * grad_out).astype(jnp.bfloat16).reshape(row_count, D)
        d_branch_own, d_branch_sib = split(d_branch)
        bias_fc2 = jnp.sum(d_branch, axis=0, dtype=jnp.float32)
        d_active = times_t(d_branch_own, fc2_own) + times_t(d_branch_sib, fc2_sib)
        d_hidden = jax.vjp(gelu_tanh, hidden)[1](d_active)[0].astype(jnp.bfloat16)
        d_hidden_own, d_hidden_sib = split(d_hidden)
        bias_fc1 = jnp.sum(d_hidden, axis=0, dtype=jnp.float32)
        d_mlp_in = (times_t(d_hidden_own, fc1_own) + times_t(d_hidden_sib, fc1_sib)).reshape(
            images, SEQ, D
        )
        d_shift_two = jnp.sum(d_mlp_in, axis=1)
        d_scale_two = jnp.sum(d_mlp_in * normed_two, axis=1)
        d_middle = grad_out + norm_back(d_mlp_in * (1.0 + scale_two), normed_two, inverse_two)
        d_gate_one = jnp.sum(d_middle * attn_out, axis=1)
        d_attn = (gate_one * d_middle).astype(jnp.bfloat16).reshape(row_count, D)
        d_attn_own, d_attn_sib = split(d_attn)
        bias_proj = jnp.sum(d_attn, axis=0, dtype=jnp.float32)
        d_attended = times_t(d_attn_own, proj_own) + times_t(d_attn_sib, proj_sib)
        d_attended = d_attended.astype(jnp.bfloat16).reshape(images, SEQ, H, HD)
        soft_again = jnp.exp(masked_scores(query, keys, valid_keys) - log_total)
        grad_values = jnp.einsum(
            "bhlm,blhc->bmhc",
            soft_again.astype(jnp.bfloat16),
            d_attended,
            preferred_element_type=jnp.float32,
        )
        d_probs = jnp.einsum("blhc,bmhc->bhlm", d_attended, values, preferred_element_type=jnp.float32)
        d_scores = soft_again * (d_probs - jnp.sum(soft_again * d_probs, axis=-1, keepdims=True))
        d_scores = jnp.where(valid_keys[:, None, None, :], d_scores, 0.0).astype(jnp.bfloat16)
        grad_query = jnp.einsum(
            "bhlm,bmhc->blhc", d_scores, keys, preferred_element_type=jnp.float32
        ) * HD ** (-0.5)
        grad_keys = jnp.einsum(
            "bhlm,blhc->bmhc", d_scores, query, preferred_element_type=jnp.float32
        ) * HD ** (-0.5)
        d_qkv = (
            jnp.stack([grad_query, grad_keys, grad_values], axis=2)
            .astype(jnp.bfloat16)
            .reshape(row_count, 3 * D)
        )
        d_qkv_own, d_qkv_sib = split(d_qkv)
        bias_query = jnp.sum(d_qkv[:, :D], axis=0, dtype=jnp.float32)
        bias_value = jnp.sum(d_qkv[:, 2 * D :], axis=0, dtype=jnp.float32)
        d_attn_in = (times_t(d_qkv_own, qkv_own) + times_t(d_qkv_sib, qkv_sib)).reshape(
            images, SEQ, D
        )
        d_shift_one = jnp.sum(d_attn_in, axis=1)
        d_scale_one = jnp.sum(d_attn_in * normed_one, axis=1)
        grad_tokens = (
            d_middle + norm_back(d_attn_in * (1.0 + scale_one), normed_one, inverse_one)
        ).astype(jnp.bfloat16)
        d_modul = jnp.concatenate(
            [d_shift_one, d_scale_one, d_gate_one, d_shift_two, d_scale_two, d_gate_two], axis=1
        ).astype(jnp.bfloat16)
    silu_pull = jax.vjp(jax.nn.silu, cond_float)[1]
    grad_condition = silu_pull(jnp.dot(d_modul, w_ada, preferred_element_type=jnp.float32))[0]
    biases = [bias_query, bias_value, bias_proj, bias_fc1, bias_fc2]
    note = jnp.concatenate(
        biases + [d_modul.astype(jnp.float32).reshape(-1), jnp.zeros((2 * lanes,), jnp.float32)]
    ).reshape(-1, lanes)

    if fast:
        pairs = [(attn_in_t, d_split), (attended_t, d_attn)]
        (grad_qkv, grad_proj), note_own, note_sib = scatter_all(pairs, [w_qkv, w_proj], note)
    else:
        terms = [
            (attended.T, d_attn_own, d_attn_sib, w_proj),
            (active.T, d_branch_own, d_branch_sib, w_fc2),
            (attn_in.T, d_qkv_own, d_qkv_sib, w_qkv),
            (mlp_in.T, d_hidden_own, d_hidden_sib, w_fc1),
        ]
        summed_grads, note_own, note_sib = scatter_plain(terms, note)
        grad_proj, grad_fc2, grad_qkv, grad_fc1 = summed_grads
    stacked = (-1,) + note.shape
    total_note = (
        jnp.sum(note_own.reshape(stacked), axis=0) + jnp.sum(note_sib.reshape(stacked), axis=0)
    ).reshape(-1)
    summed, start = [], 0
    for vector in biases + [b_ada]:
        summed.append(total_note[start : start + vector.shape[0]])
        start += vector.shape[0]
    first = start - b_ada.shape[0]
    share_rows = 6 * D // lax.axis_size(("dp", "fsdp"))
    own_start = first + lax.axis_index(("dp", "fsdp")) * share_rows
    notes = jnp.concatenate([note_own, note_sib]).reshape(-1, note.size)
    silus = jnp.concatenate([own_facts, sib_facts])[:, 1:10].reshape(-1, D)
    columns = lax.dynamic_slice_in_dim(notes, own_start, share_rows, 1)
    grad_ada = lax.dot_general(
        columns.astype(jnp.bfloat16),
        silus.astype(jnp.bfloat16),
        ROWS_DIMS,
        preferred_element_type=jnp.float32,
    )
    return (
        result,
        grad_tokens,
        grad_condition,
        grad_qkv,
        summed[0],
        summed[1],
        grad_proj,
        summed[2],
        grad_fc1,
        summed[3],
        grad_fc2,
        summed[4],
        grad_ada,
        summed[5],
    )


def solution(mesh):
    in_specs = (
        P(("dp", "fsdp"), None, None),
        P(("dp", "fsdp"), None),
        P(("dp", "fsdp"), None, None),
        P(("dp", "fsdp"), None),
        P(("dp", "fsdp")),
        P(),
        P("dp", "fsdp"),
        P(),
        P(),
        P("dp", "fsdp"),
        P(),
        P("dp", "fsdp"),
        P(),
        P("dp", "fsdp"),
        P(),
        P(),
        P(),
    )
    out_specs = (
        P(("dp", "fsdp"), None, None),
        P(("dp", "fsdp"), None, None),
        P(("dp", "fsdp"), None),
        P("dp", "fsdp"),
        P(),
        P(),
        P("dp", "fsdp"),
        P(),
        P("dp", "fsdp"),
        P(),
        P("dp", "fsdp"),
        P(),
        P(("dp", "fsdp"), None),
        P(),
    )
    return jax.shard_map(
        functools.partial(shards, dict(mesh.shape) == {"dp": 16, "fsdp": 2}),
        mesh=mesh,
        in_specs=in_specs,
        out_specs=out_specs,
        check_vma=False,
    )
```

```python
import functools

import jax
import jax.numpy as jnp
from jax import lax
from jax.experimental import pallas as pl
from jax.experimental.pallas import tpu as pltpu
from jax.sharding import PartitionSpec as P

D = 1152
H = 16
HD = 72
BINS = 16
SEQ = 256


NEG_FILL = -1e30
NORM_EPS = 1e-06
GELU_COEF = 0.7978845608028654
CUBIC_COEF = 0.044715
ROWS_DIMS = (((0,), (0,)), ((), ()))
LAST_DIMS = (((1,), (1,)), ((), ()))


def gelu_tanh(values_in):
    return (
        0.5
        * values_in
        * (1.0 + jnp.tanh(GELU_COEF * (values_in + CUBIC_COEF * values_in * values_in * values_in)))
    )


def norm_rows(inputs):
    centered = inputs - jnp.mean(inputs, axis=-1, keepdims=True)
    inverse = lax.rsqrt(jnp.mean(centered * centered, axis=-1, keepdims=True) + NORM_EPS)
    return (centered * inverse, inverse)


def norm_back(grad_normed, normed, inverse):
    centered_grad = grad_normed - jnp.mean(grad_normed, axis=-1, keepdims=True)
    return inverse * (
        centered_grad - normed * jnp.mean(grad_normed * normed, axis=-1, keepdims=True)
    )


VMEM_LIMIT = 67_000_000
ANY = pl.BlockSpec(memory_space=pl.ANY)
VMEM = pl.BlockSpec(memory_space=pltpu.VMEM)
ZS = 4
TILE = 256
MID = (1,)
ORDER = (
    (0, 1, 0),
    (0, 0, 0),
    (2, 1, 0),
    (1, 0, 0),
    (0, 0, 1),
    (0, 1, 1),
    (2, 0, 0),
    (1, 0, 1),
    (2, 1, 1),
    (2, 1, 2),
    (2, 0, 1),
    (1, 1, 0),
    (2, 0, 2),
    (3, 1, 0),
    (3, 0, 0),
)
BACK_MID = ()
BACK_ORDER = (
    (0, -1, 0),
    (1, -1, 0),
    (0, 0, 0),
    (0, 0, 1),
    (1, -1, 1),
    (1, -1, 2),
    (2, -1, 0),
    (0, 1, 0),
    (3, -1, 0),
    (4, -1, 0),
    (5, -1, 0),
    (5, -1, 1),
    (1, 0, 0),
    (1, 0, 1),
    (5, -1, 2),
    (1, 1, 0),
    (0, 1, 1),
    (2, 0, 0),
    (2, 0, 1),
    (5, -1, 3),
    (1, 1, 1),
    (2, 1, 0),
    (6, -1, 0),
    (2, 0, 2),
    (3, 0, 0),
    (2, 1, 1),
    (2, 1, 2),
    (7, -1, 0),
    (8, -1, 0),
    (3, 1, 0),
)
BACK_TASKS = ("seed", "widen", "mix", "centre", "project", "attend", "part", "query", "leave")
OFFSETS = (0, -1, 1, -2, 2, -3, 3)
STEPS = ("column", "relay", "last")
TASKS = ("start", "mod", "ln", "load", "query", "attend", "project", "mid", "widen", "narrow", "last")
WEIGHTS = ("qkv", "proj", "fc1", "fc2")
STAGES = ("near", "far", "line", "own")
GATHER_MID = (3,)
GATHER_ORDER = (
    (0, 0, 0),
    (0, 1, 0),
    (0, 2, 0),
    (0, 1, -1),
    (0, 1, 1),
    (0, 3, 0),
    (0, 1, -2),
    (0, 0, -1),
    (0, 1, 2),
    (0, 2, 1),
    (0, -1, 0),
    (0, 1, 3),
    (0, 1, -3),
    (1, 1, 0),
    (0, 2, -1),
    (1, 2, 0),
    (0, 2, 2),
    (0, 0, -2),
    (0, 2, -2),
    (0, 3, 1),
    (0, 2, -3),
    (1, -1, 0),
    (1, 1, -3),
    (0, 0, 1),
    (0, 4, 0),
    (2, 1, -3),
    (1, 2, 1),
    (0, 3, 2),
    (0, 0, -3),
    (1, 1, 3),
    (1, 1, 1),
    (1, 3, 0),
    (0, 3, -1),
    (1, 2, -1),
    (0, 0, 2),
    (1, 1, -1),
    (1, 0, 0),
    (1, 0, -3),
    (1, 3, -1),
    (1, 1, -2),
    (1, 0, -2),
    (2, 1, 3),
    (2, 1, 0),
    (2, 0, -3),
    (1, 1, 2),
    (1, 3, -2),
    (0, 4, -1),
    (1, 2, -3),
    (0, 4, 1),
    (1, 2, -2),
    (1, -1, 1),
    (2, -1, 0),
    (1, 3, -3),
    (2, 0, -2),
    (0, 4, -2),
    (0, 2, 3),
    (1, 3, 1),
    (1, 2, 2),
    (2, 1, 2),
    (2, 0, 0),
    (1, 3, 2),
    (2, 1, -1),
    (0, 0, 3),
    (2, 1, 1),
    (2, 1, -2),
    (0, 4, 2),
    (2, 3, 0),
    (0, 4, -3),
    (3, -1, 0),
    (2, 2, -3),
    (1, 4, 0),
    (4, -1, 0),
    (4, -1, 1),
    (1, 3, 3),
    (0, 3, -2),
    (1, 0, 2),
    (1, 2, 3),
    (2, 3, -1),
    (5, -1, 0),
    (5, -1, 1),
    (2, 2, 0),
    (1, 4, -2),
    (0, 3, -3),
    (0, 3, 3),
    (1, 4, -1),
    (2, 2, 1),
    (1, 0, 3),
    (5, -1, 2),
    (2, 2, 2),
    (2, 2, 3),
    (5, -1, 3),
    (2, 2, -1),
    (2, 2, -2),
    (0, 4, 3),
    (3, -1, 1),
    (1, 4, -3),
    (2, 0, 3),
    (2, 0, 2),
    (2, 3, -3),
    (2, 3, 3),
    (1, 4, 2),
    (1, 4, 1),
    (2, 4, 0),
    (2, 3, 2),
    (6, -1, 0),
    (2, 3, 1),
    (6, -1, 1),
    (1, 4, 3),
    (2, 3, -2),
    (7, -1, 0),
    (3, -1, 2),
    (8, -1, 0),
    (1, 0, 1),
    (2, 4, -1),
    (2, 4, 1),
    (8, -1, 1),
    (2, 4, 2),
    (2, 4, -2),
    (2, 4, -3),
    (8, -1, 2),
    (2, 4, 3),
    (1, 0, -1),
    (2, 0, 1),
    (3, -1, 3),
    (2, 0, -1),
    (9, -1, 0),
    (9, -1, 1),
    (10, -1, 0),
)


class Place:
    def __init__(self):
        self.i = lax.axis_index("dp")
        self.c = lax.axis_index("fsdp")
        self.z = self.i // 4
        self.q = self.i % 4
        self.y = self.q // 2
        self.x = self.q % 2
        self.to_y = 2 * (1 - 2 * self.y)
        self.to_x = 1 - 2 * self.x

    def partners(self, level):
        odd = level % 2
        first = odd * self.to_x + (1 - odd) * self.to_y
        return first, self.to_x + self.to_y - first

    def greet(self):
        barrier = pltpu.get_barrier_semaphore()

        def signal(i, c):
            pl.semaphore_signal(
                barrier,
                inc=1,
                device_id={"dp": i, "fsdp": c},
                device_id_type=pl.DeviceIdType.MESH,
            )

        signal(self.i, 1 - self.c)
        signal(self.i + self.to_y, self.c)
        signal(self.i + self.to_x, self.c)
        up, down = self.z < ZS - 1, self.z > 0
        pl.when(up)(lambda: signal(self.i + 4, self.c))
        pl.when(down)(lambda: signal(self.i - 4, self.c))
        pl.semaphore_wait(barrier, 3 + up.astype(jnp.int32) + down.astype(jnp.int32))


def remote(src, dst, send, recv, i, c):
    return pltpu.make_async_remote_copy(
        src_ref=src,
        dst_ref=dst,
        send_sem=send,
        recv_sem=recv,
        device_id={"dp": i, "fsdp": c},
        device_id_type=pl.DeviceIdType.MESH,
    )


def gather_sems(count):
    dma = pltpu.SemaphoreType.DMA
    return [
        dma((count, 16)),
        dma((count, 16)),
        dma((count, 2, ZS, 2)),
        dma((count, ZS, 3)),
        dma((count, 16)),
        dma((count,)),
    ]


class Gather:
    def __init__(self, at, k, shard, own, sib, sems, mid=False):
        self.mid = mid
        self.at, self.k, self.shard, self.own, self.sib = at, k, shard, own, sib
        self.recv, self.core, self.line, self.pair, self.over, self.local = sems

    def block(self, ref, j):
        rows = self.shard.shape[0]
        return ref.at[pl.ds(pl.multiple_of(j * rows, 8), rows)]

    def send(self, src, j, sem, i):
        return remote(src, self.block(self.own, j), sem, self.recv.at[self.k, j], i, self.at.c)

    def across(self, src, j):
        at, k = self.at, self.k
        return remote(
            src, self.block(self.sib, j), self.over.at[k, j], self.core.at[k, j], at.i, 1 - at.c
        )

    def arrived(self, j):
        at = self.at
        remote(
            self.block(self.own, j),
            self.block(self.own, j),
            self.over.at[self.k, j],
            self.recv.at[self.k, j],
            at.i,
            1 - at.c,
        ).wait_recv()

    def pieces(self, level):
        first, second = self.at.partners(level)
        column = level * 4 + self.at.q
        return first, second, column

    def guard(self, off, run):
        level = self.at.z + off
        if off == 0:
            run(level)
        else:
            pl.when((level >= 0) & (level < ZS))(lambda: run(level))

    def line_copies(self, off, level, slot, src, j):
        at, k = self.at, self.k
        out = []
        if off <= 0:
            copy = self.send(src, j, self.line.at[k, 0, level, slot], at.i + 4)
            out.append((at.z < ZS - 1, copy))
        if off >= 0:
            copy = self.send(src, j, self.line.at[k, 1, level, slot], at.i - 4)
            out.append((at.z > 0, copy))
        return out

    def column_copies(self, off, level):
        at, k = self.at, self.k
        first, second, j = self.pieces(level)
        src = self.shard if off == 0 else self.block(self.own, j)
        lines = self.line_copies(off, level, 0, src, j)
        near = [self.send(src, j, self.pair.at[k, level, 0], at.i + first)]
        rest = [self.send(src, j, self.pair.at[k, level, 1], at.i + second), self.across(src, j)]
        if not self.mid:
            return [], lines, near + rest
        return (near if off == 0 else []), lines, rest

    def column(self, off):
        def run(level):
            if off:
                self.arrived(level * 4 + self.at.q)
            before, lines, after = self.column_copies(off, level)
            for copy in before:
                copy.start()
            for where, copy in lines:
                pl.when(where)(copy.start)
            for copy in after:
                copy.start()
            if off == 0:
                self.keep().start()

        self.guard(off, run)

    def keep(self):
        return pltpu.make_async_copy(
            self.shard, self.block(self.own, self.at.i), self.local.at[self.k]
        )

    def relay_copies(self, off, level):
        first, second, column = self.pieces(level)
        j = column + first
        src = self.block(self.own, j)
        lines = self.line_copies(off, level, 1, src, j) if self.mid else []
        return lines, [
            self.send(src, j, self.pair.at[self.k, level, 2], self.at.i + second),
            self.across(src, j),
        ]

    def relay(self, off):
        def run(level):
            first, _, column = self.pieces(level)
            self.arrived(column + first)
            lines, after = self.relay_copies(off, level)
            for where, copy in lines:
                pl.when(where)(copy.start)
            for copy in after:
                copy.start()

        self.guard(off, run)

    def last_copies(self, level):
        first, second, column = self.pieces(level)
        return [(j, self.across(self.block(self.own, j), j)) for j in (column + second, column + first + second)]

    def last(self, off):
        def run(level):
            for j, copy in self.last_copies(level):
                self.arrived(j)
                copy.start()

        self.guard(off, run)

    def complete(self):
        self.keep().wait()

        @pl.loop(0, 16)
        def _(j):
            self.across(self.block(self.sib, j), j).wait_recv()

    def finish(self):
        at = self.at
        for off in OFFSETS:

            def run(level, off=off):
                before, lines, after = self.column_copies(off, level)
                more, relays = self.relay_copies(off, level)
                for where, copy in lines + more:
                    pl.when(where)(copy.wait_send)
                for copy in before + after + relays:
                    copy.wait_send()
                for _, copy in self.last_copies(level):
                    copy.wait_send()

            self.guard(off, run)

    def events(self, start, span):
        out = []
        for off in OFFSETS:
            far = abs(off)
            out.append((start + span * 0.15 * far, functools.partial(self.column, off)))
            out.append((start + span * (0.3 + 0.2 * far), functools.partial(self.relay, off)))
            out.append((start + span * (0.6 + 0.2 * far), functools.partial(self.last, off)))
        return out


def spread_rows(rows):
    def over(step):
        @pl.loop(0, rows // 32)
        def _(part):
            step(pl.ds(pl.multiple_of(part * 32, 32), 32))

    return over


def valid_row(facts):
    count = jnp.sum(facts[0:1, :], axis=1, keepdims=True)
    return lax.broadcasted_iota(jnp.int32, (1, SEQ), 1).astype(jnp.float32) < count


def flip(source, out):
    @pl.loop(0, source.shape[-1] // 128)
    def _(t):
        part = pl.ds(pl.multiple_of(t * 128, 128), 128)
        out[part, :] = source[:, part].astype(jnp.float32).T.astype(jnp.bfloat16)


def by_tiles(left, right, emit):
    width = right.shape[-1]

    @pl.loop(0, width // TILE)
    def _(t):
        columns = pl.ds(pl.multiple_of(t * TILE, TILE), TILE)
        emit(columns, jnp.dot(left[...], right[:, columns], preferred_element_type=jnp.float32))

    if width % TILE:
        columns = pl.ds(width // TILE * TILE, width % TILE)
        emit(columns, jnp.dot(left[...], right[:, columns], preferred_element_type=jnp.float32))


class Forward:
    def __init__(self, at, ins, outs, scratch, jobs):
        self.at, self.jobs = at, jobs
        self.tokens, self.condition, self.w_ada, self.bias = ins
        self.facts = jobs[0].shard
        self.b_proj, self.b_fc2 = self.bias.at[3:4], self.bias.at[8:9]
        (
            self.modul,
            self.attn_in_t,
            self.qkv,
            self.lse,
            self.attended_t,
            self.attn_out,
            self.middle,
            self.mlp_in_t,
            self.hidden,
            self.active_t,
            self.branch,
            self.result,
        ) = outs
        self.ada, self.loose = scratch[:2]
        self.weights = dict(zip(WEIGHTS, scratch[2:6]))
        self.attn_in, self.attended, self.mlp_in, self.active = scratch[6:10]
        self.silu, self.b_qkv, self.b_fc1 = scratch[10:13]
        self.ada_sem, self.load_sem = scratch[13:]

    def ada_copy(self, part):
        slot = part % 2
        rows = pl.ds(pl.multiple_of(part * D, D), D)
        return pltpu.make_async_copy(
            self.w_ada.at[rows], self.ada.at[slot], self.ada_sem.at[slot]
        )

    def start(self, _):
        self.ada_copy(0).start()
        self.lse[...] = jnp.zeros(self.lse.shape, jnp.float32)
        self.attended[...] = jnp.zeros(self.attended.shape, jnp.bfloat16)
        silu = jax.nn.silu(self.condition[...].astype(jnp.float32))
        self.silu[...] = jnp.broadcast_to(silu, self.silu.shape).astype(jnp.bfloat16)
        for flat, first in ((self.b_qkv, 0), (self.b_fc1, 4)):
            for part in range(flat.shape[1] // D):
                value = self.bias[first + part : first + part + 1, :]
                flat[:, part * D : (part + 1) * D] = jnp.broadcast_to(value, (8, D))

    def mod(self, half):
        @pl.loop(half * 3, half * 3 + 3)
        def _(part):
            pl.when(part < 5)(lambda: self.ada_copy(part + 1).start())
            self.ada_copy(part).wait()
            value = lax.dot_general(
                self.silu[...],
                self.ada[part % 2],
                LAST_DIMS,
                preferred_element_type=jnp.float32,
            )
            self.modul[part] = value[:8] + self.bias[pl.ds(9 + part, 1), :]

    def piece(self, index):
        return self.modul[index, 0:1, :]

    def ln(self, _):
        @spread_rows(SEQ)
        def _(rows):
            normed, _ = norm_rows(self.tokens[rows, :].astype(jnp.float32))
            self.attn_in[rows, :] = (normed * (1.0 + self.piece(1)) + self.piece(0)).astype(
                jnp.bfloat16
            )

        flip(self.attn_in, self.attn_in_t)

    def load_copies(self, name):
        k = WEIGHTS.index(name)
        job, held, c = self.jobs[k + 1], self.weights[name], self.at.c
        return [
            pltpu.make_async_copy(job.own, held.at[c], self.load_sem.at[k, 0]),
            pltpu.make_async_copy(job.sib, held.at[1 - c], self.load_sem.at[k, 1]),
        ]

    def load(self, k):
        name = WEIGHTS[k]
        self.jobs[k + 1].complete()
        for copy in self.load_copies(name):
            copy.start()

    def loaded(self, name):
        for copy in self.load_copies(name):
            copy.wait()

    def loosely(self, columns, value):
        self.loose[:, columns] = value

    def merge(self, out, bias, start):
        width = out.shape[-1] - start

        @spread_rows(SEQ)
        def _(rows):
            value = pltpu.roll(self.loose[rows, :width], 64, 1) + bias[0:1, start:]
            before = out[rows, start : start + 128].astype(jnp.float32)
            lane = lax.broadcasted_iota(jnp.int32, before.shape, 1)
            seam = jnp.where(lane < 64, before, value[:, :128])
            out[rows, start : start + 128] = seam.astype(out.dtype)
            out[rows, start + 128 :] = value[:, 128:].astype(out.dtype)

    def product(self, left, name, half, out, bias):
        if half == 0:
            self.loaded(name)

            def emit(columns, value):
                out[:, columns] = (value + bias[0:1, columns]).astype(out.dtype)

            by_tiles(left, self.weights[name].at[0], emit)
        else:
            by_tiles(left, self.weights[name].at[1], self.loosely)
            self.merge(out, bias, out.shape[-1] // 256 * 128)

    def query(self, half):
        self.product(self.attn_in, "qkv", half, self.qkv, self.b_qkv)

    def attend(self, part):
        is_valid = valid_row(self.facts)

        @pl.loop(part * 4, part * 4 + 4)
        def _(head):
            begin = head * HD
            tile = begin // 128
            tile = tile - tile // 8
            first = pl.multiple_of(tile * 128, 128)
            window = pl.ds(first, 256)
            lane = lax.broadcasted_iota(jnp.int32, (SEQ, 256), 1) + tile * 128
            inside = (lane >= begin) & (lane < begin + HD)
            query = jnp.where(inside, self.qkv[:, window].astype(jnp.float32), 0.0)
            keys = self.qkv[:, pl.ds(pl.multiple_of(D + tile * 128, 128), 256)]
            values = self.qkv[:, pl.ds(pl.multiple_of(2 * D + tile * 128, 128), 256)]
            scores = lax.dot_general(
                query.astype(jnp.bfloat16), keys, LAST_DIMS, preferred_element_type=jnp.float32
            ) * HD ** (-0.5)
            scores = jnp.where(is_valid, scores, NEG_FILL)
            row_max = jnp.max(scores, axis=1, keepdims=True)
            exponent = jnp.exp(scores - row_max)
            row_total = jnp.sum(exponent, axis=1, keepdims=True)
            probs = (exponent / row_total).astype(jnp.bfloat16)
            value = jnp.dot(probs, values, preferred_element_type=jnp.float32)
            before = self.attended[:, window].astype(jnp.float32)
            self.attended[:, window] = jnp.where(inside, value, before).astype(jnp.bfloat16)
            column = lax.broadcasted_iota(jnp.int32, (SEQ, 128), 1)
            self.lse[...] = jnp.where(
                column == head, row_max + jnp.log(row_total), self.lse[...]
            )

    def project(self, half):
        self.product(self.attended, "proj", half, self.attn_out, self.b_proj)
        if half:
            flip(self.attended, self.attended_t)

    def mid(self, _):
        @spread_rows(SEQ)
        def _(rows):
            middle = (
                self.tokens[rows, :].astype(jnp.float32) + self.piece(2) * self.attn_out[rows, :]
            )
            self.middle[rows, :] = middle
            normed, _ = norm_rows(middle)
            self.mlp_in[rows, :] = (normed * (1.0 + self.piece(4)) + self.piece(3)).astype(
                jnp.bfloat16
            )

        flip(self.mlp_in, self.mlp_in_t)

    def widen(self, part):
        if part == 0:
            self.loaded("fc1")
        weight = self.weights["fc1"]

        @pl.loop(part * 6, part * 6 + 6)
        def _(t):
            columns = pl.ds(pl.multiple_of(t * TILE, TILE), TILE)
            within = pl.ds(pl.multiple_of(t % 9 * TILE, TILE), TILE)
            hidden = (
                jnp.dot(
                    self.mlp_in[...],
                    weight[t // 9, :, within],
                    preferred_element_type=jnp.float32,
                )
                + self.b_fc1[0:1, columns]
            )
            self.hidden[:, columns] = hidden
            active = gelu_tanh(hidden)
            self.active[:, columns] = active.astype(jnp.bfloat16)
            self.active_t[columns, :] = active.T.astype(jnp.bfloat16)

    def narrow(self, half):
        self.product(self.active, "fc2", half, self.branch, self.b_fc2)

    def last(self, _):
        @spread_rows(SEQ)
        def _(rows):
            self.result[rows, :] = (
                self.middle[rows, :] + self.piece(5) * self.branch[rows, :]
            ).astype(jnp.bfloat16)


def gather_kernel(count, *refs):
    refs = list(refs)

    def take(n):
        out = refs[:n]
        del refs[:n]
        return out

    shards, ins = take(count), take(4)
    own, sib, outs = take(count), take(count), take(12)
    sems, scratch = take(6), take(15)
    at = Place()
    at.greet()
    jobs = [
        Gather(at, k, shards[k], own[k], sib[k], sems, k in GATHER_MID) for k in range(count)
    ]
    forward = Forward(at, ins, outs, scratch, jobs)
    for step, k, off in GATHER_ORDER:
        getattr(forward if k < 0 else jobs[k], (TASKS if k < 0 else STEPS)[step])(off)
    jobs[0].complete()
    for job in jobs:
        job.finish()


def gather_all(shards, ins):
    count = len(shards)
    spread = [jax.ShapeDtypeStruct((16 * s.shape[0], s.shape[1]), s.dtype) for s in shards]
    kinds = [
        ((6, 8, D), jnp.float32),
        ((D, SEQ), jnp.bfloat16),
        ((SEQ, 3 * D), jnp.bfloat16),
        ((SEQ, 128), jnp.float32),
        ((D, SEQ), jnp.bfloat16),
        ((SEQ, D), jnp.float32),
        ((SEQ, D), jnp.float32),
        ((D, SEQ), jnp.bfloat16),
        ((SEQ, 4 * D), jnp.float32),
        ((4 * D, SEQ), jnp.bfloat16),
        ((SEQ, D), jnp.float32),
        ((SEQ, D), jnp.bfloat16),
    ]
    dma = pltpu.SemaphoreType.DMA
    outs = pl.pallas_call(
        functools.partial(gather_kernel, count),
        out_shape=spread + spread + [jax.ShapeDtypeStruct(*kind) for kind in kinds],
        in_specs=[VMEM] * count + [VMEM, VMEM, ANY, VMEM],
        out_specs=[ANY] * (2 * count) + [VMEM] * len(kinds),
        scratch_shapes=gather_sems(count)
        + [pltpu.VMEM((2, D, D), jnp.bfloat16), pltpu.VMEM((SEQ, 1792), jnp.float32)]
        + [pltpu.VMEM((2,) + s.shape, s.dtype) for s in spread[1:]]
        + [pltpu.VMEM((SEQ, width), jnp.bfloat16) for width in (D, D, D, 4 * D)]
        + [pltpu.VMEM((16, D), jnp.bfloat16)]
        + [pltpu.VMEM((8, width), jnp.float32) for width in (3 * D, 4 * D)]
        + [dma((2,)), dma((4, 2))],
        compiler_params=pltpu.CompilerParams(
            collective_id=0, has_side_effects=True, vmem_limit_bytes=VMEM_LIMIT
        ),
        name="gather_all",
    )(*shards, *ins)
    return outs[:count], outs[count : 2 * count], outs[2 * count :]


def blocked(shape):
    rows, cols = shape
    return (rows, cols) if rows % 16 == 0 else (rows // 8, 8, cols)


def total(*values):
    out = values[0].astype(jnp.float32)
    for value in values[1:]:
        out = out + value.astype(jnp.float32)
    return out


class Scatter:
    def __init__(self, at, k, ins, result, bufs, sems):
        self.at, self.k = at, k
        self.left, halves = ins
        self.right, self.away = halves.at[at.c], halves.at[1 - at.c]
        self.result = result
        self.left_sib, self.right_sib, self.held, self.near, self.far, self.line = bufs
        self.mid = self.line.shape[2] == 2
        (
            self.swap_send,
            self.swap_recv,
            self.near_send,
            self.near_recv,
            self.far_send,
            self.far_recv,
            self.line_send,
            self.line_recv,
        ) = sems

    def swaps(self):
        at, k = self.at, self.k
        pairs = ((self.left, self.left_sib), (self.away, self.right_sib))
        return [
            remote(
                src, dst, self.swap_send.at[k, s], self.swap_recv.at[k, s], at.i, 1 - at.c
            )
            for s, (src, dst) in enumerate(pairs)
        ]

    def near_copies(self, level):
        at, k = self.at, self.k
        first, second = at.partners(level)
        column = level * 4 + at.q
        return [
            remote(
                self.held.at[j],
                self.near.at[level, slot],
                self.near_send.at[k, level, slot],
                self.near_recv.at[k, level, slot],
                at.i + second,
                at.c,
            )
            for slot, j in enumerate((column + second, column + first + second))
        ]

    def far_copy(self, level):
        at, k = self.at, self.k
        first, _ = at.partners(level)
        j = level * 4 + at.q + first
        slot = 0 if self.mid else level
        return remote(
            self.held.at[j],
            self.far.at[slot],
            self.far_send.at[k, slot],
            self.far_recv.at[k, slot],
            at.i + first,
            at.c,
        )

    def line_copies(self, way, level):
        at, k = self.at, self.k
        first, _ = at.partners(level)
        column = level * 4 + at.q
        return [
            remote(
                self.held.at[j],
                self.line.at[way, level, slot],
                self.line_send.at[k, way, level, slot],
                self.line_recv.at[k, way, level, slot],
                at.i + (4 if way == 0 else -4),
                at.c,
            )
            for slot, j in enumerate((column, column + first)[: 2 if self.mid else 1])
        ]

    def line_arrived(self, way, level):
        for copy in self.line_copies(way, level):
            if way == 0:
                pl.when(self.at.z > 0)(copy.wait_recv)
            else:
                pl.when(self.at.z < ZS - 1)(copy.wait_recv)

    def begin(self, part):
        self.swaps()[part].start()

    def clear(self):
        zeros = jnp.zeros(self.line.shape[3:], self.line.dtype)

        @pl.when(self.at.z == 0)
        def _():
            @pl.loop(0, ZS)
            def _(level):
                for slot in range(self.line.shape[2]):
                    self.line[0, level, slot] = zeros

        @pl.when(self.at.z == ZS - 1)
        def _():
            @pl.loop(0, ZS)
            def _(level):
                for slot in range(self.line.shape[2]):
                    self.line[1, level, slot] = zeros

    def multiply(self, level):
        cols = self.held.shape[-1]
        rows = self.left.shape[0] // 16
        group = max(1, 288 // rows)
        height = group * rows
        wide = cols // TILE

        def block(part, columns):
            where = pl.ds(pl.multiple_of((level * 4 + part * group) * rows, 32), height)
            value = jnp.dot(
                self.left[where, :], self.right[:, columns], preferred_element_type=jnp.float32
            ) + jnp.dot(
                self.left_sib[where, :],
                self.right_sib[:, columns],
                preferred_element_type=jnp.float32,
            )
            for g in range(group):
                piece = value[g * rows : (g + 1) * rows]
                if len(self.held.shape) == 4:
                    piece = piece.reshape((rows // 8, 8, piece.shape[-1]))
                self.held[level * 4 + part * group + g, ..., columns] = piece.astype(jnp.bfloat16)

        @pl.loop(0, 4 // group)
        def _(part):
            @pl.loop(0, wide)
            def _(t):
                block(part, pl.ds(pl.multiple_of(t * TILE, TILE), TILE))

            if cols % TILE:
                block(part, pl.ds(wide * TILE, cols % TILE))

    def ready(self):
        for copy in self.swaps():
            copy.wait_recv()

    def stage_near(self, pair):
        @pl.loop(0, 2)
        def _(t):
            level = (1 - pair) * 3 * t + pair * (1 + t)
            self.multiply(level)
            for copy in self.near_copies(level):
                copy.start()

    def stage_far(self, pair):
        if self.mid:
            self.far_mid()
        else:
            pl.loop(0, 2)(lambda t: self.far_level((1 - pair) * 3 * t + pair * (1 + t)))

    def far_level(self, level):
        first, _ = self.at.partners(level)
        j = level * 4 + self.at.q + first
        for copy in self.near_copies(level):
            copy.wait_recv()
        self.held[j] = total(self.held[j], self.near[level, 1]).astype(jnp.bfloat16)
        self.far_copy(level).start()

    def far_mid(self):
        level = self.at.z
        first, _ = self.at.partners(level)
        j = level * 4 + self.at.q + first
        for copy in self.near_copies(level):
            copy.wait_recv()
        self.line_arrived(0, level)
        self.line_arrived(1, level)
        self.held[j] = total(
            self.held[j], self.near[level, 1], self.line[0, level, 1], self.line[1, level, 1]
        ).astype(jnp.bfloat16)
        self.far_copy(level).start()

    def pass_on(self, way, level):
        first, _ = self.at.partners(level)
        column = level * 4 + self.at.q
        if self.mid:
            for copy in self.near_copies(level):
                copy.wait_recv()
        else:
            self.far_copy(level).wait_recv()
        self.line_arrived(way, level)
        copies = self.line_copies(way, level)
        for slot, copy in enumerate(copies):
            j = column + slot * first
            values = [self.held[j], self.near[level, slot], self.line[way, level, slot]]
            if not self.mid:
                values.append(self.far[level])
            self.held[j] = total(*values).astype(jnp.bfloat16)
            copy.start()

    def stage_line(self, back):
        z = self.at.z
        if back < ZS - 1:
            up, down = ZS - 1 - back, back
            pl.when(z < up)(lambda: self.pass_on(0, up))
            pl.when(z > down)(lambda: self.pass_on(1, down))

    def stage_own(self, _):
        z = self.at.z
        j = self.at.i
        self.far_copy(z).wait_recv()
        if not self.mid:
            self.line_arrived(0, z)
            self.line_arrived(1, z)
        whole = total(
            self.held[j],
            self.near[z, 0],
            self.far[0 if self.mid else z],
            self.line[0, z, 0],
            self.line[1, z, 0],
        )
        self.result[...] = whole.reshape(self.result.shape)

    def finish(self):
        z = self.at.z
        for copy in self.swaps():
            copy.wait_send()

        if self.mid:
            self.far_copy(z).wait_send()

        @pl.loop(0, ZS)
        def _(level):
            for copy in self.near_copies(level):
                copy.wait_send()
            if not self.mid:
                self.far_copy(level).wait_send()
            for way in (0, 1):
                beyond = level > z if way == 0 else level < z
                for copy in self.line_copies(way, level):
                    pl.when(beyond)(copy.wait_send)


def fold(value):
    rows, cols = value.shape
    return jnp.sum(value.reshape(rows // 8, 8, cols), axis=0)


def halve(out, rows, value):
    width = out.shape[-1]
    rest = value[:, width // 128 * 128 :]
    out[0, rows, :] = value[:, :width].astype(jnp.bfloat16)
    rest = pltpu.roll(rest, rest.shape[-1] - 64, 1)
    out[1, rows, :] = rest[:, :width].astype(jnp.bfloat16)


class Backward:
    def __init__(self, at, ins, outs, scratch, jobs):
        self.at, self.jobs = at, jobs
        (
            self.modul,
            self.facts,
            self.facts_own,
            self.facts_sib,
            self.cotangent,
            self.branch,
            self.hidden,
            self.middle,
            self.attn_out,
            self.lse,
            self.qkv,
            self.tokens,
        ) = ins[:12]
        self.own, self.sib = ins[12:16], ins[16:20]
        self.d_attn, self.d_split, self.grad_tokens, self.note = outs
        (
            self.d_branch,
            self.d_hidden,
            self.flow,
            self.d_middle,
            self.d_attended,
            self.d_qkv,
            self.sums,
            self.sums_fc1,
            self.weight,
            self.slim,
            self.wide,
            self.long,
            self.slim_sem,
            self.wide_sem,
            self.long_sem,
        ) = scratch

    def piece(self, index):
        return self.modul[index, 0:1, :]

    def fetches(self, k, t):
        if k in (1, 3):
            buffer, sem = self.slim.at[t % 2], self.slim_sem.at[t % 2]
        else:
            buffer, sem = (self.long, self.long_sem) if k == 0 else (self.wide, self.wide_sem)
        rows = pl.ds(pl.multiple_of(t * 384, 384), 384)
        return [
            pltpu.make_async_copy(self.own[k].at[rows], buffer.at[self.at.c], sem.at[0]),
            pltpu.make_async_copy(self.sib[k].at[rows], buffer.at[1 - self.at.c], sem.at[1]),
        ]

    def fetch(self, k, t):
        for copy in self.fetches(k, t):
            copy.start()

    def fetched(self, k, t):
        for copy in self.fetches(k, t):
            copy.wait()

    def back(self, halves, buffer):
        return lax.dot_general(
            halves[0], buffer[0], LAST_DIMS, preferred_element_type=jnp.float32
        ) + lax.dot_general(halves[1], buffer[1], LAST_DIMS, preferred_element_type=jnp.float32)

    def seed(self, _):
        self.fetch(3, 0)
        self.fetch(2, 0)
        self.fetch(0, 0)
        self.sums[...] = jnp.zeros(self.sums.shape, jnp.float32)
        self.d_qkv[...] = jnp.zeros(self.d_qkv.shape, jnp.bfloat16)
        shape = self.facts_own.shape
        is_count = lax.broadcasted_iota(jnp.int32, shape, 0) % 16 == 0
        counts = jnp.sum(
            jnp.where(is_count, self.facts_own[...] + self.facts_sib[...], 0.0),
            axis=0,
            keepdims=True,
        )
        is_bin = lax.broadcasted_iota(jnp.int32, counts.shape, 1) < BINS
        mean = jnp.sum(counts, axis=1, keepdims=True) / BINS
        bin_scale = self.facts[10:11, :] * mean / jnp.where(is_bin, counts, 1.0)
        mine = self.facts[0:1, :]
        scale = jnp.sum(jnp.where(mine > 0.0, bin_scale, 0.0), axis=1, keepdims=True)
        tokens = jnp.sum(mine, axis=1, keepdims=True)
        row = lax.broadcasted_iota(jnp.int32, shape, 0).astype(jnp.float32)
        self.weight[...] = jnp.where(row < tokens, scale, 0.0)

        @spread_rows(SEQ)
        def _(rows):
            grad = self.cotangent[rows, :].astype(jnp.float32) * self.weight[rows, 0:1]
            d_branch = (self.piece(5) * grad).astype(jnp.bfloat16).astype(jnp.float32)
            self.sums[5] += fold(grad * self.branch[rows, :])
            self.sums[9] += fold(d_branch)
            halve(self.d_branch, rows, d_branch)

        self.jobs[0].begin(1)

    def widen(self, part):
        @pl.loop(part * 4, part * 4 + 4)
        def _(t):
            pl.when(t < 11)(lambda: self.fetch(3, t + 1))
            self.fetched(3, t)
            columns = pl.ds(pl.multiple_of(t * 384, 384), 384)
            within = pl.ds(pl.multiple_of(t % 6 * 384, 384), 384)
            d_active = self.back(self.d_branch, self.slim.at[t % 2])
            pull = jax.vjp(gelu_tanh, self.hidden[:, columns])[1]
            d_hidden = pull(d_active)[0].astype(jnp.bfloat16)
            self.d_hidden[t // 6, :, within] = d_hidden
            self.sums_fc1[:, columns] = fold(d_hidden.astype(jnp.float32))

        if part == 2:
            self.jobs[1].begin(1)
            self.fetch(1, 0)

    def mix(self, _):
        @pl.loop(0, 3)
        def _(t):
            self.fetched(2, t)
            columns = pl.ds(pl.multiple_of(t * 384, 384), 384)
            self.flow[:, columns] = self.back(self.d_hidden, self.wide)
            pl.when(t < 2)(lambda: self.fetch(2, t + 1))

    def centre(self, _):
        @spread_rows(SEQ)
        def _(rows):
            grad = self.cotangent[rows, :].astype(jnp.float32) * self.weight[rows, 0:1]
            normed, inverse = norm_rows(self.middle[rows, :])
            d_mlp = self.flow[rows, :]
            self.sums[3] += fold(d_mlp)
            self.sums[4] += fold(d_mlp * normed)
            d_middle = grad + norm_back(d_mlp * (1.0 + self.piece(4)), normed, inverse)
            self.d_middle[rows, :] = d_middle
            self.sums[2] += fold(d_middle * self.attn_out[rows, :])
            d_attn = (self.piece(2) * d_middle).astype(jnp.bfloat16).astype(jnp.float32)
            self.sums[8] += fold(d_attn)
            halve(self.d_attn, rows, d_attn)

    def project(self, _):
        @pl.loop(0, 3)
        def _(t):
            pl.when(t < 2)(lambda: self.fetch(1, t + 1))
            self.fetched(1, t)
            columns = pl.ds(pl.multiple_of(t * 384, 384), 384)
            self.d_attended[:, columns] = self.back(self.d_attn, self.slim.at[t % 2]).astype(
                jnp.bfloat16
            )

    def attend(self, part):
        is_valid = valid_row(self.facts)

        @pl.loop(part * 4, part * 4 + 4)
        def _(head):
            begin = head * HD
            tile = begin // 128
            tile = tile - tile // 8
            spots = [
                pl.ds(pl.multiple_of(kind * D + tile * 128, 128), 256) for kind in range(3)
            ]
            lane = lax.broadcasted_iota(jnp.int32, (SEQ, 256), 1) + tile * 128
            inside = (lane >= begin) & (lane < begin + HD)

            def only(ref, spot):
                return jnp.where(inside, ref[:, spot].astype(jnp.float32), 0.0).astype(
                    jnp.bfloat16
                )

            query, d_out = only(self.qkv, spots[0]), only(self.d_attended, spots[0])
            keys, values = self.qkv[:, spots[1]], self.qkv[:, spots[2]]
            column = lax.broadcasted_iota(jnp.int32, (SEQ, 128), 1)
            log_total = jnp.sum(
                jnp.where(column == head, self.lse[...], 0.0), axis=1, keepdims=True
            )
            scores = lax.dot_general(
                query, keys, LAST_DIMS, preferred_element_type=jnp.float32
            ) * HD ** (-0.5)
            probs = jnp.exp(jnp.where(is_valid, scores, NEG_FILL) - log_total)
            d_probs = lax.dot_general(
                d_out, values, LAST_DIMS, preferred_element_type=jnp.float32
            )
            inner = jnp.sum(probs * d_probs, axis=1, keepdims=True)
            d_scores = jnp.where(is_valid, probs * (d_probs - inner), 0.0).astype(jnp.bfloat16)
            grads = (
                jnp.dot(d_scores, keys, preferred_element_type=jnp.float32) * HD ** (-0.5),
                lax.dot_general(d_scores, query, ROWS_DIMS, preferred_element_type=jnp.float32)
                * HD ** (-0.5),
                lax.dot_general(
                    probs.astype(jnp.bfloat16),
                    d_out,
                    ROWS_DIMS,
                    preferred_element_type=jnp.float32,
                ),
            )
            for spot, grad in zip(spots, grads):
                before = self.d_qkv[:, spot].astype(jnp.float32)
                self.d_qkv[:, spot] = jnp.where(inside, grad, before).astype(jnp.bfloat16)

    def part(self, _):
        @spread_rows(SEQ)
        def _(rows):
            value = self.d_qkv[rows, :].astype(jnp.float32)
            self.sums[6] += fold(value[:, :D])
            self.sums[7] += fold(value[:, 2 * D :])
            halve(self.d_split, rows, value)

    def query(self, _):
        @pl.loop(0, 3)
        def _(t):
            self.fetched(0, t)
            columns = pl.ds(pl.multiple_of(t * 384, 384), 384)
            self.flow[:, columns] = self.back(self.d_split, self.long)
            pl.when(t < 2)(lambda: self.fetch(0, t + 1))

    def leave(self, _):
        @spread_rows(SEQ)
        def _(rows):
            normed, inverse = norm_rows(self.tokens[rows, :].astype(jnp.float32))
            d_in = self.flow[rows, :]
            self.sums[0] += fold(d_in)
            self.sums[1] += fold(d_in * normed)
            self.grad_tokens[rows, :] = (
                self.d_middle[rows, :] + norm_back(d_in * (1.0 + self.piece(1)), normed, inverse)
            ).astype(jnp.bfloat16)

        for index in range(10):
            row = jnp.sum(self.sums[index], axis=0, keepdims=True)
            if index < 6:
                row = row.astype(jnp.bfloat16).astype(jnp.float32)
            self.note[index : index + 1, :] = row
        for index in range(4):
            self.note[10 + index : 11 + index, :] = jnp.sum(
                self.sums_fc1[:, index * D : (index + 1) * D], axis=0, keepdims=True
            )
        self.note[14:16, :] = jnp.zeros((2, D), jnp.float32)


def scatter_bufs(terms):
    scratch = []
    for left, halves, shard, mid in terms:
        piece = blocked(shard.shape)
        scratch.append(pltpu.VMEM(left.shape, jnp.bfloat16))
        scratch.append(pltpu.VMEM((SEQ, shard.shape[1]), jnp.bfloat16))
        for lead in ((16,), (ZS, 2), (1 if mid else ZS,), (2, ZS, 2 if mid else 1)):
            scratch.append(pltpu.VMEM(lead + piece, jnp.bfloat16))
    dma, count = pltpu.SemaphoreType.DMA, len(terms)
    pairs = ((count, 2), (count, ZS, 2), (count, ZS), (count, 2, ZS, 2))
    return scratch + [dma(shape) for shape in pairs for _ in range(2)]


def back_kernel(*refs):
    refs = list(refs)

    def take(n):
        out = refs[:n]
        del refs[:n]
        return out

    lefts, ins = take(2), take(20)
    results, outs = take(2), take(4)
    scratch = take(15)
    bufs = [take(6) for _ in range(2)]
    sems = take(8)
    at = Place()
    at.greet()
    jobs = [
        Scatter(at, k, (lefts[k], scratch[k]), results[k], bufs[k], sems) for k in range(2)
    ]
    for job in jobs:
        job.begin(0)
        job.clear()
    backward = Backward(at, ins, outs, scratch, jobs)
    seen = set()
    for stage, k, part in BACK_ORDER:
        if k < 0:
            getattr(backward, BACK_TASKS[stage])(part)
            continue
        if k not in seen:
            jobs[k].ready()
            seen.add(k)
        getattr(jobs[k], "stage_" + STAGES[stage])(part)
    for job in jobs:
        job.finish()


def back_all(lefts, ins, shards):
    bf16, f32 = jnp.bfloat16, jnp.float32
    kinds = [
        ((2, SEQ, D // 2), bf16),
        ((2, SEQ, 3 * D // 2), bf16),
        ((SEQ, D), bf16),
        ((16, D), f32),
    ]
    own = [
        ((2, SEQ, D // 2), bf16),
        ((2, SEQ, 2 * D), bf16),
        ((SEQ, D), f32),
        ((SEQ, D), f32),
        ((SEQ, D), bf16),
        ((SEQ, 3 * D), bf16),
        ((10, 8, D), f32),
        ((8, 4 * D), f32),
        ((SEQ, 128), f32),
        ((2, 2, 384, D // 2), bf16),
        ((2, 384, 2 * D), bf16),
        ((2, 384, 3 * D // 2), bf16),
    ]
    dma = pltpu.SemaphoreType.DMA
    terms = [(left, None, shard, k in BACK_MID) for k, (left, shard) in enumerate(zip(lefts, shards))]
    outs = pl.pallas_call(
        back_kernel,
        out_shape=[jax.ShapeDtypeStruct(shard.shape, f32) for shard in shards]
        + [jax.ShapeDtypeStruct(*kind) for kind in kinds],
        in_specs=[VMEM] * 14 + [ANY] * 8,
        out_specs=[VMEM] * 6,
        scratch_shapes=[pltpu.VMEM(*kind) for kind in own]
        + [dma((2, 2)), dma((2,)), dma((2,))]
        + scatter_bufs(terms),
        compiler_params=pltpu.CompilerParams(
            collective_id=1, has_side_effects=True, vmem_limit_bytes=VMEM_LIMIT
        ),
        name="back_all",
    )(*lefts, *ins)
    return outs[:2], outs[2:]


def scatter_kernel(count, *refs):
    refs = list(refs)

    def take(n):
        out = refs[:n]
        del refs[:n]
        return out

    ins = [take(2) for _ in range(count)]
    note, w_ada = take(2)
    results = take(count)
    note_own, note_sib, d_silu = take(3)
    bufs = [take(6) for _ in range(count)]
    sems, note_sems = take(8), take(6)
    ada, ada_sem = take(2)

    def ada_copy(part):
        rows = pl.ds(part * D, D)
        return pltpu.make_async_copy(w_ada.at[rows], ada.at[part % 2], ada_sem.at[part % 2])

    def silu_part(part):
        if part < 5:
            ada_copy(part + 1).start()
        ada_copy(part).wait()
        row = jnp.broadcast_to(note[part : part + 1, :], (16, D)).astype(jnp.bfloat16)
        value = jnp.dot(row, ada[part % 2], preferred_element_type=jnp.float32)
        d_silu[...] = value if part == 0 else d_silu[...] + value

    at = Place()
    at.greet()
    jobs = [Scatter(at, k, ins[k], results[k], bufs[k], sems) for k in range(count)]
    word = Gather(at, 0, note, note_own, note_sib, note_sems)
    whisper = [action for _, action in sorted(word.events(0.0, 1.0), key=lambda item: item[0])]
    for job in jobs:
        job.begin(0)
        job.begin(1)
        job.clear()

    def speak(n):
        for action in whisper[:n]:
            action()
        del whisper[:n]

    ada_copy(0).start()
    speak(1)
    seen = set()
    for turn, (stage, k, part) in enumerate(ORDER):
        if k not in seen:
            jobs[k].ready()
            seen.add(k)
        getattr(jobs[k], "stage_" + STAGES[stage])(part)
        speak(2)
        if turn % 2 and turn < 12:
            silu_part(turn // 2)
    speak(len(whisper))
    for job in jobs:
        job.finish()
    word.complete()
    word.finish()


def scatter_all(pairs, shards, note, w_ada):
    count = len(pairs)
    spread = jax.ShapeDtypeStruct((16 * note.shape[0], note.shape[1]), note.dtype)
    dma = pltpu.SemaphoreType.DMA
    terms = [
        (left, halves, shard, k in MID) for k, ((left, halves), shard) in enumerate(zip(pairs, shards))
    ]
    outs = pl.pallas_call(
        functools.partial(scatter_kernel, count),
        out_shape=[jax.ShapeDtypeStruct(shard.shape, jnp.float32) for shard in shards]
        + [spread, spread, jax.ShapeDtypeStruct((16, D), jnp.float32)],
        in_specs=[VMEM, VMEM] * count + [VMEM, ANY],
        out_specs=[VMEM] * count + [ANY, ANY, VMEM],
        scratch_shapes=scatter_bufs(terms)
        + gather_sems(1)
        + [pltpu.VMEM((2, D, D), jnp.bfloat16), dma((2,))],
        compiler_params=pltpu.CompilerParams(
            collective_id=2, has_side_effects=True, vmem_limit_bytes=VMEM_LIMIT
        ),
        name="scatter_all",
    )(*[part for pair in pairs for part in pair], note, w_ada)
    return outs[:count], outs[count], outs[count + 1], outs[count + 2]


def gather_plain(shards):
    own = [lax.all_gather(s, "dp", axis=0, tiled=True) for s in shards]
    pair = [lax.all_gather(g, "fsdp", axis=0) for g in own]
    other = 1 - lax.axis_index("fsdp")
    return own, [lax.dynamic_index_in_dim(p, other, 0, keepdims=False) for p in pair]


def scatter_plain(terms, note):
    c = lax.axis_index("fsdp")
    results = []
    for left, right, away, shard in terms:
        own, sib = [
            jnp.dot(left, half, preferred_element_type=jnp.float32)
            .astype(jnp.bfloat16)
            .reshape((-1,) + shard.shape)
            for half in (right, away)
        ]
        pair = jnp.where(c == 0, jnp.stack([own, sib]), jnp.stack([sib, own]))
        half = lax.psum_scatter(pair, "fsdp", scatter_dimension=0, tiled=False)
        results.append(
            lax.psum_scatter(
                half.astype(jnp.float32), "dp", scatter_dimension=0, tiled=False
            )
        )
    own, sib = gather_plain([note])
    return results, own[0], sib[0]


def masked_scores(query, keys, valid_keys):
    scaled = jnp.einsum(
        "blhc,bmhc->bhlm", query, keys, preferred_element_type=jnp.float32
    ) * HD ** (-0.5)
    return jnp.where(valid_keys[:, None, None, :], scaled, NEG_FILL)


def shards(
    fast,
    tokens,
    condition,
    cotangent,
    image_grids,
    noise_bins,
    bin_weights,
    w_qkv,
    b_query,
    b_value,
    w_proj,
    b_proj,
    w_fc1,
    b_fc1,
    w_fc2,
    b_fc2,
    w_ada,
    b_ada,
):
    images = tokens.shape[0]
    row_count = images * SEQ
    core = lax.axis_index("fsdp")

    def join(own, sib):
        return jnp.where(
            core == 0,
            jnp.concatenate([own, sib], axis=-1),
            jnp.concatenate([sib, own], axis=-1),
        )

    def split(full):
        half = full.shape[-1] // 2
        low, high = full[..., :half], full[..., half:]
        return jnp.where(core == 0, low, high), jnp.where(core == 0, high, low)

    token_count = image_grids[:, 0] * image_grids[:, 1]
    valid_keys = lax.broadcasted_iota(jnp.int32, (images, SEQ), 1) < token_count[:, None]
    bin_table = (noise_bins[:, None] == lax.broadcasted_iota(jnp.int32, (images, BINS), 1)).astype(
        jnp.float32
    )
    local_counts = jnp.sum(bin_table * token_count[:, None].astype(jnp.float32), axis=0)
    cond_float = condition.astype(jnp.float32)
    silu_cond = jax.nn.silu(cond_float).astype(jnp.bfloat16)
    lanes = 128
    head = jnp.concatenate([local_counts, jnp.zeros((lanes - BINS,), jnp.float32)])[None]
    facts = jnp.concatenate(
        [
            head,
            silu_cond.astype(jnp.float32).reshape(-1, lanes),
            jnp.pad(bin_weights.astype(jnp.float32), (0, lanes - BINS))[None],
            jnp.zeros((5, lanes), jnp.float32),
        ]
    )
    shares = [facts, w_qkv, w_proj, w_fc1, w_fc2]
    bias_qkv = jnp.concatenate([b_query, jnp.zeros_like(b_query), b_value])
    if fast:
        bias = jnp.concatenate(
            [bias_qkv, b_proj, b_fc1, b_fc2, b_ada, jnp.zeros((D,), jnp.float32)]
        ).reshape(16, D)
        ins = [tokens.reshape(SEQ, D), condition, w_ada, bias]
        own, sib, outs = gather_all(shares, ins)
    else:
        own, sib = gather_plain(shares)
        outs = None
    qkv_own, proj_own, fc1_own, fc2_own = own[1:]
    qkv_sib, proj_sib, fc1_sib, fc2_sib = sib[1:]
    own_facts, sib_facts = own[0].reshape(-1, 16, lanes), sib[0].reshape(-1, 16, lanes)
    def times(left, right):
        return jnp.dot(left, right, preferred_element_type=jnp.float32)

    def times_t(left, right):
        return lax.dot_general(left, right, LAST_DIMS, preferred_element_type=jnp.float32)

    if fast:
        modul, attn_in_t, qkv_all, lse, attended_t, attn_out, middle = outs[:7]
        mlp_in_t, hidden, active_t, branch, result = outs[7:]
        ins_back = [
            modul,
            facts,
            own[0],
            sib[0],
            cotangent.reshape(SEQ, D),
            branch,
            hidden,
            middle,
            attn_out,
            lse,
            qkv_all,
            tokens.reshape(SEQ, D),
        ]
        (grad_fc2, grad_fc1), outs = back_all(
            [active_t, mlp_in_t], ins_back + list(own[1:]) + list(sib[1:]), [w_fc2, w_fc1]
        )
        d_attn, d_split, grad_tokens, note = outs
        pairs = [(attn_in_t, d_split), (attended_t, d_attn)]
        (grad_qkv, grad_proj), note_own, note_sib, d_silu = scatter_all(
            pairs, [w_qkv, w_proj], note, w_ada
        )
        d_silu = d_silu[0:1]
        result, grad_tokens = result.reshape(tokens.shape), grad_tokens.reshape(tokens.shape)
    else:
        counts = (jnp.sum(own_facts, axis=0) + jnp.sum(sib_facts, axis=0))[0, :BINS]
        bin_scale = bin_weights.astype(jnp.float32) * (jnp.sum(counts) / BINS) / counts
        image_scale = jnp.sum(bin_table * bin_scale[None, :], axis=1)
        token_float = tokens.astype(jnp.float32)
        normed_one, inverse_one = norm_rows(token_float)
        modul = (
            lax.dot_general(silu_cond, w_ada, LAST_DIMS, preferred_element_type=jnp.float32) + b_ada
        )
        pieces = [modul[:, None, part_index * D : (part_index + 1) * D] for part_index in range(6)]
        shift_one, scale_one, gate_one, shift_two, scale_two, gate_two = pieces
        attn_in = (
            (normed_one * (1.0 + scale_one) + shift_one).astype(jnp.bfloat16).reshape(row_count, D)
        )
        qkv_all = (join(times(attn_in, qkv_own), times(attn_in, qkv_sib)) + bias_qkv).astype(
            jnp.bfloat16
        )
        qkv_heads = qkv_all.reshape(images, SEQ, 3, H, HD)
        query, keys, values = (qkv_heads[:, :, 0], qkv_heads[:, :, 1], qkv_heads[:, :, 2])
        scores = masked_scores(query, keys, valid_keys)
        row_max = jnp.max(scores, axis=-1, keepdims=True)
        exponent = jnp.exp(scores - row_max)
        row_total = jnp.sum(exponent, axis=-1, keepdims=True)
        soft_probs = exponent / row_total
        log_total = row_max + jnp.log(row_total)
        attended = jnp.einsum(
            "bhlm,bmhc->blhc",
            soft_probs.astype(jnp.bfloat16),
            values,
            preferred_element_type=jnp.float32,
        )
        attended = attended.astype(jnp.bfloat16).reshape(row_count, D)
        attn_out = (join(times(attended, proj_own), times(attended, proj_sib)) + b_proj).reshape(
            images, SEQ, D
        )
        middle = token_float + gate_one * attn_out
        normed_two, inverse_two = norm_rows(middle)
        mlp_in = (
            (normed_two * (1.0 + scale_two) + shift_two).astype(jnp.bfloat16).reshape(row_count, D)
        )
        hidden = join(times(mlp_in, fc1_own), times(mlp_in, fc1_sib)) + b_fc1
        active = gelu_tanh(hidden).astype(jnp.bfloat16)
        branch = (join(times(active, fc2_own), times(active, fc2_sib)) + b_fc2).reshape(
            images, SEQ, D
        )
        result = (middle + gate_two * branch).astype(jnp.bfloat16)
        grad_out = (
            cotangent.astype(jnp.float32)
            * (valid_keys.astype(jnp.float32) * image_scale[:, None])[:, :, None]
        )
        d_gate_two = jnp.sum(grad_out * branch, axis=1)
        d_branch = (gate_two * grad_out).astype(jnp.bfloat16).reshape(row_count, D)
        d_branch_own, d_branch_sib = split(d_branch)
        bias_fc2 = jnp.sum(d_branch, axis=0, dtype=jnp.float32)
        d_active = times_t(d_branch_own, fc2_own) + times_t(d_branch_sib, fc2_sib)
        d_hidden = jax.vjp(gelu_tanh, hidden)[1](d_active)[0].astype(jnp.bfloat16)
        d_hidden_own, d_hidden_sib = split(d_hidden)
        bias_fc1 = jnp.sum(d_hidden, axis=0, dtype=jnp.float32)
        d_mlp_in = (times_t(d_hidden_own, fc1_own) + times_t(d_hidden_sib, fc1_sib)).reshape(
            images, SEQ, D
        )
        d_shift_two = jnp.sum(d_mlp_in, axis=1)
        d_scale_two = jnp.sum(d_mlp_in * normed_two, axis=1)
        d_middle = grad_out + norm_back(d_mlp_in * (1.0 + scale_two), normed_two, inverse_two)
        d_gate_one = jnp.sum(d_middle * attn_out, axis=1)
        d_attn = (gate_one * d_middle).astype(jnp.bfloat16).reshape(row_count, D)
        d_attn_own, d_attn_sib = split(d_attn)
        bias_proj = jnp.sum(d_attn, axis=0, dtype=jnp.float32)
        d_attended = times_t(d_attn_own, proj_own) + times_t(d_attn_sib, proj_sib)
        d_attended = d_attended.astype(jnp.bfloat16).reshape(images, SEQ, H, HD)
        soft_again = jnp.exp(masked_scores(query, keys, valid_keys) - log_total)
        grad_values = jnp.einsum(
            "bhlm,blhc->bmhc",
            soft_again.astype(jnp.bfloat16),
            d_attended,
            preferred_element_type=jnp.float32,
        )
        d_probs = jnp.einsum("blhc,bmhc->bhlm", d_attended, values, preferred_element_type=jnp.float32)
        d_scores = soft_again * (d_probs - jnp.sum(soft_again * d_probs, axis=-1, keepdims=True))
        d_scores = jnp.where(valid_keys[:, None, None, :], d_scores, 0.0).astype(jnp.bfloat16)
        grad_query = jnp.einsum(
            "bhlm,bmhc->blhc", d_scores, keys, preferred_element_type=jnp.float32
        ) * HD ** (-0.5)
        grad_keys = jnp.einsum(
            "bhlm,blhc->bmhc", d_scores, query, preferred_element_type=jnp.float32
        ) * HD ** (-0.5)
        d_qkv = (
            jnp.stack([grad_query, grad_keys, grad_values], axis=2)
            .astype(jnp.bfloat16)
            .reshape(row_count, 3 * D)
        )
        d_qkv_own, d_qkv_sib = split(d_qkv)
        bias_query = jnp.sum(d_qkv[:, :D], axis=0, dtype=jnp.float32)
        bias_value = jnp.sum(d_qkv[:, 2 * D :], axis=0, dtype=jnp.float32)
        d_attn_in = (times_t(d_qkv_own, qkv_own) + times_t(d_qkv_sib, qkv_sib)).reshape(
            images, SEQ, D
        )
        d_shift_one = jnp.sum(d_attn_in, axis=1)
        d_scale_one = jnp.sum(d_attn_in * normed_one, axis=1)
        grad_tokens = (
            d_middle + norm_back(d_attn_in * (1.0 + scale_one), normed_one, inverse_one)
        ).astype(jnp.bfloat16)
        d_modul = jnp.concatenate(
            [d_shift_one, d_scale_one, d_gate_one, d_shift_two, d_scale_two, d_gate_two], axis=1
        ).astype(jnp.bfloat16)
        d_silu = jnp.dot(d_modul, w_ada, preferred_element_type=jnp.float32)
        note = jnp.concatenate(
            [d_modul.astype(jnp.float32).reshape(-1)]
            + [bias_query, bias_value, bias_proj, bias_fc2, bias_fc1]
            + [jnp.zeros((2 * D,), jnp.float32)]
        ).reshape(16, D)
        terms = [
            (attended.T, d_attn_own, d_attn_sib, w_proj),
            (active.T, d_branch_own, d_branch_sib, w_fc2),
            (attn_in.T, d_qkv_own, d_qkv_sib, w_qkv),
            (mlp_in.T, d_hidden_own, d_hidden_sib, w_fc1),
        ]
        summed_grads, note_own, note_sib = scatter_plain(terms, note)
        grad_proj, grad_fc2, grad_qkv, grad_fc1 = summed_grads
    grad_condition = jax.vjp(jax.nn.silu, cond_float)[1](d_silu)[0]
    note_own, note_sib = note_own.reshape(-1, 16, D), note_sib.reshape(-1, 16, D)
    summed = jnp.sum(note_own, axis=0) + jnp.sum(note_sib, axis=0)
    share_rows = 6 * D // lax.axis_size(("dp", "fsdp"))
    own_start = lax.axis_index(("dp", "fsdp")) * share_rows
    notes = lax.dynamic_slice_in_dim(
        jnp.concatenate([note_own, note_sib]), own_start // D, 2, 1
    ).reshape(-1, 2 * D)
    silus = jnp.concatenate([own_facts, sib_facts])[:, 1:10].reshape(-1, D)
    columns = lax.dynamic_slice_in_dim(notes, own_start % D, share_rows, 1)
    grad_ada = lax.dot_general(
        columns.astype(jnp.bfloat16),
        silus.astype(jnp.bfloat16),
        ROWS_DIMS,
        preferred_element_type=jnp.float32,
    )
    return (
        result,
        grad_tokens,
        grad_condition,
        grad_qkv,
        summed[6],
        summed[7],
        grad_proj,
        summed[8],
        grad_fc1,
        summed[10:14].reshape(-1),
        grad_fc2,
        summed[9],
        grad_ada,
        summed[:6].reshape(-1),
    )


def solution(mesh):
    in_specs = (
        P(("dp", "fsdp"), None, None),
        P(("dp", "fsdp"), None),
        P(("dp", "fsdp"), None, None),
        P(("dp", "fsdp"), None),
        P(("dp", "fsdp")),
        P(),
        P("dp", "fsdp"),
        P(),
        P(),
        P("dp", "fsdp"),
        P(),
        P("dp", "fsdp"),
        P(),
        P("dp", "fsdp"),
        P(),
        P(),
        P(),
    )
    out_specs = (
        P(("dp", "fsdp"), None, None),
        P(("dp", "fsdp"), None, None),
        P(("dp", "fsdp"), None),
        P("dp", "fsdp"),
        P(),
        P(),
        P("dp", "fsdp"),
        P(),
        P("dp", "fsdp"),
        P(),
        P("dp", "fsdp"),
        P(),
        P(("dp", "fsdp"), None),
        P(),
    )
    return jax.shard_map(
        functools.partial(shards, dict(mesh.shape) == {"dp": 16, "fsdp": 2}),
        mesh=mesh,
        in_specs=in_specs,
        out_specs=out_specs,
        check_vma=False,
    )
```

```python
import functools

import jax
import jax.numpy as jnp
from jax import lax
from jax.experimental import pallas as pl
from jax.experimental.pallas import tpu as pltpu
from jax.sharding import PartitionSpec as P

D = 1152
H = 16
HD = 72
BINS = 16
SEQ = 256


NEG_FILL = -1e30
NORM_EPS = 1e-06
GELU_COEF = 0.7978845608028654
CUBIC_COEF = 0.044715
ROWS_DIMS = (((0,), (0,)), ((), ()))
LAST_DIMS = (((1,), (1,)), ((), ()))


def gelu_tanh(values_in):
    return (
        0.5
        * values_in
        * (1.0 + jnp.tanh(GELU_COEF * (values_in + CUBIC_COEF * values_in * values_in * values_in)))
    )


def norm_rows(inputs):
    centered = inputs - jnp.mean(inputs, axis=-1, keepdims=True)
    inverse = lax.rsqrt(jnp.mean(centered * centered, axis=-1, keepdims=True) + NORM_EPS)
    return (centered * inverse, inverse)


def norm_back(grad_normed, normed, inverse):
    centered_grad = grad_normed - jnp.mean(grad_normed, axis=-1, keepdims=True)
    return inverse * (
        centered_grad - normed * jnp.mean(grad_normed * normed, axis=-1, keepdims=True)
    )


VMEM_LIMIT = 67_000_000
ANY = pl.BlockSpec(memory_space=pl.ANY)
VMEM = pl.BlockSpec(memory_space=pltpu.VMEM)
ZS = 4
TILE = 256
PARTS = (
    (0, 0, 72, 0, 1152, False),
    (0, 0, 72, 1152, 1152, False),
    (1, 0, 72, 0, 896, True),
    (1, 0, 72, 896, 832, False),
    (2, 0, 72, 0, 576, True),
)
ORDER = (
    (0, 4, 0),
    (0, 4, 1),
    (0, 2, 0),
    (0, 0, 0),
    (0, 2, 1),
    (2, 4, 3),
    (2, 4, 0),
    (0, 3, 0),
    (2, 4, 4),
    (2, 2, 0),
    (0, 1, 0),
    (2, 2, 3),
    (2, 2, 4),
    (2, 4, 1),
    (2, 2, 5),
    (2, 4, 5),
    (0, 1, 1),
    (1, 1, 0),
    (2, 4, 2),
    (2, 2, 1),
    (1, 3, 0),
    (0, 3, 1),
    (1, 0, 0),
    (2, 1, 3),
    (1, 1, 1),
    (0, 0, 1),
    (2, 3, 3),
    (2, 1, 4),
    (2, 1, 0),
    (2, 2, 2),
    (2, 1, 5),
    (2, 0, 0),
    (2, 3, 0),
    (1, 3, 1),
    (2, 1, 1),
    (1, 0, 1),
    (1, 4, 0),
    (2, 1, 2),
    (2, 3, 1),
    (2, 0, 3),
    (2, 0, 1),
    (2, 3, 2),
    (2, 3, 4),
    (2, 0, 4),
    (1, 2, 0),
    (2, 3, 5),
    (3, 4, 0),
    (2, 0, 2),
    (3, 1, 0),
    (2, 0, 5),
    (3, 2, 0),
    (3, 3, 0),
    (3, 0, 0),
)
BACK_PARTS = (
    (0, 0, 144, 0, 576, False),
    (0, 144, 144, 0, 576, False),
)
BACK_ORDER = (
    (0, -1, 0),
    (1, -1, 0),
    (0, 1, 0),
    (1, -1, 1),
    (0, 0, 0),
    (1, -1, 2),
    (0, 0, 1),
    (2, -1, 0),
    (1, 1, 0),
    (3, -1, 0),
    (4, -1, 0),
    (1, 0, 0),
    (5, -1, 0),
    (0, 1, 1),
    (2, 1, 0),
    (5, -1, 1),
    (5, -1, 2),
    (1, 0, 1),
    (2, 0, 0),
    (1, 1, 1),
    (2, 0, 1),
    (2, 1, 3),
    (5, -1, 3),
    (2, 1, 1),
    (6, -1, 0),
    (2, 1, 2),
    (2, 0, 3),
    (2, 0, 4),
    (7, -1, 0),
    (2, 1, 4),
    (8, -1, 0),
    (2, 0, 5),
    (2, 0, 2),
    (3, 0, 0),
    (2, 1, 5),
    (3, 1, 0),
)
BACK_TASKS = ("seed", "widen", "mix", "centre", "project", "attend", "part", "query", "leave")
OFFSETS = (0, -1, 1, -2, 2, -3, 3)
STEPS = ("column", "relay", "last")
TASKS = ("start", "mod", "ln", "load", "query", "attend", "project", "mid", "widen", "narrow", "last")
WEIGHTS = ("qkv", "proj", "fc1", "fc2")
STAGES = ("near", "far", "line", "own")
GATHER_MID = (3,)
GATHER_ORDER = (
    (0, 0, 0),
    (0, 1, 0),
    (0, 2, 0),
    (0, 1, -1),
    (0, 1, 1),
    (0, 3, 0),
    (0, 1, -2),
    (0, 0, -1),
    (0, 1, 2),
    (0, 2, 1),
    (0, -1, 0),
    (0, 1, 3),
    (0, 1, -3),
    (1, 1, 0),
    (0, 2, -1),
    (1, 2, 0),
    (0, 2, 2),
    (0, 0, -2),
    (0, 2, -2),
    (0, 3, 1),
    (0, 2, -3),
    (1, -1, 0),
    (1, 1, -3),
    (0, 0, 1),
    (0, 4, 0),
    (2, 1, -3),
    (1, 2, 1),
    (0, 3, 2),
    (0, 0, -3),
    (1, 1, 3),
    (1, 1, 1),
    (1, 3, 0),
    (0, 3, -1),
    (1, 2, -1),
    (0, 0, 2),
    (1, 1, -1),
    (1, 0, 0),
    (1, 0, -3),
    (1, 3, -1),
    (1, 1, -2),
    (1, 0, -2),
    (2, 1, 3),
    (2, 1, 0),
    (2, 0, -3),
    (1, 1, 2),
    (1, 3, -2),
    (0, 4, -1),
    (1, 2, -3),
    (0, 4, 1),
    (1, 2, -2),
    (1, -1, 1),
    (2, -1, 0),
    (1, 3, -3),
    (2, 0, -2),
    (0, 4, -2),
    (0, 2, 3),
    (1, 3, 1),
    (1, 2, 2),
    (2, 1, 2),
    (2, 0, 0),
    (1, 3, 2),
    (2, 1, -1),
    (0, 0, 3),
    (2, 1, 1),
    (2, 1, -2),
    (0, 4, 2),
    (2, 3, 0),
    (0, 4, -3),
    (3, -1, 0),
    (2, 2, -3),
    (1, 4, 0),
    (4, -1, 0),
    (4, -1, 1),
    (1, 3, 3),
    (0, 3, -2),
    (1, 0, 2),
    (1, 2, 3),
    (2, 3, -1),
    (5, -1, 0),
    (5, -1, 1),
    (2, 2, 0),
    (1, 4, -2),
    (0, 3, -3),
    (0, 3, 3),
    (1, 4, -1),
    (2, 2, 1),
    (1, 0, 3),
    (5, -1, 2),
    (2, 2, 2),
    (2, 2, 3),
    (5, -1, 3),
    (2, 2, -1),
    (2, 2, -2),
    (0, 4, 3),
    (3, -1, 1),
    (1, 4, -3),
    (2, 0, 3),
    (2, 0, 2),
    (2, 3, -3),
    (2, 3, 3),
    (1, 4, 2),
    (1, 4, 1),
    (2, 4, 0),
    (2, 3, 2),
    (6, -1, 0),
    (2, 3, 1),
    (6, -1, 1),
    (1, 4, 3),
    (2, 3, -2),
    (7, -1, 0),
    (3, -1, 2),
    (8, -1, 0),
    (1, 0, 1),
    (2, 4, -1),
    (2, 4, 1),
    (8, -1, 1),
    (2, 4, 2),
    (2, 4, -2),
    (2, 4, -3),
    (8, -1, 2),
    (2, 4, 3),
    (1, 0, -1),
    (2, 0, 1),
    (3, -1, 3),
    (2, 0, -1),
    (9, -1, 0),
    (9, -1, 1),
    (10, -1, 0),
)


class Place:
    def __init__(self):
        self.i = lax.axis_index("dp")
        self.c = lax.axis_index("fsdp")
        self.z = self.i // 4
        self.q = self.i % 4
        self.y = self.q // 2
        self.x = self.q % 2
        self.to_y = 2 * (1 - 2 * self.y)
        self.to_x = 1 - 2 * self.x

    def partners(self, level):
        odd = level % 2
        first = odd * self.to_x + (1 - odd) * self.to_y
        return first, self.to_x + self.to_y - first

    def greet(self):
        barrier = pltpu.get_barrier_semaphore()

        def signal(i, c):
            pl.semaphore_signal(
                barrier,
                inc=1,
                device_id={"dp": i, "fsdp": c},
                device_id_type=pl.DeviceIdType.MESH,
            )

        signal(self.i, 1 - self.c)
        signal(self.i + self.to_y, self.c)
        signal(self.i + self.to_x, self.c)
        up, down = self.z < ZS - 1, self.z > 0
        pl.when(up)(lambda: signal(self.i + 4, self.c))
        pl.when(down)(lambda: signal(self.i - 4, self.c))
        pl.semaphore_wait(barrier, 3 + up.astype(jnp.int32) + down.astype(jnp.int32))


def remote(src, dst, send, recv, i, c):
    return pltpu.make_async_remote_copy(
        src_ref=src,
        dst_ref=dst,
        send_sem=send,
        recv_sem=recv,
        device_id={"dp": i, "fsdp": c},
        device_id_type=pl.DeviceIdType.MESH,
    )


def gather_sems(count):
    dma = pltpu.SemaphoreType.DMA
    return [
        dma((count, 16)),
        dma((count, 16)),
        dma((count, 2, ZS, 2)),
        dma((count, ZS, 3)),
        dma((count, 16)),
        dma((count,)),
    ]


class Gather:
    def __init__(self, at, k, shard, own, sib, sems, mid=False):
        self.mid = mid
        self.at, self.k, self.shard, self.own, self.sib = at, k, shard, own, sib
        self.recv, self.core, self.line, self.pair, self.over, self.local = sems

    def block(self, ref, j):
        rows = self.shard.shape[0]
        return ref.at[pl.ds(pl.multiple_of(j * rows, 8), rows)]

    def send(self, src, j, sem, i):
        return remote(src, self.block(self.own, j), sem, self.recv.at[self.k, j], i, self.at.c)

    def across(self, src, j):
        at, k = self.at, self.k
        return remote(
            src, self.block(self.sib, j), self.over.at[k, j], self.core.at[k, j], at.i, 1 - at.c
        )

    def arrived(self, j):
        at = self.at
        remote(
            self.block(self.own, j),
            self.block(self.own, j),
            self.over.at[self.k, j],
            self.recv.at[self.k, j],
            at.i,
            1 - at.c,
        ).wait_recv()

    def pieces(self, level):
        first, second = self.at.partners(level)
        column = level * 4 + self.at.q
        return first, second, column

    def guard(self, off, run):
        level = self.at.z + off
        if off == 0:
            run(level)
        else:
            pl.when((level >= 0) & (level < ZS))(lambda: run(level))

    def line_copies(self, off, level, slot, src, j):
        at, k = self.at, self.k
        out = []
        if off <= 0:
            copy = self.send(src, j, self.line.at[k, 0, level, slot], at.i + 4)
            out.append((at.z < ZS - 1, copy))
        if off >= 0:
            copy = self.send(src, j, self.line.at[k, 1, level, slot], at.i - 4)
            out.append((at.z > 0, copy))
        return out

    def column_copies(self, off, level):
        at, k = self.at, self.k
        first, second, j = self.pieces(level)
        src = self.shard if off == 0 else self.block(self.own, j)
        lines = self.line_copies(off, level, 0, src, j)
        near = [self.send(src, j, self.pair.at[k, level, 0], at.i + first)]
        rest = [self.send(src, j, self.pair.at[k, level, 1], at.i + second), self.across(src, j)]
        if not self.mid:
            return [], lines, near + rest
        return (near if off == 0 else []), lines, rest

    def column(self, off):
        def run(level):
            if off:
                self.arrived(level * 4 + self.at.q)
            before, lines, after = self.column_copies(off, level)
            for copy in before:
                copy.start()
            for where, copy in lines:
                pl.when(where)(copy.start)
            for copy in after:
                copy.start()
            if off == 0:
                self.keep().start()

        self.guard(off, run)

    def keep(self):
        return pltpu.make_async_copy(
            self.shard, self.block(self.own, self.at.i), self.local.at[self.k]
        )

    def relay_copies(self, off, level):
        first, second, column = self.pieces(level)
        j = column + first
        src = self.block(self.own, j)
        lines = self.line_copies(off, level, 1, src, j) if self.mid else []
        return lines, [
            self.send(src, j, self.pair.at[self.k, level, 2], self.at.i + second),
            self.across(src, j),
        ]

    def relay(self, off):
        def run(level):
            first, _, column = self.pieces(level)
            self.arrived(column + first)
            lines, after = self.relay_copies(off, level)
            for where, copy in lines:
                pl.when(where)(copy.start)
            for copy in after:
                copy.start()

        self.guard(off, run)

    def last_copies(self, level):
        first, second, column = self.pieces(level)
        return [(j, self.across(self.block(self.own, j), j)) for j in (column + second, column + first + second)]

    def last(self, off):
        def run(level):
            for j, copy in self.last_copies(level):
                self.arrived(j)
                copy.start()

        self.guard(off, run)

    def complete(self):
        self.keep().wait()

        @pl.loop(0, 16)
        def _(j):
            self.across(self.block(self.sib, j), j).wait_recv()

    def finish(self):
        at = self.at
        for off in OFFSETS:

            def run(level, off=off):
                before, lines, after = self.column_copies(off, level)
                more, relays = self.relay_copies(off, level)
                for where, copy in lines + more:
                    pl.when(where)(copy.wait_send)
                for copy in before + after + relays:
                    copy.wait_send()
                for _, copy in self.last_copies(level):
                    copy.wait_send()

            self.guard(off, run)

    def events(self, start, span):
        out = []
        for off in OFFSETS:
            far = abs(off)
            out.append((start + span * 0.15 * far, functools.partial(self.column, off)))
            out.append((start + span * (0.3 + 0.2 * far), functools.partial(self.relay, off)))
            out.append((start + span * (0.6 + 0.2 * far), functools.partial(self.last, off)))
        return out


def spread_rows(rows):
    def over(step):
        @pl.loop(0, rows // 32)
        def _(part):
            step(pl.ds(pl.multiple_of(part * 32, 32), 32))

    return over


def valid_row(facts):
    count = jnp.sum(facts[0:1, :], axis=1, keepdims=True)
    return lax.broadcasted_iota(jnp.int32, (1, SEQ), 1).astype(jnp.float32) < count


def flip(source, out):
    @pl.loop(0, source.shape[-1] // 128)
    def _(t):
        part = pl.ds(pl.multiple_of(t * 128, 128), 128)
        out[part, :] = source[:, part].astype(jnp.float32).T.astype(jnp.bfloat16)


def by_tiles(left, right, emit):
    width = right.shape[-1]

    @pl.loop(0, width // TILE)
    def _(t):
        columns = pl.ds(pl.multiple_of(t * TILE, TILE), TILE)
        emit(columns, jnp.dot(left[...], right[:, columns], preferred_element_type=jnp.float32))

    if width % TILE:
        columns = pl.ds(width // TILE * TILE, width % TILE)
        emit(columns, jnp.dot(left[...], right[:, columns], preferred_element_type=jnp.float32))


class Forward:
    def __init__(self, at, ins, outs, scratch, jobs):
        self.at, self.jobs = at, jobs
        self.tokens, self.condition, self.w_ada, self.bias = ins
        self.facts = jobs[0].shard
        self.b_proj, self.b_fc2 = self.bias.at[3:4], self.bias.at[8:9]
        (
            self.modul,
            self.attn_in_t,
            self.qkv,
            self.lse,
            self.attended_t,
            self.attn_out,
            self.middle,
            self.mlp_in_t,
            self.hidden,
            self.active_t,
            self.branch,
            self.result,
        ) = outs
        self.ada, self.loose = scratch[:2]
        self.weights = dict(zip(WEIGHTS, scratch[2:6]))
        self.attn_in, self.attended, self.mlp_in, self.active = scratch[6:10]
        self.silu, self.b_qkv, self.b_fc1 = scratch[10:13]
        self.ada_sem, self.load_sem = scratch[13:]

    def ada_copy(self, part):
        slot = part % 2
        rows = pl.ds(pl.multiple_of(part * D, D), D)
        return pltpu.make_async_copy(
            self.w_ada.at[rows], self.ada.at[slot], self.ada_sem.at[slot]
        )

    def start(self, _):
        self.ada_copy(0).start()
        self.lse[...] = jnp.zeros(self.lse.shape, jnp.float32)
        self.attended[...] = jnp.zeros(self.attended.shape, jnp.bfloat16)
        silu = jax.nn.silu(self.condition[...].astype(jnp.float32))
        self.silu[...] = jnp.broadcast_to(silu, self.silu.shape).astype(jnp.bfloat16)
        for flat, first in ((self.b_qkv, 0), (self.b_fc1, 4)):
            for part in range(flat.shape[1] // D):
                value = self.bias[first + part : first + part + 1, :]
                flat[:, part * D : (part + 1) * D] = jnp.broadcast_to(value, (8, D))

    def mod(self, half):
        @pl.loop(half * 3, half * 3 + 3)
        def _(part):
            pl.when(part < 5)(lambda: self.ada_copy(part + 1).start())
            self.ada_copy(part).wait()
            value = lax.dot_general(
                self.silu[...],
                self.ada[part % 2],
                LAST_DIMS,
                preferred_element_type=jnp.float32,
            )
            self.modul[part] = value[:8] + self.bias[pl.ds(9 + part, 1), :]

    def piece(self, index):
        return self.modul[index, 0:1, :]

    def ln(self, _):
        @spread_rows(SEQ)
        def _(rows):
            normed, _ = norm_rows(self.tokens[rows, :].astype(jnp.float32))
            self.attn_in[rows, :] = (normed * (1.0 + self.piece(1)) + self.piece(0)).astype(
                jnp.bfloat16
            )

        flip(self.attn_in, self.attn_in_t)

    def load_copies(self, name):
        k = WEIGHTS.index(name)
        job, held, c = self.jobs[k + 1], self.weights[name], self.at.c
        return [
            pltpu.make_async_copy(job.own, held.at[c], self.load_sem.at[k, 0]),
            pltpu.make_async_copy(job.sib, held.at[1 - c], self.load_sem.at[k, 1]),
        ]

    def load(self, k):
        name = WEIGHTS[k]
        self.jobs[k + 1].complete()
        for copy in self.load_copies(name):
            copy.start()

    def loaded(self, name):
        for copy in self.load_copies(name):
            copy.wait()

    def loosely(self, columns, value):
        self.loose[:, columns] = value

    def merge(self, out, bias, start):
        width = out.shape[-1] - start

        @spread_rows(SEQ)
        def _(rows):
            value = pltpu.roll(self.loose[rows, :width], 64, 1) + bias[0:1, start:]
            before = out[rows, start : start + 128].astype(jnp.float32)
            lane = lax.broadcasted_iota(jnp.int32, before.shape, 1)
            seam = jnp.where(lane < 64, before, value[:, :128])
            out[rows, start : start + 128] = seam.astype(out.dtype)
            out[rows, start + 128 :] = value[:, 128:].astype(out.dtype)

    def product(self, left, name, half, out, bias):
        if half == 0:
            self.loaded(name)

            def emit(columns, value):
                out[:, columns] = (value + bias[0:1, columns]).astype(out.dtype)

            by_tiles(left, self.weights[name].at[0], emit)
        else:
            by_tiles(left, self.weights[name].at[1], self.loosely)
            self.merge(out, bias, out.shape[-1] // 256 * 128)

    def query(self, half):
        self.product(self.attn_in, "qkv", half, self.qkv, self.b_qkv)

    def attend(self, part):
        is_valid = valid_row(self.facts)

        @pl.loop(part * 4, part * 4 + 4)
        def _(head):
            begin = head * HD
            tile = begin // 128
            tile = tile - tile // 8
            first = pl.multiple_of(tile * 128, 128)
            window = pl.ds(first, 256)
            lane = lax.broadcasted_iota(jnp.int32, (SEQ, 256), 1) + tile * 128
            inside = (lane >= begin) & (lane < begin + HD)
            query = jnp.where(inside, self.qkv[:, window].astype(jnp.float32), 0.0)
            keys = self.qkv[:, pl.ds(pl.multiple_of(D + tile * 128, 128), 256)]
            values = self.qkv[:, pl.ds(pl.multiple_of(2 * D + tile * 128, 128), 256)]
            scores = lax.dot_general(
                query.astype(jnp.bfloat16), keys, LAST_DIMS, preferred_element_type=jnp.float32
            ) * HD ** (-0.5)
            scores = jnp.where(is_valid, scores, NEG_FILL)
            row_max = jnp.max(scores, axis=1, keepdims=True)
            exponent = jnp.exp(scores - row_max)
            row_total = jnp.sum(exponent, axis=1, keepdims=True)
            probs = (exponent / row_total).astype(jnp.bfloat16)
            value = jnp.dot(probs, values, preferred_element_type=jnp.float32)
            before = self.attended[:, window].astype(jnp.float32)
            self.attended[:, window] = jnp.where(inside, value, before).astype(jnp.bfloat16)
            column = lax.broadcasted_iota(jnp.int32, (SEQ, 128), 1)
            self.lse[...] = jnp.where(
                column == head, row_max + jnp.log(row_total), self.lse[...]
            )

    def project(self, half):
        self.product(self.attended, "proj", half, self.attn_out, self.b_proj)
        if half:
            flip(self.attended, self.attended_t)

    def mid(self, _):
        @spread_rows(SEQ)
        def _(rows):
            middle = (
                self.tokens[rows, :].astype(jnp.float32) + self.piece(2) * self.attn_out[rows, :]
            )
            self.middle[rows, :] = middle
            normed, _ = norm_rows(middle)
            self.mlp_in[rows, :] = (normed * (1.0 + self.piece(4)) + self.piece(3)).astype(
                jnp.bfloat16
            )

        flip(self.mlp_in, self.mlp_in_t)

    def widen(self, part):
        if part == 0:
            self.loaded("fc1")
        weight = self.weights["fc1"]

        @pl.loop(part * 6, part * 6 + 6)
        def _(t):
            columns = pl.ds(pl.multiple_of(t * TILE, TILE), TILE)
            within = pl.ds(pl.multiple_of(t % 9 * TILE, TILE), TILE)
            hidden = (
                jnp.dot(
                    self.mlp_in[...],
                    weight[t // 9, :, within],
                    preferred_element_type=jnp.float32,
                )
                + self.b_fc1[0:1, columns]
            )
            self.hidden[:, columns] = hidden
            active = gelu_tanh(hidden)
            self.active[:, columns] = active.astype(jnp.bfloat16)
            self.active_t[columns, :] = active.T.astype(jnp.bfloat16)

    def narrow(self, half):
        self.product(self.active, "fc2", half, self.branch, self.b_fc2)

    def last(self, _):
        @spread_rows(SEQ)
        def _(rows):
            self.result[rows, :] = (
                self.middle[rows, :] + self.piece(5) * self.branch[rows, :]
            ).astype(jnp.bfloat16)


def gather_kernel(count, *refs):
    refs = list(refs)

    def take(n):
        out = refs[:n]
        del refs[:n]
        return out

    shards, ins = take(count), take(4)
    own, sib, outs = take(count), take(count), take(12)
    sems, scratch = take(6), take(15)
    at = Place()
    at.greet()
    jobs = [
        Gather(at, k, shards[k], own[k], sib[k], sems, k in GATHER_MID) for k in range(count)
    ]
    forward = Forward(at, ins, outs, scratch, jobs)
    for step, k, off in GATHER_ORDER:
        getattr(forward if k < 0 else jobs[k], (TASKS if k < 0 else STEPS)[step])(off)
    jobs[0].complete()
    for job in jobs:
        job.finish()


def gather_all(shards, ins):
    count = len(shards)
    spread = [jax.ShapeDtypeStruct((16 * s.shape[0], s.shape[1]), s.dtype) for s in shards]
    kinds = [
        ((6, 8, D), jnp.float32),
        ((D, SEQ), jnp.bfloat16),
        ((SEQ, 3 * D), jnp.bfloat16),
        ((SEQ, 128), jnp.float32),
        ((D, SEQ), jnp.bfloat16),
        ((SEQ, D), jnp.float32),
        ((SEQ, D), jnp.float32),
        ((D, SEQ), jnp.bfloat16),
        ((SEQ, 4 * D), jnp.float32),
        ((4 * D, SEQ), jnp.bfloat16),
        ((SEQ, D), jnp.float32),
        ((SEQ, D), jnp.bfloat16),
    ]
    dma = pltpu.SemaphoreType.DMA
    outs = pl.pallas_call(
        functools.partial(gather_kernel, count),
        out_shape=spread + spread + [jax.ShapeDtypeStruct(*kind) for kind in kinds],
        in_specs=[VMEM] * count + [VMEM, VMEM, ANY, VMEM],
        out_specs=[ANY] * (2 * count) + [VMEM] * len(kinds),
        scratch_shapes=gather_sems(count)
        + [pltpu.VMEM((2, D, D), jnp.bfloat16), pltpu.VMEM((SEQ, 1792), jnp.float32)]
        + [pltpu.VMEM((2,) + s.shape, s.dtype) for s in spread[1:]]
        + [pltpu.VMEM((SEQ, width), jnp.bfloat16) for width in (D, D, D, 4 * D)]
        + [pltpu.VMEM((16, D), jnp.bfloat16)]
        + [pltpu.VMEM((8, width), jnp.float32) for width in (3 * D, 4 * D)]
        + [dma((2,)), dma((4, 2))],
        compiler_params=pltpu.CompilerParams(
            collective_id=0, has_side_effects=True, vmem_limit_bytes=VMEM_LIMIT
        ),
        name="gather_all",
    )(*shards, *ins)
    return outs[:count], outs[count : 2 * count], outs[2 * count :]


def blocked(shape):
    rows, cols = shape
    return (rows, cols) if rows % 16 == 0 else (rows // 8, 8, cols)


def total(*values):
    out = values[0].astype(jnp.float32)
    for value in values[1:]:
        out = out + value.astype(jnp.float32)
    return out


class Swap:
    def __init__(self, at, w, ins, bufs, sems):
        self.left, halves = ins
        self.right, away = halves.at[at.c], halves.at[1 - at.c]
        self.left_sib, self.right_sib = bufs
        send, recv = sems
        pairs = ((self.left, self.left_sib), (away, self.right_sib))
        self.copies = lambda: [
            remote(src, dst, send.at[w, s], recv.at[w, s], at.i, 1 - at.c)
            for s, (src, dst) in enumerate(pairs)
        ]
        self.arrived = False

    def begin(self, part):
        self.copies()[part].start()

    def ready(self):
        if not self.arrived:
            for copy in self.copies():
                copy.wait_recv()
        self.arrived = True

    def finish(self):
        for copy in self.copies():
            copy.wait_send()


class Scatter:
    def __init__(self, at, k, swap, part, result, bufs, sems):
        self.at, self.k, self.swap = at, k, swap
        _, self.first_row, rows, self.first_column, columns, _ = part
        self.rows = rows
        self.result = result.at[
            pl.ds(self.first_row, rows), pl.ds(self.first_column, columns)
        ]
        self.held, self.near, self.far, self.line = bufs
        self.mid = self.line.shape[2] == 2
        (
            self.near_send,
            self.near_recv,
            self.far_send,
            self.far_recv,
            self.line_send,
            self.line_recv,
        ) = sems

    def near_copies(self, level):
        at, k = self.at, self.k
        first, second = at.partners(level)
        column = level * 4 + at.q
        return [
            remote(
                self.held.at[j],
                self.near.at[level, slot],
                self.near_send.at[k, level, slot],
                self.near_recv.at[k, level, slot],
                at.i + second,
                at.c,
            )
            for slot, j in enumerate((column + second, column + first + second))
        ]

    def far_copy(self, level):
        at, k = self.at, self.k
        first, _ = at.partners(level)
        j = level * 4 + at.q + first
        slot = 0 if self.mid else level
        return remote(
            self.held.at[j],
            self.far.at[slot],
            self.far_send.at[k, slot],
            self.far_recv.at[k, slot],
            at.i + first,
            at.c,
        )

    def line_copies(self, way, level):
        at, k = self.at, self.k
        first, _ = at.partners(level)
        column = level * 4 + at.q
        return [
            remote(
                self.held.at[j],
                self.line.at[way, level, slot],
                self.line_send.at[k, way, level, slot],
                self.line_recv.at[k, way, level, slot],
                at.i + (4 if way == 0 else -4),
                at.c,
            )
            for slot, j in enumerate((column, column + first)[: 2 if self.mid else 1])
        ]

    def line_arrived(self, way, level):
        for copy in self.line_copies(way, level):
            if way == 0:
                pl.when(self.at.z > 0)(copy.wait_recv)
            else:
                pl.when(self.at.z < ZS - 1)(copy.wait_recv)

    def clear(self):
        zeros = jnp.zeros(self.line.shape[3:], self.line.dtype)

        @pl.when(self.at.z == 0)
        def _():
            @pl.loop(0, ZS)
            def _(level):
                for slot in range(self.line.shape[2]):
                    self.line[0, level, slot] = zeros

        @pl.when(self.at.z == ZS - 1)
        def _():
            @pl.loop(0, ZS)
            def _(level):
                for slot in range(self.line.shape[2]):
                    self.line[1, level, slot] = zeros

    def multiply(self, level):
        cols, rows, swap = self.held.shape[-1], self.rows, self.swap
        whole = swap.left.shape[0] // 16
        group = max(1, 288 // rows) if rows == whole else 1
        height = group * rows
        wide = cols // TILE

        def block(part, start, width):
            where = pl.ds(
                pl.multiple_of((level * 4 + part * group) * whole + self.first_row, 16), height
            )
            columns = pl.ds(pl.multiple_of(self.first_column + start, 128), width)
            value = jnp.dot(
                swap.left[where, :], swap.right[:, columns], preferred_element_type=jnp.float32
            ) + jnp.dot(
                swap.left_sib[where, :],
                swap.right_sib[:, columns],
                preferred_element_type=jnp.float32,
            )
            spot = pl.ds(pl.multiple_of(start, 128), width)
            for g in range(group):
                piece = value[g * rows : (g + 1) * rows]
                if len(self.held.shape) == 4:
                    piece = piece.reshape((rows // 8, 8, piece.shape[-1]))
                self.held[level * 4 + part * group + g, ..., spot] = piece.astype(jnp.bfloat16)

        @pl.loop(0, 4 // group)
        def _(part):
            @pl.loop(0, wide)
            def _(t):
                block(part, t * TILE, TILE)

            if cols % TILE:
                block(part, wide * TILE, cols % TILE)

    def stage_near(self, pair):
        @pl.loop(0, 2)
        def _(t):
            level = (1 - pair) * 3 * t + pair * (1 + t)
            self.multiply(level)
            for copy in self.near_copies(level):
                copy.start()

    def stage_far(self, pair):
        if self.mid:
            self.far_mid()
        else:
            pl.loop(0, 2)(lambda t: self.far_level((1 - pair) * 3 * t + pair * (1 + t)))

    def far_level(self, level):
        first, _ = self.at.partners(level)
        j = level * 4 + self.at.q + first
        for copy in self.near_copies(level):
            copy.wait_recv()
        self.held[j] = total(self.held[j], self.near[level, 1]).astype(jnp.bfloat16)
        self.far_copy(level).start()

    def far_mid(self):
        level = self.at.z
        first, _ = self.at.partners(level)
        j = level * 4 + self.at.q + first
        for copy in self.near_copies(level):
            copy.wait_recv()
        self.line_arrived(0, level)
        self.line_arrived(1, level)
        self.held[j] = total(
            self.held[j], self.near[level, 1], self.line[0, level, 1], self.line[1, level, 1]
        ).astype(jnp.bfloat16)
        self.far_copy(level).start()

    def pass_on(self, way, level):
        first, _ = self.at.partners(level)
        column = level * 4 + self.at.q
        if self.mid:
            for copy in self.near_copies(level):
                copy.wait_recv()
        else:
            self.far_copy(level).wait_recv()
        self.line_arrived(way, level)
        copies = self.line_copies(way, level)
        for slot, copy in enumerate(copies):
            j = column + slot * first
            values = [self.held[j], self.near[level, slot], self.line[way, level, slot]]
            if not self.mid:
                values.append(self.far[level])
            self.held[j] = total(*values).astype(jnp.bfloat16)
            copy.start()

    def stage_line(self, part):
        way, back = part // 3, part % 3
        level = back if way else ZS - 1 - back
        beyond = self.at.z > level if way else self.at.z < level
        pl.when(beyond)(lambda: self.pass_on(way, level))

    def stage_own(self, _):
        z = self.at.z
        j = self.at.i
        self.far_copy(z).wait_recv()
        if not self.mid:
            self.line_arrived(0, z)
            self.line_arrived(1, z)
        whole = total(
            self.held[j],
            self.near[z, 0],
            self.far[0 if self.mid else z],
            self.line[0, z, 0],
            self.line[1, z, 0],
        )
        self.result[...] = whole.reshape(self.result.shape)

    def finish(self):
        z = self.at.z

        if self.mid:
            self.far_copy(z).wait_send()

        @pl.loop(0, ZS)
        def _(level):
            for copy in self.near_copies(level):
                copy.wait_send()
            if not self.mid:
                self.far_copy(level).wait_send()
            for way in (0, 1):
                beyond = level > z if way == 0 else level < z
                for copy in self.line_copies(way, level):
                    pl.when(beyond)(copy.wait_send)


def fold(value):
    rows, cols = value.shape
    return jnp.sum(value.reshape(rows // 8, 8, cols), axis=0)


def halve(out, rows, value):
    width = out.shape[-1]
    rest = value[:, width // 128 * 128 :]
    out[0, rows, :] = value[:, :width].astype(jnp.bfloat16)
    rest = pltpu.roll(rest, rest.shape[-1] - 64, 1)
    out[1, rows, :] = rest[:, :width].astype(jnp.bfloat16)


class Backward:
    def __init__(self, at, ins, outs, scratch, jobs):
        self.at, self.jobs = at, jobs
        (
            self.modul,
            self.facts,
            self.facts_own,
            self.facts_sib,
            self.cotangent,
            self.branch,
            self.hidden,
            self.middle,
            self.attn_out,
            self.lse,
            self.qkv,
            self.tokens,
        ) = ins[:12]
        self.own, self.sib = ins[12:16], ins[16:20]
        self.d_attn, self.d_split, self.grad_tokens, self.note, self.d_hidden = outs
        (
            self.d_branch,
            self.flow,
            self.d_middle,
            self.d_attended,
            self.d_qkv,
            self.sums,
            self.sums_fc1,
            self.weight,
            self.slim,
            self.wide,
            self.long,
            self.slim_sem,
            self.wide_sem,
            self.long_sem,
        ) = scratch

    def piece(self, index):
        return self.modul[index, 0:1, :]

    def fetches(self, k, t):
        if k in (1, 3):
            buffer, sem = self.slim.at[t % 2], self.slim_sem.at[t % 2]
        else:
            buffer, sem = (self.long, self.long_sem) if k == 0 else (self.wide, self.wide_sem)
        rows = pl.ds(pl.multiple_of(t * 384, 384), 384)
        return [
            pltpu.make_async_copy(self.own[k].at[rows], buffer.at[self.at.c], sem.at[0]),
            pltpu.make_async_copy(self.sib[k].at[rows], buffer.at[1 - self.at.c], sem.at[1]),
        ]

    def fetch(self, k, t):
        for copy in self.fetches(k, t):
            copy.start()

    def fetched(self, k, t):
        for copy in self.fetches(k, t):
            copy.wait()

    def back(self, halves, buffer):
        return lax.dot_general(
            halves[0], buffer[0], LAST_DIMS, preferred_element_type=jnp.float32
        ) + lax.dot_general(halves[1], buffer[1], LAST_DIMS, preferred_element_type=jnp.float32)

    def seed(self, _):
        self.fetch(3, 0)
        self.fetch(2, 0)
        self.fetch(0, 0)
        self.sums[...] = jnp.zeros(self.sums.shape, jnp.float32)
        self.d_qkv[...] = jnp.zeros(self.d_qkv.shape, jnp.bfloat16)
        shape = self.facts_own.shape
        is_count = lax.broadcasted_iota(jnp.int32, shape, 0) % 16 == 0
        counts = jnp.sum(
            jnp.where(is_count, self.facts_own[...] + self.facts_sib[...], 0.0),
            axis=0,
            keepdims=True,
        )
        is_bin = lax.broadcasted_iota(jnp.int32, counts.shape, 1) < BINS
        mean = jnp.sum(counts, axis=1, keepdims=True) / BINS
        bin_scale = self.facts[10:11, :] * mean / jnp.where(is_bin, counts, 1.0)
        mine = self.facts[0:1, :]
        scale = jnp.sum(jnp.where(mine > 0.0, bin_scale, 0.0), axis=1, keepdims=True)
        tokens = jnp.sum(mine, axis=1, keepdims=True)
        row = lax.broadcasted_iota(jnp.int32, shape, 0).astype(jnp.float32)
        self.weight[...] = jnp.where(row < tokens, scale, 0.0)

        @spread_rows(SEQ)
        def _(rows):
            grad = self.cotangent[rows, :].astype(jnp.float32) * self.weight[rows, 0:1]
            d_branch = (self.piece(5) * grad).astype(jnp.bfloat16).astype(jnp.float32)
            self.sums[5] += fold(grad * self.branch[rows, :])
            self.sums[9] += fold(d_branch)
            halve(self.d_branch, rows, d_branch)

        self.jobs[0].begin(1)

    def widen(self, part):
        @pl.loop(part * 4, part * 4 + 4)
        def _(t):
            pl.when(t < 11)(lambda: self.fetch(3, t + 1))
            self.fetched(3, t)
            columns = pl.ds(pl.multiple_of(t * 384, 384), 384)
            within = pl.ds(pl.multiple_of(t % 6 * 384, 384), 384)
            d_active = self.back(self.d_branch, self.slim.at[t % 2])
            pull = jax.vjp(gelu_tanh, self.hidden[:, columns])[1]
            d_hidden = pull(d_active)[0].astype(jnp.bfloat16)
            self.d_hidden[t // 6, :, within] = d_hidden
            self.sums_fc1[:, columns] = fold(d_hidden.astype(jnp.float32))

        if part == 2:
            self.fetch(1, 0)

    def mix(self, _):
        @pl.loop(0, 3)
        def _(t):
            self.fetched(2, t)
            columns = pl.ds(pl.multiple_of(t * 384, 384), 384)
            self.flow[:, columns] = self.back(self.d_hidden, self.wide)
            pl.when(t < 2)(lambda: self.fetch(2, t + 1))

    def centre(self, _):
        @spread_rows(SEQ)
        def _(rows):
            grad = self.cotangent[rows, :].astype(jnp.float32) * self.weight[rows, 0:1]
            normed, inverse = norm_rows(self.middle[rows, :])
            d_mlp = self.flow[rows, :]
            self.sums[3] += fold(d_mlp)
            self.sums[4] += fold(d_mlp * normed)
            d_middle = grad + norm_back(d_mlp * (1.0 + self.piece(4)), normed, inverse)
            self.d_middle[rows, :] = d_middle
            self.sums[2] += fold(d_middle * self.attn_out[rows, :])
            d_attn = (self.piece(2) * d_middle).astype(jnp.bfloat16).astype(jnp.float32)
            self.sums[8] += fold(d_attn)
            halve(self.d_attn, rows, d_attn)

    def project(self, _):
        @pl.loop(0, 3)
        def _(t):
            pl.when(t < 2)(lambda: self.fetch(1, t + 1))
            self.fetched(1, t)
            columns = pl.ds(pl.multiple_of(t * 384, 384), 384)
            self.d_attended[:, columns] = self.back(self.d_attn, self.slim.at[t % 2]).astype(
                jnp.bfloat16
            )

    def attend(self, part):
        is_valid = valid_row(self.facts)

        @pl.loop(part * 4, part * 4 + 4)
        def _(head):
            begin = head * HD
            tile = begin // 128
            tile = tile - tile // 8
            spots = [
                pl.ds(pl.multiple_of(kind * D + tile * 128, 128), 256) for kind in range(3)
            ]
            lane = lax.broadcasted_iota(jnp.int32, (SEQ, 256), 1) + tile * 128
            inside = (lane >= begin) & (lane < begin + HD)

            def only(ref, spot):
                return jnp.where(inside, ref[:, spot].astype(jnp.float32), 0.0).astype(
                    jnp.bfloat16
                )

            query, d_out = only(self.qkv, spots[0]), only(self.d_attended, spots[0])
            keys, values = self.qkv[:, spots[1]], self.qkv[:, spots[2]]
            column = lax.broadcasted_iota(jnp.int32, (SEQ, 128), 1)
            log_total = jnp.sum(
                jnp.where(column == head, self.lse[...], 0.0), axis=1, keepdims=True
            )
            scores = lax.dot_general(
                query, keys, LAST_DIMS, preferred_element_type=jnp.float32
            ) * HD ** (-0.5)
            probs = jnp.exp(jnp.where(is_valid, scores, NEG_FILL) - log_total)
            d_probs = lax.dot_general(
                d_out, values, LAST_DIMS, preferred_element_type=jnp.float32
            )
            inner = jnp.sum(probs * d_probs, axis=1, keepdims=True)
            d_scores = jnp.where(is_valid, probs * (d_probs - inner), 0.0).astype(jnp.bfloat16)
            grads = (
                jnp.dot(d_scores, keys, preferred_element_type=jnp.float32) * HD ** (-0.5),
                lax.dot_general(d_scores, query, ROWS_DIMS, preferred_element_type=jnp.float32)
                * HD ** (-0.5),
                lax.dot_general(
                    probs.astype(jnp.bfloat16),
                    d_out,
                    ROWS_DIMS,
                    preferred_element_type=jnp.float32,
                ),
            )
            for spot, grad in zip(spots, grads):
                before = self.d_qkv[:, spot].astype(jnp.float32)
                self.d_qkv[:, spot] = jnp.where(inside, grad, before).astype(jnp.bfloat16)

    def part(self, _):
        @spread_rows(SEQ)
        def _(rows):
            value = self.d_qkv[rows, :].astype(jnp.float32)
            self.sums[6] += fold(value[:, :D])
            self.sums[7] += fold(value[:, 2 * D :])
            halve(self.d_split, rows, value)

    def query(self, _):
        @pl.loop(0, 3)
        def _(t):
            self.fetched(0, t)
            columns = pl.ds(pl.multiple_of(t * 384, 384), 384)
            self.flow[:, columns] = self.back(self.d_split, self.long)
            pl.when(t < 2)(lambda: self.fetch(0, t + 1))

    def leave(self, _):
        @spread_rows(SEQ)
        def _(rows):
            normed, inverse = norm_rows(self.tokens[rows, :].astype(jnp.float32))
            d_in = self.flow[rows, :]
            self.sums[0] += fold(d_in)
            self.sums[1] += fold(d_in * normed)
            self.grad_tokens[rows, :] = (
                self.d_middle[rows, :] + norm_back(d_in * (1.0 + self.piece(1)), normed, inverse)
            ).astype(jnp.bfloat16)

        for index in range(10):
            row = jnp.sum(self.sums[index], axis=0, keepdims=True)
            if index < 6:
                row = row.astype(jnp.bfloat16).astype(jnp.float32)
            self.note[index : index + 1, :] = row
        for index in range(4):
            self.note[10 + index : 11 + index, :] = jnp.sum(
                self.sums_fc1[:, index * D : (index + 1) * D], axis=0, keepdims=True
            )
        self.note[14:16, :] = jnp.zeros((2, D), jnp.float32)


def scatter_bufs(pairs, parts):
    scratch = []
    for left, halves in pairs:
        scratch.append(pltpu.VMEM(left.shape, jnp.bfloat16))
        scratch.append(pltpu.VMEM(halves[1:], jnp.bfloat16))
    for _, _, rows, _, columns, mid in parts:
        piece = blocked((rows, columns))
        for lead in ((16,), (ZS, 2), (1 if mid else ZS,), (2, ZS, 2 if mid else 1)):
            scratch.append(pltpu.VMEM(lead + piece, jnp.bfloat16))
    dma, count = pltpu.SemaphoreType.DMA, len(parts)
    kinds = ((len(pairs), 2), (count, ZS, 2), (count, ZS), (count, 2, ZS, 2))
    return scratch + [dma(shape) for shape in kinds for _ in range(2)]


def scatter_jobs(at, ins, results, take, parts):
    bufs = [take(2) for _ in ins]
    pieces = [take(4) for _ in parts]
    swap_sems, sems = take(2), take(6)
    swaps = [Swap(at, w, ins[w], bufs[w], swap_sems) for w in range(len(ins))]
    jobs = [
        Scatter(at, k, swaps[part[0]], part, results[part[0]], pieces[k], sems)
        for k, part in enumerate(parts)
    ]
    return swaps, jobs


def back_kernel(*refs):
    refs = list(refs)

    def take(n):
        out = refs[:n]
        del refs[:n]
        return out

    lefts, ins = take(1), take(20)
    results, outs = take(1), take(5)
    scratch = take(14)
    at = Place()
    at.greet()
    swaps, jobs = scatter_jobs(at, [(lefts[0], scratch[0])], results, take, BACK_PARTS)
    swaps[0].begin(0)
    for job in jobs:
        job.clear()
    backward = Backward(at, ins, outs, scratch, swaps)
    for stage, k, part in BACK_ORDER:
        if k < 0:
            getattr(backward, BACK_TASKS[stage])(part)
            continue
        jobs[k].swap.ready()
        getattr(jobs[k], "stage_" + STAGES[stage])(part)
    for job in swaps + jobs:
        job.finish()


def back_all(lefts, ins, shards):
    bf16, f32 = jnp.bfloat16, jnp.float32
    kinds = [
        ((2, SEQ, D // 2), bf16),
        ((2, SEQ, 3 * D // 2), bf16),
        ((SEQ, D), bf16),
        ((16, D), f32),
        ((2, SEQ, 2 * D), bf16),
    ]
    own = [
        ((2, SEQ, D // 2), bf16),
        ((SEQ, D), f32),
        ((SEQ, D), f32),
        ((SEQ, D), bf16),
        ((SEQ, 3 * D), bf16),
        ((10, 8, D), f32),
        ((8, 4 * D), f32),
        ((SEQ, 128), f32),
        ((2, 2, 384, D // 2), bf16),
        ((2, 384, 2 * D), bf16),
        ((2, 384, 3 * D // 2), bf16),
    ]
    dma = pltpu.SemaphoreType.DMA
    pairs = [(lefts[0], (2, SEQ, D // 2))]
    outs = pl.pallas_call(
        back_kernel,
        out_shape=[jax.ShapeDtypeStruct(shard.shape, f32) for shard in shards]
        + [jax.ShapeDtypeStruct(*kind) for kind in kinds],
        in_specs=[VMEM] * 13 + [ANY] * 8,
        out_specs=[VMEM] * 6,
        scratch_shapes=[pltpu.VMEM(*kind) for kind in own]
        + [dma((2, 2)), dma((2,)), dma((2,))]
        + scatter_bufs(pairs, BACK_PARTS),
        compiler_params=pltpu.CompilerParams(
            collective_id=1, has_side_effects=True, vmem_limit_bytes=VMEM_LIMIT
        ),
        name="back_all",
    )(*lefts, *ins)
    return outs[:1], outs[1:]


def scatter_kernel(count, *refs):
    refs = list(refs)

    def take(n):
        out = refs[:n]
        del refs[:n]
        return out

    ins = [take(2) for _ in range(count)]
    note, w_ada = take(2)
    results = take(count)
    note_own, note_sib, d_silu = take(3)
    at = Place()
    at.greet()
    swaps, jobs = scatter_jobs(at, ins, results, take, PARTS)
    note_sems = take(6)
    ada, ada_sem = take(2)

    def ada_copy(part):
        rows = pl.ds(part * D, D)
        return pltpu.make_async_copy(w_ada.at[rows], ada.at[part % 2], ada_sem.at[part % 2])

    def silu_part(part):
        if part < 5:
            ada_copy(part + 1).start()
        ada_copy(part).wait()
        row = jnp.broadcast_to(note[part : part + 1, :], (16, D)).astype(jnp.bfloat16)
        value = jnp.dot(row, ada[part % 2], preferred_element_type=jnp.float32)
        d_silu[...] = value if part == 0 else d_silu[...] + value

    word = Gather(at, 0, note, note_own, note_sib, note_sems)
    whisper = [action for _, action in sorted(word.events(0.0, 1.0), key=lambda item: item[0])]
    for swap in swaps:
        swap.begin(0)
        swap.begin(1)
    for job in jobs:
        job.clear()

    def speak(n):
        for action in whisper[:n]:
            action()
        del whisper[:n]

    ada_copy(0).start()
    speak(1)
    for turn, (stage, k, part) in enumerate(ORDER):
        jobs[k].swap.ready()
        getattr(jobs[k], "stage_" + STAGES[stage])(part)
        speak(1)
        if turn % 2 and turn < 12:
            silu_part(turn // 2)
    speak(len(whisper))
    for job in swaps + jobs:
        job.finish()
    word.complete()
    word.finish()


def scatter_all(pairs, shards, note, w_ada):
    count = len(pairs)
    spread = jax.ShapeDtypeStruct((16 * note.shape[0], note.shape[1]), note.dtype)
    dma = pltpu.SemaphoreType.DMA
    shapes = [(left, halves.shape) for left, halves in pairs]
    outs = pl.pallas_call(
        functools.partial(scatter_kernel, count),
        out_shape=[jax.ShapeDtypeStruct(shard.shape, jnp.float32) for shard in shards]
        + [spread, spread, jax.ShapeDtypeStruct((16, D), jnp.float32)],
        in_specs=[VMEM, VMEM] * count + [VMEM, ANY],
        out_specs=[VMEM] * count + [ANY, ANY, VMEM],
        scratch_shapes=scatter_bufs(shapes, PARTS)
        + gather_sems(1)
        + [pltpu.VMEM((2, D, D), jnp.bfloat16), dma((2,))],
        compiler_params=pltpu.CompilerParams(
            collective_id=2, has_side_effects=True, vmem_limit_bytes=VMEM_LIMIT
        ),
        name="scatter_all",
    )(*[part for pair in pairs for part in pair], note, w_ada)
    return outs[:count], outs[count], outs[count + 1], outs[count + 2]


def gather_plain(shards):
    own = [lax.all_gather(s, "dp", axis=0, tiled=True) for s in shards]
    pair = [lax.all_gather(g, "fsdp", axis=0) for g in own]
    other = 1 - lax.axis_index("fsdp")
    return own, [lax.dynamic_index_in_dim(p, other, 0, keepdims=False) for p in pair]


def scatter_plain(terms, note):
    c = lax.axis_index("fsdp")
    results = []
    for left, right, away, shard in terms:
        own, sib = [
            jnp.dot(left, half, preferred_element_type=jnp.float32)
            .astype(jnp.bfloat16)
            .reshape((-1,) + shard.shape)
            for half in (right, away)
        ]
        pair = jnp.where(c == 0, jnp.stack([own, sib]), jnp.stack([sib, own]))
        half = lax.psum_scatter(pair, "fsdp", scatter_dimension=0, tiled=False)
        results.append(
            lax.psum_scatter(
                half.astype(jnp.float32), "dp", scatter_dimension=0, tiled=False
            )
        )
    own, sib = gather_plain([note])
    return results, own[0], sib[0]


def masked_scores(query, keys, valid_keys):
    scaled = jnp.einsum(
        "blhc,bmhc->bhlm", query, keys, preferred_element_type=jnp.float32
    ) * HD ** (-0.5)
    return jnp.where(valid_keys[:, None, None, :], scaled, NEG_FILL)


def shards(
    fast,
    tokens,
    condition,
    cotangent,
    image_grids,
    noise_bins,
    bin_weights,
    w_qkv,
    b_query,
    b_value,
    w_proj,
    b_proj,
    w_fc1,
    b_fc1,
    w_fc2,
    b_fc2,
    w_ada,
    b_ada,
):
    images = tokens.shape[0]
    row_count = images * SEQ
    core = lax.axis_index("fsdp")

    def join(own, sib):
        return jnp.where(
            core == 0,
            jnp.concatenate([own, sib], axis=-1),
            jnp.concatenate([sib, own], axis=-1),
        )

    def split(full):
        half = full.shape[-1] // 2
        low, high = full[..., :half], full[..., half:]
        return jnp.where(core == 0, low, high), jnp.where(core == 0, high, low)

    token_count = image_grids[:, 0] * image_grids[:, 1]
    valid_keys = lax.broadcasted_iota(jnp.int32, (images, SEQ), 1) < token_count[:, None]
    bin_table = (noise_bins[:, None] == lax.broadcasted_iota(jnp.int32, (images, BINS), 1)).astype(
        jnp.float32
    )
    local_counts = jnp.sum(bin_table * token_count[:, None].astype(jnp.float32), axis=0)
    cond_float = condition.astype(jnp.float32)
    silu_cond = jax.nn.silu(cond_float).astype(jnp.bfloat16)
    lanes = 128
    head = jnp.concatenate([local_counts, jnp.zeros((lanes - BINS,), jnp.float32)])[None]
    facts = jnp.concatenate(
        [
            head,
            silu_cond.astype(jnp.float32).reshape(-1, lanes),
            jnp.pad(bin_weights.astype(jnp.float32), (0, lanes - BINS))[None],
            jnp.zeros((5, lanes), jnp.float32),
        ]
    )
    shares = [facts, w_qkv, w_proj, w_fc1, w_fc2]
    bias_qkv = jnp.concatenate([b_query, jnp.zeros_like(b_query), b_value])
    if fast:
        bias = jnp.concatenate(
            [bias_qkv, b_proj, b_fc1, b_fc2, b_ada, jnp.zeros((D,), jnp.float32)]
        ).reshape(16, D)
        ins = [tokens.reshape(SEQ, D), condition, w_ada, bias]
        own, sib, outs = gather_all(shares, ins)
    else:
        own, sib = gather_plain(shares)
        outs = None
    qkv_own, proj_own, fc1_own, fc2_own = own[1:]
    qkv_sib, proj_sib, fc1_sib, fc2_sib = sib[1:]
    own_facts, sib_facts = own[0].reshape(-1, 16, lanes), sib[0].reshape(-1, 16, lanes)
    def times(left, right):
        return jnp.dot(left, right, preferred_element_type=jnp.float32)

    def times_t(left, right):
        return lax.dot_general(left, right, LAST_DIMS, preferred_element_type=jnp.float32)

    if fast:
        modul, attn_in_t, qkv_all, lse, attended_t, attn_out, middle = outs[:7]
        mlp_in_t, hidden, active_t, branch, result = outs[7:]
        ins_back = [
            modul,
            facts,
            own[0],
            sib[0],
            cotangent.reshape(SEQ, D),
            branch,
            hidden,
            middle,
            attn_out,
            lse,
            qkv_all,
            tokens.reshape(SEQ, D),
        ]
        (grad_fc2,), outs = back_all(
            [active_t], ins_back + list(own[1:]) + list(sib[1:]), [w_fc2]
        )
        d_attn, d_split, grad_tokens, note, d_hidden = outs
        pairs = [(mlp_in_t, d_hidden), (attn_in_t, d_split), (attended_t, d_attn)]
        (grad_fc1, grad_qkv, grad_proj), note_own, note_sib, d_silu = scatter_all(
            pairs, [w_fc1, w_qkv, w_proj], note, w_ada
        )
        d_silu = d_silu[0:1]
        result, grad_tokens = result.reshape(tokens.shape), grad_tokens.reshape(tokens.shape)
    else:
        counts = (jnp.sum(own_facts, axis=0) + jnp.sum(sib_facts, axis=0))[0, :BINS]
        bin_scale = bin_weights.astype(jnp.float32) * (jnp.sum(counts) / BINS) / counts
        image_scale = jnp.sum(bin_table * bin_scale[None, :], axis=1)
        token_float = tokens.astype(jnp.float32)
        normed_one, inverse_one = norm_rows(token_float)
        modul = (
            lax.dot_general(silu_cond, w_ada, LAST_DIMS, preferred_element_type=jnp.float32) + b_ada
        )
        pieces = [modul[:, None, part_index * D : (part_index + 1) * D] for part_index in range(6)]
        shift_one, scale_one, gate_one, shift_two, scale_two, gate_two = pieces
        attn_in = (
            (normed_one * (1.0 + scale_one) + shift_one).astype(jnp.bfloat16).reshape(row_count, D)
        )
        qkv_all = (join(times(attn_in, qkv_own), times(attn_in, qkv_sib)) + bias_qkv).astype(
            jnp.bfloat16
        )
        qkv_heads = qkv_all.reshape(images, SEQ, 3, H, HD)
        query, keys, values = (qkv_heads[:, :, 0], qkv_heads[:, :, 1], qkv_heads[:, :, 2])
        scores = masked_scores(query, keys, valid_keys)
        row_max = jnp.max(scores, axis=-1, keepdims=True)
        exponent = jnp.exp(scores - row_max)
        row_total = jnp.sum(exponent, axis=-1, keepdims=True)
        soft_probs = exponent / row_total
        log_total = row_max + jnp.log(row_total)
        attended = jnp.einsum(
            "bhlm,bmhc->blhc",
            soft_probs.astype(jnp.bfloat16),
            values,
            preferred_element_type=jnp.float32,
        )
        attended = attended.astype(jnp.bfloat16).reshape(row_count, D)
        attn_out = (join(times(attended, proj_own), times(attended, proj_sib)) + b_proj).reshape(
            images, SEQ, D
        )
        middle = token_float + gate_one * attn_out
        normed_two, inverse_two = norm_rows(middle)
        mlp_in = (
            (normed_two * (1.0 + scale_two) + shift_two).astype(jnp.bfloat16).reshape(row_count, D)
        )
        hidden = join(times(mlp_in, fc1_own), times(mlp_in, fc1_sib)) + b_fc1
        active = gelu_tanh(hidden).astype(jnp.bfloat16)
        branch = (join(times(active, fc2_own), times(active, fc2_sib)) + b_fc2).reshape(
            images, SEQ, D
        )
        result = (middle + gate_two * branch).astype(jnp.bfloat16)
        grad_out = (
            cotangent.astype(jnp.float32)
            * (valid_keys.astype(jnp.float32) * image_scale[:, None])[:, :, None]
        )
        d_gate_two = jnp.sum(grad_out * branch, axis=1)
        d_branch = (gate_two * grad_out).astype(jnp.bfloat16).reshape(row_count, D)
        d_branch_own, d_branch_sib = split(d_branch)
        bias_fc2 = jnp.sum(d_branch, axis=0, dtype=jnp.float32)
        d_active = times_t(d_branch_own, fc2_own) + times_t(d_branch_sib, fc2_sib)
        d_hidden = jax.vjp(gelu_tanh, hidden)[1](d_active)[0].astype(jnp.bfloat16)
        d_hidden_own, d_hidden_sib = split(d_hidden)
        bias_fc1 = jnp.sum(d_hidden, axis=0, dtype=jnp.float32)
        d_mlp_in = (times_t(d_hidden_own, fc1_own) + times_t(d_hidden_sib, fc1_sib)).reshape(
            images, SEQ, D
        )
        d_shift_two = jnp.sum(d_mlp_in, axis=1)
        d_scale_two = jnp.sum(d_mlp_in * normed_two, axis=1)
        d_middle = grad_out + norm_back(d_mlp_in * (1.0 + scale_two), normed_two, inverse_two)
        d_gate_one = jnp.sum(d_middle * attn_out, axis=1)
        d_attn = (gate_one * d_middle).astype(jnp.bfloat16).reshape(row_count, D)
        d_attn_own, d_attn_sib = split(d_attn)
        bias_proj = jnp.sum(d_attn, axis=0, dtype=jnp.float32)
        d_attended = times_t(d_attn_own, proj_own) + times_t(d_attn_sib, proj_sib)
        d_attended = d_attended.astype(jnp.bfloat16).reshape(images, SEQ, H, HD)
        soft_again = jnp.exp(masked_scores(query, keys, valid_keys) - log_total)
        grad_values = jnp.einsum(
            "bhlm,blhc->bmhc",
            soft_again.astype(jnp.bfloat16),
            d_attended,
            preferred_element_type=jnp.float32,
        )
        d_probs = jnp.einsum("blhc,bmhc->bhlm", d_attended, values, preferred_element_type=jnp.float32)
        d_scores = soft_again * (d_probs - jnp.sum(soft_again * d_probs, axis=-1, keepdims=True))
        d_scores = jnp.where(valid_keys[:, None, None, :], d_scores, 0.0).astype(jnp.bfloat16)
        grad_query = jnp.einsum(
            "bhlm,bmhc->blhc", d_scores, keys, preferred_element_type=jnp.float32
        ) * HD ** (-0.5)
        grad_keys = jnp.einsum(
            "bhlm,blhc->bmhc", d_scores, query, preferred_element_type=jnp.float32
        ) * HD ** (-0.5)
        d_qkv = (
            jnp.stack([grad_query, grad_keys, grad_values], axis=2)
            .astype(jnp.bfloat16)
            .reshape(row_count, 3 * D)
        )
        d_qkv_own, d_qkv_sib = split(d_qkv)
        bias_query = jnp.sum(d_qkv[:, :D], axis=0, dtype=jnp.float32)
        bias_value = jnp.sum(d_qkv[:, 2 * D :], axis=0, dtype=jnp.float32)
        d_attn_in = (times_t(d_qkv_own, qkv_own) + times_t(d_qkv_sib, qkv_sib)).reshape(
            images, SEQ, D
        )
        d_shift_one = jnp.sum(d_attn_in, axis=1)
        d_scale_one = jnp.sum(d_attn_in * normed_one, axis=1)
        grad_tokens = (
            d_middle + norm_back(d_attn_in * (1.0 + scale_one), normed_one, inverse_one)
        ).astype(jnp.bfloat16)
        d_modul = jnp.concatenate(
            [d_shift_one, d_scale_one, d_gate_one, d_shift_two, d_scale_two, d_gate_two], axis=1
        ).astype(jnp.bfloat16)
        d_silu = jnp.dot(d_modul, w_ada, preferred_element_type=jnp.float32)
        note = jnp.concatenate(
            [d_modul.astype(jnp.float32).reshape(-1)]
            + [bias_query, bias_value, bias_proj, bias_fc2, bias_fc1]
            + [jnp.zeros((2 * D,), jnp.float32)]
        ).reshape(16, D)
        terms = [
            (attended.T, d_attn_own, d_attn_sib, w_proj),
            (active.T, d_branch_own, d_branch_sib, w_fc2),
            (attn_in.T, d_qkv_own, d_qkv_sib, w_qkv),
            (mlp_in.T, d_hidden_own, d_hidden_sib, w_fc1),
        ]
        summed_grads, note_own, note_sib = scatter_plain(terms, note)
        grad_proj, grad_fc2, grad_qkv, grad_fc1 = summed_grads
    grad_condition = jax.vjp(jax.nn.silu, cond_float)[1](d_silu)[0]
    note_own, note_sib = note_own.reshape(-1, 16, D), note_sib.reshape(-1, 16, D)
    summed = jnp.sum(note_own, axis=0) + jnp.sum(note_sib, axis=0)
    share_rows = 6 * D // lax.axis_size(("dp", "fsdp"))
    own_start = lax.axis_index(("dp", "fsdp")) * share_rows
    notes = lax.dynamic_slice_in_dim(
        jnp.concatenate([note_own, note_sib]), own_start // D, 2, 1
    ).reshape(-1, 2 * D)
    silus = jnp.concatenate([own_facts, sib_facts])[:, 1:10].reshape(-1, D)
    columns = lax.dynamic_slice_in_dim(notes, own_start % D, share_rows, 1)
    grad_ada = lax.dot_general(
        columns.astype(jnp.bfloat16),
        silus.astype(jnp.bfloat16),
        ROWS_DIMS,
        preferred_element_type=jnp.float32,
    )
    return (
        result,
        grad_tokens,
        grad_condition,
        grad_qkv,
        summed[6],
        summed[7],
        grad_proj,
        summed[8],
        grad_fc1,
        summed[10:14].reshape(-1),
        grad_fc2,
        summed[9],
        grad_ada,
        summed[:6].reshape(-1),
    )


def solution(mesh):
    in_specs = (
        P(("dp", "fsdp"), None, None),
        P(("dp", "fsdp"), None),
        P(("dp", "fsdp"), None, None),
        P(("dp", "fsdp"), None),
        P(("dp", "fsdp")),
        P(),
        P("dp", "fsdp"),
        P(),
        P(),
        P("dp", "fsdp"),
        P(),
        P("dp", "fsdp"),
        P(),
        P("dp", "fsdp"),
        P(),
        P(),
        P(),
    )
    out_specs = (
        P(("dp", "fsdp"), None, None),
        P(("dp", "fsdp"), None, None),
        P(("dp", "fsdp"), None),
        P("dp", "fsdp"),
        P(),
        P(),
        P("dp", "fsdp"),
        P(),
        P("dp", "fsdp"),
        P(),
        P("dp", "fsdp"),
        P(),
        P(("dp", "fsdp"), None),
        P(),
    )
    return jax.shard_map(
        functools.partial(shards, dict(mesh.shape) == {"dp": 16, "fsdp": 2}),
        mesh=mesh,
        in_specs=in_specs,
        out_specs=out_specs,
        check_vma=False,
    )
```
